32 devices in a mesh: dp: 8 (over z, x), mp: 4 (over y, core).
Axes of the slice: x: 2, y: 2, z: 4, core: 2. Of those that a mesh axis runs over, the one named last changes fastest.
Arguments:
- tokens: bfloat16 [4, 7680, 768], P(None, ('dp', 'mp')), may hold values from -6 to 6
- cotangent: float32 [4, 7680, 768], P(None, ('dp', 'mp')), may hold values from -6 to 6
- text_lengths: int32 [4, 32], P(None, 'dp'), may hold values from 1 to 40, as said below
- modality: int32 [4, 7680], P(None, 'dp'), may hold values from 0 to 1, as said below
- masked_positions: int32 [4, 32, 6], P(None, 'dp'), may hold values from 0 to 39, as said below
- joint_weight: float32 [3, 768, 768], P(None, 'dp', 'mp'), may hold values from -0.21875 to 0.21875
- joint_first: float32 [3, 768, 768], P(None, 'dp', 'mp')
- joint_second: float32 [3, 768, 768], P(None, 'dp', 'mp'), as said below
- output_weight: float32 [768, 768], P('mp', 'dp'), may hold values from -0.625 to 0.625
- output_first: float32 [768, 768], P('mp', 'dp')
- output_second: float32 [768, 768], P('mp', 'dp'), as said below
- lift_weight: float32 [2, 768, 3072], P(None, 'dp', 'mp'), may hold values from -0.21875 to 0.21875
- lift_first: float32 [2, 768, 3072], P(None, 'dp', 'mp')
- lift_second: float32 [2, 768, 3072], P(None, 'dp', 'mp'), as said below
- drop_weight: float32 [2, 3072, 768], P(None, 'mp', 'dp'), may hold values from -0.109375 to 0.109375
- drop_first: float32 [2, 3072, 768], P(None, 'mp', 'dp')
- drop_second: float32 [2, 3072, 768], P(None, 'mp', 'dp'), as said below
- norm_params: float32 [4, 768], replicated, may hold values from -0.5 to 1.3
- norm_first: float32 [4, 768], replicated
- norm_second: float32 [4, 768], replicated, as said below
- extra_params: float32 [3, 768], replicated, may hold values from -3 to 3
- extra_first: float32 [3, 768], replicated
- extra_second: float32 [3, 768], replicated, as said below
Outputs:
- block_output: float32 [4, 7680, 768], P(None, ('dp', 'mp'))
- input_grad: float32 [4, 7680, 768], P(None, ('dp', 'mp'))
- rms_values: float32 [3], replicated
- joint_weight_new: float32 [3, 768, 768], P(None, 'dp', 'mp')
- joint_first_new: float32 [3, 768, 768], P(None, 'dp', 'mp')
- joint_second_new: float32 [3, 768, 768], P(None, 'dp', 'mp')
- joint_copy: bfloat16 [3, 768, 768], P(None, 'dp', 'mp')
- output_weight_new: float32 [768, 768], P('mp', 'dp')
- output_first_new: float32 [768, 768], P('mp', 'dp')
- output_second_new: float32 [768, 768], P('mp', 'dp')
- output_copy: bfloat16 [768, 768], P('mp', 'dp')
- lift_weight_new: float32 [2, 768, 3072], P(None, 'dp', 'mp')
- lift_first_new: float32 [2, 768, 3072], P(None, 'dp', 'mp')
- lift_second_new: float32 [2, 768, 3072], P(None, 'dp', 'mp')
- lift_copy: bfloat16 [2, 768, 3072], P(None, 'dp', 'mp')
- drop_weight_new: float32 [2, 3072, 768], P(None, 'mp', 'dp')
- drop_first_new: float32 [2, 3072, 768], P(None, 'mp', 'dp')
- drop_second_new: float32 [2, 3072, 768], P(None, 'mp', 'dp')
- drop_copy: bfloat16 [2, 3072, 768], P(None, 'mp', 'dp')
- norm_params_new: float32 [4, 768], replicated
- norm_first_new: float32 [4, 768], replicated
- norm_second_new: float32 [4, 768], replicated
- norm_copy: bfloat16 [4, 768], replicated
- extra_params_new: float32 [3, 768], replicated
- extra_first_new: float32 [3, 768], replicated
- extra_second_new: float32 [3, 768], replicated
- extra_copy: bfloat16 [3, 768], replicated
The draws below stay inside these ranges and needn't reach their ends.
Inputs may be any that keep to these rules, and one draw needn't show every extreme that they name: `text_lengths`: among the 4 items of one index of dp in a micro-batch, one has exactly 40 text tokens. `modality`: follows text_lengths: in each block of 960 rows, the items' patch rows are 0, their text rows and the rows after the last item are 1, so a block holds exactly 788 zeros. `masked_positions`: each position is below its item's text length; repeats may occur. `joint_second`: Positive. `output_second`: Positive. `lift_second`: Positive. `drop_second`: Positive. `norm_second`: Positive. `extra_second`: Positive.
All inputs are finite; a program needn't handle non-finite values.
Results may differ from the reference program's by a relative error of at most 0.015.
Values may be sent and summed in bfloat16 or wider, within the bound.
No kernel may reach another device: no remote copies, remote signals or barrier semaphores. Data moves between devices by JAX's collectives and lax.ppermute only.
A program may use at most 256 MiB of HBM per device.

```python
import math
import jax
import jax.numpy as jnp
from jax import lax

D = 768
HEADS = 12
HEAD_DIM = 64
FF = 3072
PATCHES = 197
TEXT_MAX = 40
SLOT = 240
MASKS = 6
MICRO = 4
STEP = 7
ITEMS_DEV = 4
ITEMS = 32
TOK_DEV = 960
TOKENS = 7680
N_DP = 8


def shared_lengths(key):
    base_key = jax.random.fold_in(key, 101)
    lengths = jax.random.randint(jax.random.fold_in(base_key, 1), (MICRO, ITEMS), 1, TEXT_MAX + 1)
    chosen = jax.random.randint(jax.random.fold_in(base_key, 2), (MICRO, ITEMS // ITEMS_DEV, 1), 0, ITEMS_DEV)
    longest = (jnp.arange(ITEMS_DEV)[None, None, :] == chosen).reshape(MICRO, ITEMS)
    return jnp.where(longest, TEXT_MAX, lengths).astype(jnp.int32)


def draw_text_lengths(key, part):
    return shared_lengths(key)


def draw_modality(key, part):
    lengths = shared_lengths(key).reshape(MICRO, ITEMS // ITEMS_DEV, ITEMS_DEV)
    item_sizes = PATCHES + lengths
    item_ends = jnp.cumsum(item_sizes, axis=-1)
    item_starts = item_ends - item_sizes
    row_ids = jnp.arange(TOK_DEV)[None, None, :, None]
    inside = (row_ids >= item_starts[:, :, None, :]) & (row_ids < item_starts[:, :, None, :] + PATCHES)
    patch_rows = jnp.any(inside, axis=-1)
    return jnp.where(patch_rows, 0, 1).astype(jnp.int32).reshape(MICRO, TOKENS)


def draw_masked_positions(key, part):
    lengths = shared_lengths(key)
    upper_limit = jnp.broadcast_to(lengths[:, :, None], (MICRO, ITEMS, MASKS))
    return jax.random.randint(jax.random.fold_in(key, 202), (MICRO, ITEMS, MASKS), 0, upper_limit).astype(jnp.int32)


def draw_norm_params(key, part):
    gains = jax.random.uniform(jax.random.fold_in(key, 303), (2, D), jnp.float32, 0.7, 1.3)
    shifts = jax.random.uniform(jax.random.fold_in(key, 304), (2, D), jnp.float32, -0.5, 0.5)
    return jnp.stack([gains[0], shifts[0], gains[1], shifts[1]])


def gradient_size():
    return math.sqrt(MICRO * TOKENS)


def used_share():
    return math.sqrt((PATCHES + TEXT_MAX / 2.0) / SLOT)


def vision_share():
    return math.sqrt(PATCHES / SLOT)


def text_share():
    return math.sqrt((TEXT_MAX + 1) / (2.0 * SLOT))


def first_moment(key, array_shape, moment_scale):
    noise = jax.random.normal(jax.random.fold_in(key, 401), array_shape, jnp.float32)
    return 0.1 / 0.9 * moment_scale * gradient_size() * noise


def second_moment(key, array_shape, moment_scale):
    factor = jnp.exp(jax.random.uniform(jax.random.fold_in(key, 402), array_shape, jnp.float32, math.log(0.5), math.log(8.0)))
    return 0.02 / 0.98 * factor * (moment_scale * gradient_size()) ** 2


def expert_scales(vision_factor, text_factor):
    return jnp.array([vision_factor * vision_share(), text_factor * text_share()], jnp.float32)[:, None, None]


def norm_scales():
    return jnp.array([1.7, 1.7, 0.6, 0.6], jnp.float32)[:, None] * used_share()


def extra_scales():
    return jnp.array([vision_share(), text_share(), 1.5 * math.sqrt(MASKS / SLOT)], jnp.float32)[:, None]


def draw_joint_first(key, part):
    return first_moment(key, (3, D, D), used_share())


def draw_joint_second(key, part):
    return second_moment(key, (3, D, D), used_share())


def draw_output_first(key, part):
    return first_moment(key, (D, D), 0.2 * used_share())


def draw_output_second(key, part):
    return second_moment(key, (D, D), 0.2 * used_share())


def draw_lift_first(key, part):
    return first_moment(key, (2, D, FF), expert_scales(0.3, 0.3))


def draw_lift_second(key, part):
    return second_moment(key, (2, D, FF), expert_scales(0.3, 0.3))


def draw_drop_first(key, part):
    return first_moment(key, (2, FF, D), expert_scales(0.6, 0.6))


def draw_drop_second(key, part):
    return second_moment(key, (2, FF, D), expert_scales(0.6, 0.6))


def draw_norm_first(key, part):
    return first_moment(key, (4, D), norm_scales())


def draw_norm_second(key, part):
    return second_moment(key, (4, D), norm_scales())


def draw_extra_first(key, part):
    return first_moment(key, (3, D), extra_scales())


def draw_extra_second(key, part):
    return second_moment(key, (3, D), extra_scales())


def levels(rng, shape, pieces, low, largest):
    def one(position, blocks):
        heights = jax.random.uniform(jax.random.fold_in(jax.random.fold_in(rng, 6), position), (blocks,), jnp.float32, low / len(pieces), largest / len(pieces))
        return jnp.repeat(jnp.exp(heights), shape[position] // blocks).reshape((-1,) + (1,) * (len(shape) - position - 1))

    gain = one(*pieces[0])
    for cut in pieces[1:]:
        gain = gain * one(*cut)
    return gain


def scatter_about(key, shape, width, limit, cuts=(), kind=jnp.bfloat16):
    values = width * jax.random.normal(key, shape, jnp.float32)
    if cuts:
        values = values * levels(key, shape, cuts, -0.22, 0.18)
    return jnp.clip(values, -limit, limit).astype(kind)


def setup_inputs(seed: int = 0) -> dict:
    key_list = jax.random.split(jax.random.key(seed), 24)
    tokens = scatter_about(key_list[0], (MICRO, TOKENS, D), 1.0, 6.0, ((1, 32),))
    cotangent = scatter_about(key_list[1], (MICRO, TOKENS, D), 1.0, 6.0, ((1, 32),), jnp.float32)
    text_lengths = draw_text_lengths(jax.random.fold_in(key_list[23], 71), 0)
    modality = draw_modality(jax.random.fold_in(key_list[23], 71), 0)
    masked_positions = draw_masked_positions(jax.random.fold_in(key_list[23], 71), 0)
    joint_weight = scatter_about(key_list[5], (3, D, D), D ** -0.5, 0.21875, ((1, 8), (2, 4)), jnp.float32)
    joint_first = draw_joint_first(jax.random.fold_in(key_list[23], 71), 0)
    joint_second = draw_joint_second(jax.random.fold_in(key_list[23], 71), 0)
    output_weight = scatter_about(key_list[8], (D, D), (D // 8) ** -0.5, 0.625, ((0, 4), (1, 8)), jnp.float32)
    output_first = draw_output_first(jax.random.fold_in(key_list[23], 71), 0)
    output_second = draw_output_second(jax.random.fold_in(key_list[23], 71), 0)
    lift_weight = scatter_about(key_list[11], (2, D, FF), D ** -0.5, 0.21875, ((1, 8), (2, 4)), jnp.float32)
    lift_first = draw_lift_first(jax.random.fold_in(key_list[23], 71), 0)
    lift_second = draw_lift_second(jax.random.fold_in(key_list[23], 71), 0)
    drop_weight = scatter_about(key_list[14], (2, FF, D), FF ** -0.5, 0.109375, ((1, 4), (2, 8)), jnp.float32)
    drop_first = draw_drop_first(jax.random.fold_in(key_list[23], 71), 0)
    drop_second = draw_drop_second(jax.random.fold_in(key_list[23], 71), 0)
    norm_params = draw_norm_params(jax.random.fold_in(key_list[23], 71), 0)
    norm_first = draw_norm_first(jax.random.fold_in(key_list[23], 71), 0)
    norm_second = draw_norm_second(jax.random.fold_in(key_list[23], 71), 0)
    extra_params = scatter_about(key_list[20], (3, D), 0.5, 3.0, (), jnp.float32)
    extra_first = draw_extra_first(jax.random.fold_in(key_list[23], 71), 0)
    extra_second = draw_extra_second(jax.random.fold_in(key_list[23], 71), 0)
    return dict(tokens=tokens, cotangent=cotangent, text_lengths=text_lengths, modality=modality, masked_positions=masked_positions, joint_weight=joint_weight, joint_first=joint_first, joint_second=joint_second, output_weight=output_weight, output_first=output_first, output_second=output_second, lift_weight=lift_weight, lift_first=lift_first, lift_second=lift_second, drop_weight=drop_weight, drop_first=drop_first, drop_second=drop_second, norm_params=norm_params, norm_first=norm_first, norm_second=norm_second, extra_params=extra_params, extra_first=extra_first, extra_second=extra_second)


@jax.custom_vjp
def low(v):
    return lax.optimization_barrier(v.astype(jnp.bfloat16)).astype(jnp.float32)

@jax.custom_vjp
def low_back(v):
    return v

def low_keep(v):
    return (low(v), None)

def low_pass(kept, grad):
    return (grad,)

def back_keep(v):
    return (v, None)

def back_low(kept, grad):
    return (low(grad),)
low.defvjp(low_keep, low_pass)
low_back.defvjp(back_keep, back_low)
highest = lax.Precision.HIGHEST
norm_epsilon = 1e-06
masked_score = -1000000000.0
first_decay = 0.9
second_decay = 0.98
adam_epsilon = 1e-06
matrix_rate = 0.04
vector_rate = 0.5
weight_decay = 0.01

def layer_norm(values, gain_row, shift_row):
    centred = values - lax.optimization_barrier(jnp.mean(values, axis=-1, keepdims=True))
    spread = lax.optimization_barrier(jnp.mean(centred * centred, axis=-1, keepdims=True))
    return centred * lax.rsqrt(spread + norm_epsilon) * gain_row + shift_row

def gelu_exact(values):
    return jax.nn.gelu(values, approximate=False)

def block_layout(lengths, masked, total_rows):
    item_sizes = PATCHES + lengths
    item_ends = jnp.cumsum(item_sizes, dtype=jnp.int32)
    item_starts = item_ends - item_sizes
    row_ids = jnp.arange(total_rows, dtype=jnp.int32)
    segment = lax.optimization_barrier(jnp.sum((row_ids[:, None] >= item_ends[None, :]).astype(jnp.int32), axis=1, dtype=jnp.int32))
    valid_rows = segment < lengths.shape[0]
    targets = (item_starts[:, None] + PATCHES + masked).reshape(-1)
    hidden = jnp.any(row_ids[:, None] == targets[None, :], axis=1)
    return (segment, valid_rows, hidden)

def adamw(weight, first_state, second_state, gradient, step_rate, decay_rate):
    first_new = first_decay * first_state + (1.0 - first_decay) * gradient
    second_new = second_decay * second_state + (1.0 - second_decay) * gradient * gradient
    first_hat = first_new / (1.0 - first_decay ** STEP)
    second_hat = second_new / (1.0 - second_decay ** STEP)
    weight_new = weight - step_rate * (first_hat / (jnp.sqrt(second_hat) + adam_epsilon) + decay_rate * weight)
    return (weight_new, first_new, second_new, weight_new.astype(jnp.bfloat16))

def block_forward(params, input_rows, row_kinds, lengths, masked):
    joint_weight, output_weight, lift_weight, drop_weight, norm_params, extra_params = params
    total_rows = input_rows.shape[0]
    segment, valid_rows, hidden = block_layout(lengths, masked, total_rows)
    block_input = jnp.where(hidden[:, None], extra_params[2][None, :], input_rows)
    normed = low(layer_norm(block_input, norm_params[0], norm_params[1]))
    joint_rows = jnp.einsum('td,kdc->ktc', normed, low(joint_weight), precision=highest)
    joint_rows = low_back(low(joint_rows)).reshape(3, total_rows, HEADS, HEAD_DIM)
    raw_scores = low_back(jnp.einsum('qhe,khe->hqk', joint_rows[0], joint_rows[1], precision=highest))
    same_item = segment[:, None] == segment[None, :]
    scores = jnp.where(same_item[None], raw_scores * HEAD_DIM ** (-0.5), masked_score)
    row_top = lax.optimization_barrier(jnp.max(scores, axis=-1, keepdims=True))
    exp_scores = jnp.exp(scores - row_top)
    softmax_rows = low(exp_scores / lax.optimization_barrier(jnp.sum(exp_scores, axis=-1, keepdims=True)))
    mixed_rows = jnp.einsum('hqk,khe->qhe', softmax_rows, joint_rows[2], precision=highest).reshape(total_rows, D)
    mixed_rows = low_back(low(mixed_rows))
    attended = low_back(jnp.dot(mixed_rows, low(output_weight), precision=highest, preferred_element_type=jnp.float32))
    residual = block_input + attended
    feed_input = low(layer_norm(residual, norm_params[2], norm_params[3]))
    vision = (row_kinds == 0)[:, None]
    branch = []
    for expert in range(2):
        lifted = low_back(jnp.dot(feed_input, low(lift_weight[expert]), precision=highest, preferred_element_type=jnp.float32))
        activated = low(gelu_exact(lifted))
        branch.append(jnp.dot(activated, low(drop_weight[expert]), precision=highest, preferred_element_type=jnp.float32))
    feed_sum = low_back(jnp.where(vision, branch[0], branch[1]))
    feed_out = feed_sum + jnp.where(vision, extra_params[0][None, :], extra_params[1][None, :])
    return (residual + feed_out, attended, feed_out)

def reference(tokens, cotangent, text_lengths, modality, masked_positions, joint_weight, joint_first, joint_second, output_weight, output_first, output_second, lift_weight, lift_first, lift_second, drop_weight, drop_first, drop_second, norm_params, norm_first, norm_second, extra_params, extra_first, extra_second):
    blocks = MICRO * N_DP
    tokens_all = tokens.astype(jnp.float32).reshape(blocks, TOK_DEV, D)
    kinds_all = modality.reshape(blocks, TOK_DEV)
    lengths_all = text_lengths.reshape(blocks, ITEMS_DEV)
    masked_all = masked_positions.reshape(blocks, ITEMS_DEV, MASKS)
    params = (joint_weight, output_weight, lift_weight, drop_weight, norm_params, extra_params)

    def forward(params, tokens_all):

        def one_block(packed):
            return block_forward(params, packed[0], packed[1], packed[2], packed[3])
        return lax.map(jax.checkpoint(one_block), (tokens_all, kinds_all, lengths_all, masked_all))
    (outputs, attended, feed_out), pullback = jax.vjp(forward, params, tokens_all)
    valid_all = jax.vmap(lambda lengths, masked: block_layout(lengths, masked, TOK_DEV)[1])(lengths_all, masked_all)
    weight_rows = valid_all.astype(jnp.float32)[:, :, None]
    grad_out = cotangent.astype(jnp.float32).reshape(blocks, TOK_DEV, D) * weight_rows
    gradients, grad_input = pullback((grad_out, jnp.zeros_like(attended), jnp.zeros_like(feed_out)))
    entry_count = jnp.sum(weight_rows) * D
    rms_values = jnp.stack([jnp.sqrt(jnp.sum(weight_rows * branch_out * branch_out) / entry_count) for branch_out in (outputs, attended, feed_out)])
    joint_new = adamw(joint_weight, joint_first, joint_second, gradients[0], matrix_rate, weight_decay)
    output_new = adamw(output_weight, output_first, output_second, gradients[1], matrix_rate, weight_decay)
    lift_new = adamw(lift_weight, lift_first, lift_second, gradients[2], matrix_rate, weight_decay)
    drop_new = adamw(drop_weight, drop_first, drop_second, gradients[3], matrix_rate, weight_decay)
    norm_new = adamw(norm_params, norm_first, norm_second, gradients[4], vector_rate, 0.0)
    extra_new = adamw(extra_params, extra_first, extra_second, gradients[5], vector_rate, 0.0)
    block_output = outputs.reshape(MICRO, TOKENS, D)
    input_grad = grad_input.reshape(MICRO, TOKENS, D)
    return (block_output, input_grad, rms_values, joint_new[0], joint_new[1], joint_new[2], joint_new[3], output_new[0], output_new[1], output_new[2], output_new[3], lift_new[0], lift_new[1], lift_new[2], lift_new[3], drop_new[0], drop_new[1], drop_new[2], drop_new[3], norm_new[0], norm_new[1], norm_new[2], norm_new[3], extra_new[0], extra_new[1], extra_new[2], extra_new[3])
```

```python
import functools

import jax
import jax.numpy as jnp
from jax import lax
from jax.experimental import pallas as pl
from jax.experimental.pallas import tpu as pltpu
from jax.sharding import PartitionSpec as P

HEAD_DIM = 64
PATCHES = 197
TEXT_MAX = 40
STEP = 7

norm_epsilon = 1e-06
masked_score = -1000000000.0
first_decay = 0.9
second_decay = 0.98
adam_epsilon = 1e-06
matrix_rate = 0.04
vector_rate = 0.5
weight_decay = 0.01

PATCH_STRIDE = 208
TEXT_STRIDE = 48
ITEM_ROWS = PATCH_STRIDE + TEXT_STRIDE

bf16 = jnp.bfloat16
f32 = jnp.float32
VMEM_LIMIT = 58 * 1024 * 1024


def adamw(weight, first_state, second_state, gradient, step_rate, decay_rate):
    first_new = first_decay * first_state + (1.0 - first_decay) * gradient
    second_new = second_decay * second_state + (1.0 - second_decay) * gradient * gradient
    first_hat = first_new / (1.0 - first_decay**STEP)
    second_hat = second_new / (1.0 - second_decay**STEP)
    weight_new = weight - step_rate * (
        first_hat / (jnp.sqrt(second_hat) + adam_epsilon) + decay_rate * weight
    )
    return (weight_new, first_new, second_new, weight_new.astype(bf16))


def dot(left, right, left_dim, right_dim):
    return lax.dot_general(
        left,
        right,
        (((left_dim,), (right_dim,)), ((), ())),
        preferred_element_type=f32,
    )


def loop(count, body):
    lax.fori_loop(0, count, lambda i, c: (body(i), c)[1], 0)


def rows_at(index, size):
    return pl.ds(pl.multiple_of(index * size, 16), size)


def norm_forward(values, gain, shift):
    centred = values - jnp.mean(values, axis=-1, keepdims=True)
    spread = jnp.mean(centred * centred, axis=-1, keepdims=True)
    return centred * lax.rsqrt(spread + norm_epsilon) * gain + shift


def norm_backward(values, gain, grad):
    centred = values - jnp.mean(values, axis=-1, keepdims=True)
    spread = jnp.mean(centred * centred, axis=-1, keepdims=True)
    scale = lax.rsqrt(spread + norm_epsilon)
    hat = centred * scale
    grad_hat = grad * gain
    grad_values = scale * (
        grad_hat
        - jnp.mean(grad_hat, axis=-1, keepdims=True)
        - hat * jnp.mean(grad_hat * hat, axis=-1, keepdims=True)
    )
    grad_gain = jnp.sum(grad * hat, axis=0, keepdims=True)
    grad_shift = jnp.sum(grad, axis=0, keepdims=True)
    return grad_values, grad_gain, grad_shift


def one_hot(row_place, first_row, count):
    place = lax.broadcasted_iota(jnp.int32, (count, row_place.shape[1]), 0) + first_row
    return (place == row_place).astype(bf16)


def attend(query, key, value, allowed):
    scores = dot(query, key, 1, 1)
    scores = jnp.where(allowed, scores, masked_score)
    top = jnp.max(scores, axis=-1, keepdims=True)
    weights = jnp.exp(scores - top)
    total = jnp.sum(weights, axis=-1, keepdims=True)
    weights = (weights * (1.0 / total)).astype(bf16)
    return weights, dot(weights, value, 1, 0)


def attention_kernel(
    meta_ref,
    raw_ref,
    place_ref,
    hidden_ref,
    valid_ref,
    norm_ref,
    extra_ref,
    weight_ref,
    block_ref,
    normed_ref,
    joint_ref,
    mixed_ref,
    probs_ref,
    residual_ref,
    feed_ref,
    square_ref,
    *,
    items,
    heads,
    main_rows,
    all_rows,
):
    step = pl.program_id(0)
    width = heads * HEAD_DIM
    tail_rows = all_rows - main_rows

    @pl.when(step == 0)
    def _():
        def chunk(first, size):
            rows = pl.ds(first, size)
            picked = dot(one_hot(place_ref[...], first, size), raw_ref[...], 1, 0)
            picked = jnp.where(hidden_ref[rows, :] > 0, extra_ref[2:3, :], picked)
            block_ref[rows, :] = picked
            residual_ref[rows, :] = picked
            normed_ref[rows, :] = norm_forward(picked, norm_ref[0:1, :], norm_ref[1:2, :]).astype(bf16)

        loop(items, lambda i: chunk(pl.multiple_of(i * ITEM_ROWS, 16), ITEM_ROWS))
        chunk(main_rows, tail_rows)

    def project(rows):
        joint = dot(normed_ref[rows, :], weight_ref[0, :, : 3 * width], 1, 0)
        joint_ref[0, rows, :width] = (joint[:, :width].astype(bf16).astype(f32) * HEAD_DIM**-0.5).astype(bf16)
        joint_ref[0, rows, width:] = joint[:, width:].astype(bf16)

    loop(items, lambda i: project(rows_at(i, ITEM_ROWS)))
    project(pl.ds(main_rows, tail_rows))

    column = lax.broadcasted_iota(jnp.int32, (1, ITEM_ROWS), 1)

    def one_item(i):
        patch_rows = rows_at(i, PATCH_STRIDE)
        text_rows = pl.ds(pl.multiple_of(items * PATCH_STRIDE + i * TEXT_STRIDE, 16), TEXT_STRIDE)
        joint = jnp.concatenate([joint_ref[0, patch_rows, :], joint_ref[0, text_rows, :]], axis=0)
        allowed = (column < PATCHES) | (
            (column >= PATCH_STRIDE) & (column < PATCH_STRIDE + meta_ref[i])
        )
        outs = []
        for h in range(heads):
            part = lambda k: joint[:, k * width + h * HEAD_DIM : k * width + (h + 1) * HEAD_DIM]
            weights, out = attend(part(0), part(1), part(2), allowed)
            probs_ref[0, i, h] = weights
            outs.append(out.astype(bf16))
        mixed = jnp.concatenate(outs, axis=1)
        mixed_ref[0, patch_rows, :] = mixed[:PATCH_STRIDE]
        mixed_ref[0, text_rows, :] = mixed[PATCH_STRIDE:]

    loop(items, one_item)

    joint = joint_ref[0, main_rows:, :]
    allowed = lax.broadcasted_iota(jnp.int32, (1, tail_rows), 1) < meta_ref[items]
    outs = []
    for h in range(heads):
        part = lambda k: joint[:, k * width + h * HEAD_DIM : k * width + (h + 1) * HEAD_DIM]
        outs.append(attend(part(0), part(1), part(2), allowed)[1].astype(bf16))
    mixed_ref[0, main_rows:, :] = jnp.concatenate(outs, axis=1)

    def add_output(rows):
        residual_ref[rows, :] += dot(mixed_ref[0, rows, :], weight_ref[0, :, 3 * width :], 1, 1)

    loop(items, lambda i: add_output(rows_at(i, ITEM_ROWS)))
    add_output(pl.ds(main_rows, tail_rows))

    @pl.when(step == pl.num_programs(0) - 1)
    def _():
        square_ref[...] = jnp.zeros_like(square_ref)

        def chunk(rows):
            residual = residual_ref[rows, :]
            feed_ref[rows, :] = norm_forward(residual, norm_ref[2:3, :], norm_ref[3:4, :]).astype(bf16)
            attended = (residual - block_ref[rows, :]) * valid_ref[rows, :]
            square_ref[...] += jnp.sum(attended * attended, axis=0, keepdims=True)

        loop(items, lambda i: chunk(rows_at(i, ITEM_ROWS)))
        chunk(pl.ds(main_rows, tail_rows))


def attention_back_kernel(
    grad_attended_ref,
    grad_residual_ref,
    joint_ref,
    mixed_ref,
    probs_ref,
    normed_ref,
    block_ref,
    hidden_ref,
    place_ref,
    norm_ref,
    weight_ref,
    grad_weight_ref,
    grad_raw_ref,
    grad_norm_ref,
    grad_mask_ref,
    grad_normed_ref,
    grad_mixed_ref,
    grad_joint_ref,
    *,
    items,
    heads,
    main_rows,
):
    step = pl.program_id(0)
    width = heads * HEAD_DIM
    half = HEAD_DIM**-0.5

    @pl.when(step == 0)
    def _():
        grad_normed_ref[...] = jnp.zeros_like(grad_normed_ref)

    def mixed_grad(i):
        rows = rows_at(i, ITEM_ROWS)
        grad_mixed_ref[rows, :] = dot(
            grad_attended_ref[rows, :], weight_ref[0, :, 3 * width :], 1, 0
        ).astype(bf16)

    loop(items, mixed_grad)

    def one_item(i):
        patch_rows = rows_at(i, PATCH_STRIDE)
        text_rows = pl.ds(pl.multiple_of(items * PATCH_STRIDE + i * TEXT_STRIDE, 16), TEXT_STRIDE)
        joint = jnp.concatenate([joint_ref[0, patch_rows, :], joint_ref[0, text_rows, :]], axis=0)
        mixed = jnp.concatenate([mixed_ref[0, patch_rows, :], mixed_ref[0, text_rows, :]], axis=0)
        grad_mixed = jnp.concatenate([grad_mixed_ref[patch_rows, :], grad_mixed_ref[text_rows, :]], axis=0)
        grads = [[], [], []]
        for h in range(heads):
            part = lambda k: joint[:, k * width + h * HEAD_DIM : k * width + (h + 1) * HEAD_DIM]
            span = slice(h * HEAD_DIM, (h + 1) * HEAD_DIM)
            grad_out = grad_mixed[:, span]
            weights = probs_ref[0, i, h]
            grad_probs = dot(grad_out, part(2), 1, 1)
            mean_grad = jnp.sum(
                grad_out.astype(f32) * mixed[:, span].astype(f32), axis=-1, keepdims=True
            )
            grad_scores = (weights.astype(f32) * (grad_probs - mean_grad)).astype(bf16)
            grads[0].append((dot(grad_scores, part(1), 1, 0) * half).astype(bf16))
            grads[1].append(dot(grad_scores, part(0), 0, 0).astype(bf16))
            grads[2].append(dot(weights, grad_out, 0, 0).astype(bf16))
        grad_joint = jnp.concatenate(grads[0] + grads[1] + grads[2], axis=1)
        grad_joint_ref[patch_rows, :] = grad_joint[:PATCH_STRIDE]
        grad_joint_ref[text_rows, :] = grad_joint[PATCH_STRIDE:]

    loop(items, one_item)

    model_width = weight_ref.shape[1]
    for first in range(0, model_width, 256):
        cols = slice(first, first + 256)
        grad_weight_ref[0, cols, : 3 * width] = dot(
            normed_ref[:, cols], grad_joint_ref[...], 0, 0
        ).astype(bf16)
        grad_weight_ref[0, cols, 3 * width :] = dot(
            grad_attended_ref[:, cols], mixed_ref[0], 0, 0
        ).astype(bf16)

    def normed_grad(i):
        rows = rows_at(i, ITEM_ROWS)
        grad_normed_ref[rows, :] += dot(grad_joint_ref[rows, :], weight_ref[0, :, : 3 * width], 1, 1)

    loop(items, normed_grad)

    @pl.when(step == pl.num_programs(0) - 1)
    def _():
        grad_norm_ref[...] = jnp.zeros_like(grad_norm_ref)
        grad_mask_ref[...] = jnp.zeros_like(grad_mask_ref)

        def chunk(i):
            rows = rows_at(i, ITEM_ROWS)
            grad, gain, shift = norm_backward(block_ref[rows, :], norm_ref[0:1, :], grad_normed_ref[rows, :])
            grad_norm_ref[0:1, :] += gain
            grad_norm_ref[1:2, :] += shift
            grad = grad + grad_residual_ref[rows, :]
            hidden = hidden_ref[rows, :] > 0
            grad_mask_ref[...] += jnp.sum(jnp.where(hidden, grad, 0.0), axis=0, keepdims=True)
            grad_normed_ref[rows, :] = jnp.where(hidden, 0.0, grad)

        loop(items, chunk)
        unplace(place_ref, grad_normed_ref, grad_raw_ref, main_rows)


def unplace(place_ref, source_ref, raw_ref, source_rows):
    source = source_ref[...].astype(bf16)
    raw_rows = raw_ref.shape[0]
    size = 240 if raw_rows % 240 == 0 else raw_rows

    def chunk(i):
        rows = rows_at(i, size)
        place = lax.broadcasted_iota(jnp.int32, (size, source_rows), 1)
        pick = (place == place_ref[rows, :]).astype(bf16)
        raw_ref[rows, :] = dot(pick, source, 1, 0).astype(bf16)

    loop(raw_rows // size, chunk)


def lift_kernel(feed_ref, weight_ref, acted_ref, slope_ref, *, vision_rows, all_rows):
    def piece(rows, expert):
        lifted = dot(feed_ref[rows, :], weight_ref[expert, 0], 1, 0)
        cumulative = 0.5 * (1.0 + lax.erf(lifted * (0.5**0.5)))
        density = jnp.exp(-0.5 * lifted * lifted) * ((2.0 * jnp.pi) ** -0.5)
        acted_ref[0, rows, :] = (lifted * cumulative).astype(bf16)
        slope_ref[0, rows, :] = (cumulative + lifted * density).astype(bf16)

    loop(vision_rows // PATCH_STRIDE, lambda i: piece(rows_at(i, PATCH_STRIDE), 0))
    text = all_rows - vision_rows
    loop(3, lambda i: piece(pl.ds(pl.multiple_of(vision_rows + i * (text // 3), 16), text // 3), 1))


def drop_weight_kernel(
    raw_ref, place_ref, acted_ref, grad_ref, grad_bias_ref, grad_weight_ref, *, vision_rows, main_rows
):
    @pl.when(pl.program_id(0) == 0)
    def _():
        def chunk(i):
            rows = rows_at(i, ITEM_ROWS)
            grad_ref[rows, :] = dot(
                one_hot(place_ref[...], i * ITEM_ROWS, ITEM_ROWS), raw_ref[...], 1, 0
            ).astype(bf16)

        loop(main_rows // ITEM_ROWS, chunk)
        grad_bias_ref[0:1, :] = jnp.sum(
            grad_ref[:vision_rows, :].astype(f32), axis=0, keepdims=True
        )
        grad_bias_ref[1:2, :] = jnp.sum(
            grad_ref[vision_rows:, :].astype(f32), axis=0, keepdims=True
        )

    for expert, rows in ((0, slice(0, vision_rows)), (1, slice(vision_rows, main_rows))):
        for first in range(0, grad_ref.shape[1], 256):
            cols = slice(first, first + 256)
            grad_weight_ref[expert, 0, cols, :] = dot(
                grad_ref[rows, cols], acted_ref[0, rows, :], 0, 0
            ).astype(bf16)


def drop_kernel(
    acted_ref,
    residual_ref,
    valid_ref,
    place_ref,
    extra_ref,
    weight_ref,
    raw_ref,
    square_ref,
    total_ref,
    *,
    vision_rows,
    all_rows,
):
    step = pl.program_id(0)
    text = all_rows - vision_rows

    @pl.when(step == 0)
    def _():
        total_ref[:vision_rows, :] = jnp.broadcast_to(extra_ref[0:1, :], (vision_rows, total_ref.shape[1]))
        total_ref[vision_rows:, :] = jnp.broadcast_to(extra_ref[1:2, :], (text, total_ref.shape[1]))

    def piece(rows, expert):
        total_ref[rows, :] += dot(acted_ref[0, rows, :], weight_ref[expert, 0], 1, 1)

    def everything(body):
        loop(vision_rows // PATCH_STRIDE, lambda i: body(rows_at(i, PATCH_STRIDE), 0))
        loop(3, lambda i: body(pl.ds(pl.multiple_of(vision_rows + i * (text // 3), 16), text // 3), 1))

    everything(piece)

    @pl.when(step == pl.num_programs(0) - 1)
    def _():
        square_ref[...] = jnp.zeros_like(square_ref)

        def finish(rows, expert):
            fed = total_ref[rows, :]
            out = residual_ref[rows, :] + fed
            valid = valid_ref[rows, :]
            square_ref[0:1, :] += jnp.sum(valid * out * out, axis=0, keepdims=True)
            square_ref[1:2, :] += jnp.sum(valid * fed * fed, axis=0, keepdims=True)
            total_ref[rows, :] = out

        everything(finish)
        unplace(place_ref, total_ref, raw_ref, all_rows)


def expert_back_kernel(
    grad_ref,
    slope_ref,
    feed_ref,
    residual_ref,
    norm_ref,
    drop_ref,
    lift_ref,
    grad_weight_ref,
    grad_residual_ref,
    grad_attended_ref,
    grad_norm_ref,
    grad_lifted_ref,
    *,
    vision_rows,
    main_rows,
):
    step = pl.program_id(0)

    @pl.when(step == 0)
    def _():
        grad_residual_ref[...] = jnp.zeros_like(grad_residual_ref)

    def piece(rows, expert):
        grad_acted = dot(grad_ref[rows, :], drop_ref[expert, 0], 1, 0)
        grad_lifted = (grad_acted * slope_ref[0, rows, :].astype(f32)).astype(bf16)
        grad_lifted_ref[rows, :] = grad_lifted
        grad_residual_ref[rows, :] += dot(grad_lifted, lift_ref[expert, 0], 1, 1)

    loop(vision_rows // PATCH_STRIDE, lambda i: piece(rows_at(i, PATCH_STRIDE), 0))
    piece(pl.ds(vision_rows, main_rows - vision_rows), 1)

    for expert, rows in ((0, slice(0, vision_rows)), (1, slice(vision_rows, main_rows))):
        for first in range(0, feed_ref.shape[1], 256):
            cols = slice(first, first + 256)
            grad_weight_ref[expert, 0, cols, :] = dot(
                feed_ref[rows, cols], grad_lifted_ref[rows, :], 0, 0
            ).astype(bf16)

    @pl.when(step == pl.num_programs(0) - 1)
    def _():
        grad_norm_ref[...] = jnp.zeros_like(grad_norm_ref)

        def chunk(i):
            rows = rows_at(i, ITEM_ROWS)
            grad, gain, shift = norm_backward(
                residual_ref[rows, :], norm_ref[2:3, :], grad_residual_ref[rows, :]
            )
            grad_norm_ref[0:1, :] += gain
            grad_norm_ref[1:2, :] += shift
            grad = grad + grad_ref[rows, :].astype(f32)
            grad_residual_ref[rows, :] = grad
            grad_attended_ref[rows, :] = grad.astype(bf16)

        loop(main_rows // ITEM_ROWS, chunk)


def whole(*shape):
    return pl.BlockSpec(shape, lambda *_: (0,) * len(shape))


def stepped(*shape):
    return pl.BlockSpec(shape, lambda i, *_: (i,) + (0,) * (len(shape) - 1))


def stepped_pair(*shape):
    return pl.BlockSpec(shape, lambda i, *_: (0, i) + (0,) * (len(shape) - 2))


def call(kernel, name, steps, in_specs, out_specs, out_shapes, scratch, flops, moved, args, scalars=0):
    return pl.pallas_call(
        kernel,
        name=name,
        grid_spec=pltpu.PrefetchScalarGridSpec(
            num_scalar_prefetch=scalars,
            grid=(steps,),
            in_specs=in_specs,
            out_specs=out_specs,
            scratch_shapes=scratch,
        ),
        out_shape=[jax.ShapeDtypeStruct(s, d) for s, d in out_shapes],
        compiler_params=pltpu.CompilerParams(
            dimension_semantics=("arbitrary",), vmem_limit_bytes=VMEM_LIMIT
        ),
        cost_estimate=pl.CostEstimate(flops=flops, bytes_accessed=moved, transcendentals=0),
    )(*args)


def body(
    tokens,
    cotangent,
    text_lengths,
    modality,
    masked_positions,
    joint_weight,
    joint_first,
    joint_second,
    output_weight,
    output_first,
    output_second,
    lift_weight,
    lift_first,
    lift_second,
    drop_weight,
    drop_first,
    drop_second,
    norm_params,
    norm_first,
    norm_second,
    extra_params,
    extra_first,
    extra_second,
):
    micro_count, shard_rows, model_width = tokens.shape
    block_rows = modality.shape[1]
    parts = block_rows // shard_rows
    assert micro_count == parts
    items = text_lengths.shape[1]
    width = joint_weight.shape[2]
    heads = width // HEAD_DIM
    hidden_width = lift_weight.shape[2]
    shard = joint_weight.shape[1]
    vision_rows = items * PATCH_STRIDE
    main_rows = items * ITEM_ROWS
    tail = block_rows - items * PATCHES - TEXT_MAX - (items - 1)
    tail = (tail + 47) // 48 * 48
    all_rows = main_rows + tail
    assert 4 * width == model_width and hidden_width == model_width

    shard_attend = jnp.concatenate(
        [joint_weight[0], joint_weight[1], joint_weight[2], output_weight.T], axis=1
    ).astype(bf16)
    shard_lift = lift_weight.astype(bf16)
    shard_drop = jnp.swapaxes(drop_weight, 1, 2).astype(bf16)

    def gather(values, axis):
        return lax.all_gather(values, ("mp", "dp"), axis=axis, tiled=True)

    def scatter(values, axis):
        return lax.psum_scatter(values, ("mp", "dp"), scatter_dimension=axis, tiled=True)

    def exchange(values):
        return lax.all_to_all(values, "mp", split_axis=0, concat_axis=1, tiled=True)[0]

    def give_back(values):
        return lax.all_to_all(
            values.reshape(parts, shard_rows, model_width), "mp", split_axis=0, concat_axis=0, tiled=True
        )

    raw_tokens = exchange(tokens)
    attend_all = gather(shard_attend, 0).reshape(parts, model_width, model_width)
    raw_grad = exchange(cotangent.astype(bf16))
    lift_all = gather(shard_lift, 1).reshape(2, parts, model_width, hidden_width)
    drop_all = gather(shard_drop, 1).reshape(2, parts, model_width, hidden_width)

    micro = lax.axis_index("mp")
    lengths = lax.dynamic_index_in_dim(text_lengths, micro, 0, keepdims=False)
    masked = lax.dynamic_index_in_dim(masked_positions, micro, 0, keepdims=False)
    item_ids = jnp.arange(items, dtype=jnp.int32)
    sizes = PATCHES + lengths
    ends = jnp.sum(jnp.where(item_ids[:, None] <= item_ids[None, :], sizes[:, None], 0), axis=0)
    used = jnp.sum(sizes)

    def place_of(row):
        segment = jnp.sum((row[..., None] >= ends).astype(jnp.int32), axis=-1)
        start = jnp.sum(jnp.where(row[..., None] >= ends, sizes, 0), axis=-1)
        inside = row - start
        return jnp.where(
            segment == items,
            main_rows + inside,
            jnp.where(
                inside < PATCHES,
                PATCH_STRIDE * segment + inside,
                vision_rows + TEXT_STRIDE * segment + inside - PATCHES,
            ),
        )

    place_row = place_of(jnp.arange(block_rows, dtype=jnp.int32))[None, :]
    place_column = place_of(jnp.arange(block_rows, dtype=jnp.int32))[:, None]
    targets = (vision_rows + TEXT_STRIDE * item_ids[:, None] + masked).reshape(-1)
    spots = jnp.arange(all_rows, dtype=jnp.int32)
    hidden = jnp.any(spots[:, None] == targets[None, :], axis=1).astype(jnp.int32)[:, None]
    text_spot = spots - vision_rows
    text_item = text_spot // TEXT_STRIDE
    text_end = jnp.sum(jnp.where(text_item[:, None] == item_ids, lengths, 0), axis=1)
    valid = jnp.where(
        text_spot < 0, spots % PATCH_STRIDE < PATCHES, text_spot - text_item * TEXT_STRIDE < text_end
    )
    valid = valid.astype(f32)[:, None]
    meta = jnp.concatenate([lengths, (block_rows - used)[None]])

    square = model_width * model_width
    block_input, normed, joint_rows, mixed, probs, residual, feed_input, attended_square = call(
        functools.partial(
            attention_kernel, items=items, heads=heads, main_rows=main_rows, all_rows=all_rows
        ),
        "attention",
        parts,
        [
            whole(block_rows, model_width),
            whole(1, block_rows),
            whole(all_rows, 1),
            whole(all_rows, 1),
            whole(4, model_width),
            whole(3, model_width),
            stepped(1, model_width, model_width),
        ],
        [
            whole(all_rows, model_width),
            whole(all_rows, model_width),
            stepped(1, all_rows, 3 * width),
            stepped(1, all_rows, width),
            stepped(1, items, heads, ITEM_ROWS, ITEM_ROWS),
            whole(all_rows, model_width),
            whole(all_rows, model_width),
            whole(1, model_width),
        ],
        [
            ((all_rows, model_width), f32),
            ((all_rows, model_width), bf16),
            ((parts, all_rows, 3 * width), bf16),
            ((parts, all_rows, width), bf16),
            ((parts, items, heads, ITEM_ROWS, ITEM_ROWS), bf16),
            ((all_rows, model_width), f32),
            ((all_rows, model_width), bf16),
            ((1, model_width), f32),
        ],
        [],
        2 * all_rows * square * parts + 2 * block_rows * all_rows * model_width,
        40 << 20,
        (meta, raw_tokens, place_row, hidden, valid, norm_params, extra_params, attend_all),
        scalars=1,
    )
    acted, slope = call(
        functools.partial(lift_kernel, vision_rows=vision_rows, all_rows=all_rows),
        "lift",
        parts,
        [whole(all_rows, model_width), stepped_pair(2, 1, model_width, hidden_width)],
        [stepped(1, all_rows, hidden_width)] * 2,
        [((parts, all_rows, hidden_width), bf16)] * 2,
        [],
        2 * all_rows * square * parts,
        30 << 20,
        (feed_input, lift_all),
    )
    grad_rows, grad_bias, grad_drop = call(
        functools.partial(drop_weight_kernel, vision_rows=vision_rows, main_rows=main_rows),
        "drop_weight_grad",
        parts,
        [
            whole(block_rows, model_width),
            whole(1, block_rows),
            stepped(1, main_rows, hidden_width),
        ],
        [
            whole(main_rows, model_width),
            whole(2, model_width),
            stepped_pair(2, 1, model_width, hidden_width),
        ],
        [
            ((main_rows, model_width), bf16),
            ((2, model_width), f32),
            ((2, parts, model_width, hidden_width), bf16),
        ],
        [],
        2 * main_rows * square * parts,
        20 << 20,
        (raw_grad, place_row, acted),
    )
    drop_sum = scatter(grad_drop.reshape(2, parts * model_width, hidden_width), 1)

    grad_lift, grad_residual, grad_attended, grad_norm_second = call(
        functools.partial(expert_back_kernel, vision_rows=vision_rows, main_rows=main_rows),
        "expert_back",
        parts,
        [
            whole(main_rows, model_width),
            stepped(1, main_rows, hidden_width),
            whole(main_rows, model_width),
            whole(main_rows, model_width),
            whole(4, model_width),
            stepped_pair(2, 1, model_width, hidden_width),
            stepped_pair(2, 1, model_width, hidden_width),
        ],
        [
            stepped_pair(2, 1, model_width, hidden_width),
            whole(main_rows, model_width),
            whole(main_rows, model_width),
            whole(2, model_width),
        ],
        [
            ((2, parts, model_width, hidden_width), bf16),
            ((main_rows, model_width), f32),
            ((main_rows, model_width), bf16),
            ((2, model_width), f32),
        ],
        [pltpu.VMEM((main_rows, hidden_width), bf16)],
        6 * main_rows * square * parts,
        45 << 20,
        (grad_rows, slope, feed_input, residual, norm_params, drop_all, lift_all),
    )
    lift_sum = scatter(grad_lift.reshape(2, parts * model_width, hidden_width), 1)

    grad_attend, grad_raw, grad_norm_first, grad_mask = call(
        functools.partial(attention_back_kernel, items=items, heads=heads, main_rows=main_rows),
        "attention_back",
        parts,
        [
            whole(main_rows, model_width),
            whole(main_rows, model_width),
            stepped(1, main_rows, 3 * width),
            stepped(1, main_rows, width),
            stepped(1, items, heads, ITEM_ROWS, ITEM_ROWS),
            whole(main_rows, model_width),
            whole(main_rows, model_width),
            whole(all_rows, 1),
            whole(block_rows, 1),
            whole(4, model_width),
            stepped(1, model_width, model_width),
        ],
        [
            stepped(1, model_width, model_width),
            whole(block_rows, model_width),
            whole(2, model_width),
            whole(1, model_width),
        ],
        [
            ((parts, model_width, model_width), bf16),
            ((block_rows, model_width), bf16),
            ((2, model_width), f32),
            ((1, model_width), f32),
        ],
        [
            pltpu.VMEM((main_rows, model_width), f32),
            pltpu.VMEM((main_rows, width), bf16),
            pltpu.VMEM((main_rows, 3 * width), bf16),
        ],
        4 * main_rows * square * parts,
        40 << 20,
        (
            grad_attended,
            grad_residual,
            joint_rows,
            mixed,
            probs,
            normed,
            block_input,
            hidden,
            place_column,
            norm_params,
            attend_all,
        ),
    )
    attend_sum = scatter(grad_attend.reshape(parts * model_width, model_width), 0)
    input_grad = give_back(grad_raw).astype(f32)

    raw_out, feed_square = call(
        functools.partial(drop_kernel, vision_rows=vision_rows, all_rows=all_rows),
        "drop",
        parts,
        [
            stepped(1, all_rows, hidden_width),
            whole(all_rows, model_width),
            whole(all_rows, 1),
            whole(block_rows, 1),
            whole(3, model_width),
            stepped_pair(2, 1, model_width, hidden_width),
        ],
        [whole(block_rows, model_width), whole(2, model_width)],
        [((block_rows, model_width), bf16), ((2, model_width), f32)],
        [pltpu.VMEM((all_rows, model_width), f32)],
        2 * all_rows * square * parts,
        25 << 20,
        (acted, residual, valid, place_column, extra_params, drop_all),
    )
    block_output = give_back(raw_out).astype(f32)

    squares = jnp.stack(
        [jnp.sum(feed_square[0]), jnp.sum(attended_square), jnp.sum(feed_square[1]), used.astype(f32)]
    )
    small = jnp.concatenate(
        [
            grad_norm_first,
            grad_norm_second,
            grad_bias,
            grad_mask,
            jnp.pad(squares, (0, model_width - 4))[None],
        ],
        axis=0,
    )
    small = lax.psum(small, ("dp", "mp"))
    norm_total, extra_total = small[:4], small[4:7]
    rms_values = jnp.sqrt(small[7, :3] / (small[7, 3] * model_width))

    attend_sum = attend_sum.astype(f32)
    joint_grad = jnp.stack([attend_sum[:, k * width : (k + 1) * width] for k in range(3)])
    output_grad = attend_sum[:, 3 * width :].T
    lift_grad = lift_sum.astype(f32)
    drop_grad = jnp.swapaxes(drop_sum, 1, 2).astype(f32)
    results = [block_output, input_grad, rms_values]
    results += adamw(joint_weight, joint_first, joint_second, joint_grad, matrix_rate, weight_decay)
    results += adamw(output_weight, output_first, output_second, output_grad, matrix_rate, weight_decay)
    results += adamw(lift_weight, lift_first, lift_second, lift_grad, matrix_rate, weight_decay)
    results += adamw(drop_weight, drop_first, drop_second, drop_grad, matrix_rate, weight_decay)
    results += adamw(norm_params, norm_first, norm_second, norm_total, vector_rate, 0.0)
    results += adamw(extra_params, extra_first, extra_second, extra_total, vector_rate, 0.0)
    return tuple(results)


def solution(mesh):
    rows = P(None, ("dp", "mp"), None)
    joint, output, lift, drop = (
        P(None, "dp", "mp"),
        P("mp", "dp"),
        P(None, "dp", "mp"),
        P(None, "mp", "dp"),
    )
    return jax.shard_map(
        body,
        mesh=mesh,
        in_specs=(rows, rows, P(None, "dp"), P(None, "dp"), P(None, "dp", None))
        + (joint,) * 3
        + (output,) * 3
        + (lift,) * 3
        + (drop,) * 3
        + (P(),) * 6,
        out_specs=(rows, rows, P())
        + (joint,) * 4
        + (output,) * 4
        + (lift,) * 4
        + (drop,) * 4
        + (P(),) * 8,
        check_vma=False,
    )
```

```python
import functools

import jax
import jax.numpy as jnp
from jax import lax
from jax.experimental import pallas as pl
from jax.experimental.pallas import tpu as pltpu
from jax.sharding import PartitionSpec as P

HEAD_DIM = 64
PATCHES = 197
TEXT_MAX = 40
STEP = 7

norm_epsilon = 1e-06
masked_score = -1000000000.0
first_decay = 0.9
second_decay = 0.98
adam_epsilon = 1e-06
matrix_rate = 0.04
vector_rate = 0.5
weight_decay = 0.01

PATCH_STRIDE = 208
TEXT_STRIDE = 48
ITEM_ROWS = PATCH_STRIDE + TEXT_STRIDE

bf16 = jnp.bfloat16
f32 = jnp.float32
VMEM_LIMIT = 58 * 1024 * 1024
ATTENTION_US = 26
LIFT_US = 17
DROP_WEIGHT_US = 8
EXPERT_BACK_US = 18
ATTENTION_BACK_US = 27
DROP_US = 24


def adamw(weight, first_state, second_state, gradient, step_rate, decay_rate):
    first_new = first_decay * first_state + (1.0 - first_decay) * gradient
    second_new = second_decay * second_state + (1.0 - second_decay) * gradient * gradient
    first_hat = first_new / (1.0 - first_decay**STEP)
    second_hat = second_new / (1.0 - second_decay**STEP)
    weight_new = weight - step_rate * (
        first_hat / (jnp.sqrt(second_hat) + adam_epsilon) + decay_rate * weight
    )
    return (weight_new, first_new, second_new, weight_new.astype(bf16))


def dot(left, right, left_dim, right_dim):
    return lax.dot_general(
        left,
        right,
        (((left_dim,), (right_dim,)), ((), ())),
        preferred_element_type=f32,
    )


def loop(count, body):
    lax.fori_loop(0, count, lambda i, c: (body(i), c)[1], 0)


def rows_at(index, size):
    return pl.ds(pl.multiple_of(index * size, 16), size)


def norm_forward(values, gain, shift):
    centred = values - jnp.mean(values, axis=-1, keepdims=True)
    spread = jnp.mean(centred * centred, axis=-1, keepdims=True)
    return centred * lax.rsqrt(spread + norm_epsilon) * gain + shift


def norm_backward(values, gain, grad):
    centred = values - jnp.mean(values, axis=-1, keepdims=True)
    spread = jnp.mean(centred * centred, axis=-1, keepdims=True)
    scale = lax.rsqrt(spread + norm_epsilon)
    hat = centred * scale
    grad_hat = grad * gain
    grad_values = scale * (
        grad_hat
        - jnp.mean(grad_hat, axis=-1, keepdims=True)
        - hat * jnp.mean(grad_hat * hat, axis=-1, keepdims=True)
    )
    grad_gain = jnp.sum(grad * hat, axis=0, keepdims=True)
    grad_shift = jnp.sum(grad, axis=0, keepdims=True)
    return grad_values, grad_gain, grad_shift


def one_hot(row_place, first_row, count):
    place = lax.broadcasted_iota(jnp.int32, (count, row_place.shape[1]), 0) + first_row
    return (place == row_place).astype(bf16)


def relative_block(mine, block):
    other = jnp.bitwise_xor(mine, block)
    return jnp.bitwise_and(other, 1) * 4 + jnp.right_shift(other, 1)


def store_grad(grad_ref, mine, index, first, rows, value):
    value = value.astype(bf16)
    size = grad_ref.shape[-2]
    for part in range(rows // size):
        place = relative_block(mine, first // size + part)
        grad_ref[0, place, index] = value[part * size : (part + 1) * size]


def attend(query, key, value, allowed):
    scores = dot(query, key, 1, 1)
    scores = jnp.where(allowed, scores, masked_score)
    top = jnp.max(scores, axis=-1, keepdims=True)
    weights = jnp.exp(scores - top)
    total = jnp.sum(weights, axis=-1, keepdims=True)
    weights = (weights * (1.0 / total)).astype(bf16)
    return weights, dot(weights, value, 1, 0)


def attention_kernel(
    meta_ref,
    raw_ref,
    place_ref,
    hidden_ref,
    norm_ref,
    extra_ref,
    weight_ref,
    block_ref,
    normed_ref,
    residual_ref,
    joint_ref,
    mixed_ref,
    probs_ref,
    **sizes,
):
    main_rows, all_rows = sizes["main_rows"], sizes["all_rows"]

    @pl.when(pl.program_id(0) == 0)
    def _():
        def chunk(first, size):
            rows = pl.ds(first, size)
            picked = dot(one_hot(place_ref[...], first, size), raw_ref[...], 1, 0)
            picked = jnp.where(hidden_ref[rows, :] > 0, extra_ref[2:3, :], picked)
            block_ref[rows, :] = picked
            residual_ref[rows, :] = picked
            normed_ref[rows, :] = norm_forward(picked, norm_ref[0:1, :], norm_ref[1:2, :]).astype(bf16)

        loop(sizes["items"], lambda i: chunk(pl.multiple_of(i * ITEM_ROWS, 16), ITEM_ROWS))
        chunk(main_rows, all_rows - main_rows)

    attend_heads(meta_ref, weight_ref, normed_ref, residual_ref, joint_ref, mixed_ref, probs_ref, **sizes)


def attention_end_kernel(
    meta_ref,
    normed_ref,
    block_ref,
    before_ref,
    valid_ref,
    norm_ref,
    weight_ref,
    residual_ref,
    joint_ref,
    mixed_ref,
    probs_ref,
    feed_ref,
    square_ref,
    **sizes,
):
    items, main_rows = sizes["items"], sizes["main_rows"]

    @pl.when(pl.program_id(0) == 0)
    def _():
        residual_ref[...] = before_ref[...]

    attend_heads(meta_ref, weight_ref, normed_ref, residual_ref, joint_ref, mixed_ref, probs_ref, **sizes)

    @pl.when(pl.program_id(0) == pl.num_programs(0) - 1)
    def _():
        square_ref[...] = jnp.zeros_like(square_ref)

        def chunk(rows):
            residual = residual_ref[rows, :]
            feed_ref[rows, :] = norm_forward(residual, norm_ref[2:3, :], norm_ref[3:4, :]).astype(bf16)
            attended = (residual - block_ref[rows, :]) * valid_ref[rows, :]
            square_ref[...] += jnp.sum(attended * attended, axis=0, keepdims=True)

        loop(items, lambda i: chunk(rows_at(i, ITEM_ROWS)))
        chunk(pl.ds(main_rows, sizes["all_rows"] - main_rows))


def attend_heads(
    meta_ref,
    weight_ref,
    normed_ref,
    residual_ref,
    joint_ref,
    mixed_ref,
    probs_ref,
    *,
    items,
    heads,
    main_rows,
    all_rows,
):
    width = heads * HEAD_DIM
    tail_rows = all_rows - main_rows

    def project(rows):
        joint = dot(normed_ref[rows, :], weight_ref[0, :, : 3 * width], 1, 0)
        joint_ref[0, rows, :width] = (joint[:, :width].astype(bf16).astype(f32) * HEAD_DIM**-0.5).astype(bf16)
        joint_ref[0, rows, width:] = joint[:, width:].astype(bf16)

    loop(items, lambda i: project(rows_at(i, ITEM_ROWS)))
    project(pl.ds(main_rows, tail_rows))

    column = lax.broadcasted_iota(jnp.int32, (1, ITEM_ROWS), 1)

    def one_item(i):
        patch_rows = rows_at(i, PATCH_STRIDE)
        text_rows = pl.ds(pl.multiple_of(items * PATCH_STRIDE + i * TEXT_STRIDE, 16), TEXT_STRIDE)
        joint = jnp.concatenate([joint_ref[0, patch_rows, :], joint_ref[0, text_rows, :]], axis=0)
        allowed = (column < PATCHES) | (
            (column >= PATCH_STRIDE) & (column < PATCH_STRIDE + meta_ref[i])
        )
        outs = []
        for h in range(heads):
            part = lambda k: joint[:, k * width + h * HEAD_DIM : k * width + (h + 1) * HEAD_DIM]
            weights, out = attend(part(0), part(1), part(2), allowed)
            probs_ref[0, i, h] = weights
            outs.append(out.astype(bf16))
        mixed = jnp.concatenate(outs, axis=1)
        mixed_ref[0, patch_rows, :] = mixed[:PATCH_STRIDE]
        mixed_ref[0, text_rows, :] = mixed[PATCH_STRIDE:]

    loop(items, one_item)

    joint = joint_ref[0, main_rows:, :]
    allowed = lax.broadcasted_iota(jnp.int32, (1, tail_rows), 1) < meta_ref[items]
    outs = []
    for h in range(heads):
        part = lambda k: joint[:, k * width + h * HEAD_DIM : k * width + (h + 1) * HEAD_DIM]
        outs.append(attend(part(0), part(1), part(2), allowed)[1].astype(bf16))
    mixed_ref[0, main_rows:, :] = jnp.concatenate(outs, axis=1)

    def add_output(rows):
        residual_ref[rows, :] += dot(mixed_ref[0, rows, :], weight_ref[0, :, 3 * width :], 1, 1)

    loop(items, lambda i: add_output(rows_at(i, ITEM_ROWS)))
    add_output(pl.ds(main_rows, tail_rows))


def attention_back_kernel(
    mine_ref,
    grad_attended_ref,
    joint_ref,
    mixed_ref,
    probs_ref,
    normed_ref,
    weight_ref,
    grad_weight_ref,
    grad_normed_ref,
    grad_mixed_ref,
    grad_joint_ref,
    **sizes,
):
    @pl.when(pl.program_id(0) == 0)
    def _():
        grad_normed_ref[...] = jnp.zeros_like(grad_normed_ref)

    heads_back(
        mine_ref,
        grad_attended_ref,
        joint_ref,
        mixed_ref,
        probs_ref,
        normed_ref,
        weight_ref,
        grad_weight_ref,
        grad_normed_ref,
        grad_mixed_ref,
        grad_joint_ref,
        **sizes,
    )


def attention_back_end_kernel(
    mine_ref,
    grad_attended_ref,
    joint_ref,
    mixed_ref,
    probs_ref,
    normed_ref,
    weight_ref,
    before_ref,
    grad_residual_ref,
    block_ref,
    hidden_ref,
    place_ref,
    norm_ref,
    grad_weight_ref,
    grad_raw_ref,
    grad_norm_ref,
    grad_mask_ref,
    grad_normed_ref,
    grad_mixed_ref,
    grad_joint_ref,
    **sizes,
):
    @pl.when(pl.program_id(0) == 0)
    def _():
        grad_normed_ref[...] = before_ref[...]

    heads_back(
        mine_ref,
        grad_attended_ref,
        joint_ref,
        mixed_ref,
        probs_ref,
        normed_ref,
        weight_ref,
        grad_weight_ref,
        grad_normed_ref,
        grad_mixed_ref,
        grad_joint_ref,
        **sizes,
    )

    @pl.when(pl.program_id(0) == pl.num_programs(0) - 1)
    def _():
        grad_norm_ref[...] = jnp.zeros_like(grad_norm_ref)
        grad_mask_ref[...] = jnp.zeros_like(grad_mask_ref)

        def chunk(i):
            rows = rows_at(i, ITEM_ROWS)
            grad, gain, shift = norm_backward(block_ref[rows, :], norm_ref[0:1, :], grad_normed_ref[rows, :])
            grad_norm_ref[0:1, :] += gain
            grad_norm_ref[1:2, :] += shift
            grad = grad + grad_residual_ref[rows, :]
            hidden = hidden_ref[rows, :] > 0
            grad_mask_ref[...] += jnp.sum(jnp.where(hidden, grad, 0.0), axis=0, keepdims=True)
            grad_normed_ref[rows, :] = jnp.where(hidden, 0.0, grad)

        loop(sizes["items"], chunk)
        unplace(place_ref, grad_normed_ref, grad_raw_ref, grad_normed_ref.shape[0])


def heads_back(
    mine_ref,
    grad_attended_ref,
    joint_ref,
    mixed_ref,
    probs_ref,
    normed_ref,
    weight_ref,
    grad_weight_ref,
    grad_normed_ref,
    grad_mixed_ref,
    grad_joint_ref,
    *,
    items,
    heads,
):
    width = heads * HEAD_DIM
    half = HEAD_DIM**-0.5

    def mixed_grad(i):
        rows = rows_at(i, ITEM_ROWS)
        grad_mixed_ref[rows, :] = dot(
            grad_attended_ref[rows, :], weight_ref[0, :, 3 * width :], 1, 0
        ).astype(bf16)

    loop(items, mixed_grad)

    def one_item(i):
        patch_rows = rows_at(i, PATCH_STRIDE)
        text_rows = pl.ds(pl.multiple_of(items * PATCH_STRIDE + i * TEXT_STRIDE, 16), TEXT_STRIDE)
        joint = jnp.concatenate([joint_ref[0, patch_rows, :], joint_ref[0, text_rows, :]], axis=0)
        mixed = jnp.concatenate([mixed_ref[0, patch_rows, :], mixed_ref[0, text_rows, :]], axis=0)
        grad_mixed = jnp.concatenate([grad_mixed_ref[patch_rows, :], grad_mixed_ref[text_rows, :]], axis=0)
        grads = [[], [], []]
        for h in range(heads):
            part = lambda k: joint[:, k * width + h * HEAD_DIM : k * width + (h + 1) * HEAD_DIM]
            span = slice(h * HEAD_DIM, (h + 1) * HEAD_DIM)
            grad_out = grad_mixed[:, span]
            weights = probs_ref[0, i, h]
            grad_probs = dot(grad_out, part(2), 1, 1)
            mean_grad = jnp.sum(
                grad_out.astype(f32) * mixed[:, span].astype(f32), axis=-1, keepdims=True
            )
            grad_scores = (weights.astype(f32) * (grad_probs - mean_grad)).astype(bf16)
            grads[0].append((dot(grad_scores, part(1), 1, 0) * half).astype(bf16))
            grads[1].append(dot(grad_scores, part(0), 0, 0).astype(bf16))
            grads[2].append(dot(weights, grad_out, 0, 0).astype(bf16))
        grad_joint = jnp.concatenate(grads[0] + grads[1] + grads[2], axis=1)
        grad_joint_ref[patch_rows, :] = grad_joint[:PATCH_STRIDE]
        grad_joint_ref[text_rows, :] = grad_joint[PATCH_STRIDE:]

    loop(items, one_item)

    model_width = weight_ref.shape[1]
    for first in range(0, model_width, 384):
        cols = slice(first, first + 384)
        grad_weight = jnp.concatenate(
            [
                dot(normed_ref[:, cols], grad_joint_ref[...], 0, 0),
                dot(grad_attended_ref[:, cols], mixed_ref[0], 0, 0),
            ],
            axis=1,
        )
        store_grad(grad_weight_ref, mine_ref[0], 0, first, 384, grad_weight)

    def normed_grad(i):
        rows = rows_at(i, ITEM_ROWS)
        grad_normed_ref[rows, :] += dot(grad_joint_ref[rows, :], weight_ref[0, :, : 3 * width], 1, 1)

    loop(items, normed_grad)


def unplace(place_ref, source_ref, raw_ref, source_rows):
    source = source_ref[...].astype(bf16)
    raw_rows = raw_ref.shape[0]
    size = 240 if raw_rows % 240 == 0 else raw_rows

    def chunk(i):
        rows = rows_at(i, size)
        place = lax.broadcasted_iota(jnp.int32, (size, source_rows), 1)
        pick = (place == place_ref[rows, :]).astype(bf16)
        raw_ref[rows, :] = dot(pick, source, 1, 0).astype(bf16)

    loop(raw_rows // size, chunk)


def lift_kernel(feed_ref, weight_ref, acted_ref, slope_ref, *, vision_rows, all_rows):
    def piece(rows, expert):
        lifted = dot(feed_ref[rows, :], weight_ref[expert, 0], 1, 0)
        cumulative = 0.5 * (1.0 + lax.erf(lifted * (0.5**0.5)))
        density = jnp.exp(-0.5 * lifted * lifted) * ((2.0 * jnp.pi) ** -0.5)
        acted_ref[0, rows, :] = (lifted * cumulative).astype(bf16)
        slope_ref[0, rows, :] = (cumulative + lifted * density).astype(bf16)

    loop(vision_rows // PATCH_STRIDE, lambda i: piece(rows_at(i, PATCH_STRIDE), 0))
    text = all_rows - vision_rows
    loop(3, lambda i: piece(pl.ds(pl.multiple_of(vision_rows + i * (text // 3), 16), text // 3), 1))


def place_grad_kernel(raw_ref, place_ref, grad_ref, grad_bias_ref, *, vision_rows):
    def chunk(i):
        rows = rows_at(i, ITEM_ROWS)
        pick = one_hot(place_ref[...], i * ITEM_ROWS, ITEM_ROWS)
        grad_ref[rows, :] = dot(pick, raw_ref[...], 1, 0).astype(bf16)

    loop(grad_ref.shape[0] // ITEM_ROWS, chunk)
    grad_bias_ref[0:1, :] = jnp.sum(grad_ref[:vision_rows, :].astype(f32), axis=0, keepdims=True)
    grad_bias_ref[1:2, :] = jnp.sum(grad_ref[vision_rows:, :].astype(f32), axis=0, keepdims=True)


def expert_weight_grad(grad_weight_ref, mine, left_ref, right, vision_rows):
    rows_total, width = left_ref.shape
    for expert, rows in ((0, slice(0, vision_rows)), (1, slice(vision_rows, rows_total))):
        for first in range(0, width, 384):
            grad_weight = dot(left_ref[rows, first : first + 384], right(rows), 0, 0)
            store_grad(grad_weight_ref, mine, expert, first, 384, grad_weight)


def drop_weight_kernel(mine_ref, grad_ref, acted_ref, grad_weight_ref, *, vision_rows):
    expert_weight_grad(
        grad_weight_ref, mine_ref[0], grad_ref, lambda rows: acted_ref[0, rows, :], vision_rows
    )


def drop_kernel(
    acted_ref,
    residual_ref,
    valid_ref,
    place_ref,
    extra_ref,
    weight_ref,
    raw_ref,
    square_ref,
    total_ref,
    *,
    vision_rows,
    all_rows,
):
    step = pl.program_id(0)
    text = all_rows - vision_rows

    @pl.when(step == 0)
    def _():
        total_ref[:vision_rows, :] = jnp.broadcast_to(extra_ref[0:1, :], (vision_rows, total_ref.shape[1]))
        total_ref[vision_rows:, :] = jnp.broadcast_to(extra_ref[1:2, :], (text, total_ref.shape[1]))

    def piece(rows, expert):
        total_ref[rows, :] += dot(acted_ref[0, rows, :], weight_ref[expert, 0], 1, 1)

    def everything(body):
        loop(vision_rows // PATCH_STRIDE, lambda i: body(rows_at(i, PATCH_STRIDE), 0))
        loop(3, lambda i: body(pl.ds(pl.multiple_of(vision_rows + i * (text // 3), 16), text // 3), 1))

    everything(piece)

    @pl.when(step == pl.num_programs(0) - 1)
    def _():
        square_ref[...] = jnp.zeros_like(square_ref)

        def finish(rows, expert):
            fed = total_ref[rows, :]
            out = residual_ref[rows, :] + fed
            valid = valid_ref[rows, :]
            square_ref[0:1, :] += jnp.sum(valid * out * out, axis=0, keepdims=True)
            square_ref[1:2, :] += jnp.sum(valid * fed * fed, axis=0, keepdims=True)
            total_ref[rows, :] = out

        everything(finish)
        unplace(place_ref, total_ref, raw_ref, all_rows)


def expert_back_step(
    mine_ref, grad_ref, slope_ref, feed_ref, drop_ref, lift_ref, grad_weight_ref, total_ref, lifted_ref, vision_rows
):
    def piece(rows, expert):
        grad_acted = dot(grad_ref[rows, :], drop_ref[expert, 0], 1, 0)
        grad_lifted = (grad_acted * slope_ref[0, rows, :].astype(f32)).astype(bf16)
        lifted_ref[rows, :] = grad_lifted
        total_ref[rows, :] += dot(grad_lifted, lift_ref[expert, 0], 1, 1)

    loop(vision_rows // PATCH_STRIDE, lambda i: piece(rows_at(i, PATCH_STRIDE), 0))
    piece(pl.ds(vision_rows, grad_ref.shape[0] - vision_rows), 1)
    expert_weight_grad(
        grad_weight_ref, mine_ref[0], feed_ref, lambda rows: lifted_ref[rows, :], vision_rows
    )


def expert_back_kernel(
    mine_ref,
    grad_ref,
    slope_ref,
    feed_ref,
    drop_ref,
    lift_ref,
    grad_weight_ref,
    total_ref,
    lifted_ref,
    *,
    vision_rows,
):
    @pl.when(pl.program_id(0) == 0)
    def _():
        total_ref[...] = jnp.zeros_like(total_ref)

    expert_back_step(
        mine_ref, grad_ref, slope_ref, feed_ref, drop_ref, lift_ref, grad_weight_ref, total_ref, lifted_ref, vision_rows
    )


def expert_back_end_kernel(
    mine_ref,
    grad_ref,
    slope_ref,
    feed_ref,
    drop_ref,
    lift_ref,
    before_ref,
    residual_ref,
    norm_ref,
    grad_weight_ref,
    grad_residual_ref,
    grad_attended_ref,
    grad_norm_ref,
    lifted_ref,
    *,
    vision_rows,
):
    @pl.when(pl.program_id(0) == 0)
    def _():
        grad_residual_ref[...] = before_ref[...]

    expert_back_step(
        mine_ref,
        grad_ref,
        slope_ref,
        feed_ref,
        drop_ref,
        lift_ref,
        grad_weight_ref,
        grad_residual_ref,
        lifted_ref,
        vision_rows,
    )

    @pl.when(pl.program_id(0) == pl.num_programs(0) - 1)
    def _():
        grad_norm_ref[...] = jnp.zeros_like(grad_norm_ref)

        def chunk(i):
            rows = rows_at(i, ITEM_ROWS)
            grad, gain, shift = norm_backward(
                residual_ref[rows, :], norm_ref[2:3, :], grad_residual_ref[rows, :]
            )
            grad_norm_ref[0:1, :] += gain
            grad_norm_ref[1:2, :] += shift
            grad = grad + grad_ref[rows, :].astype(f32)
            grad_residual_ref[rows, :] = grad
            grad_attended_ref[rows, :] = grad.astype(bf16)

        loop(grad_ref.shape[0] // ITEM_ROWS, chunk)


def whole(*shape):
    return pl.BlockSpec(shape, lambda *_: (0,) * len(shape))


def stepped(*shape, first=0):
    return pl.BlockSpec(shape, lambda i, *_: (i + first,) + (0,) * (len(shape) - 1))


def stepped_pair(*shape, first=0):
    return pl.BlockSpec(shape, lambda i, *_: (0, i + first) + (0,) * (len(shape) - 2))


def call(kernel, name, steps, ins, outs, scratch, microseconds, scalars=(), aliases=None):
    return pl.pallas_call(
        kernel,
        name=name,
        grid_spec=pltpu.PrefetchScalarGridSpec(
            num_scalar_prefetch=len(scalars),
            grid=(steps,),
            in_specs=[block for _, block in ins],
            out_specs=[block for _, _, block in outs],
            scratch_shapes=scratch,
        ),
        out_shape=[jax.ShapeDtypeStruct(shape, kind) for shape, kind, _ in outs],
        compiler_params=pltpu.CompilerParams(
            dimension_semantics=("arbitrary",), vmem_limit_bytes=VMEM_LIMIT
        ),
        cost_estimate=pl.CostEstimate(
            flops=int(microseconds * 1e9), bytes_accessed=int(microseconds * 1e6), transcendentals=0
        ),
    )(*scalars, *[array for array, _ in ins])


def assemble_kernel(mine_ref, *refs):
    count = len(refs) - 2
    pieces, whole_ref, sems = refs[:count], refs[count], refs[count + 1]
    size = pieces[0].shape[2]
    for step in range(4):

        @pl.when(pl.program_id(0) == step)
        def _():
            core, y = 1 - step // 2, step % 2
            copies = []
            for kind, ref in enumerate(pieces[5 * core : 5 * core + 5]):
                x, from_y = ((0, 0), (1, 0), (0, 1), (1, 1), (1, 1))[kind]
                if from_y != y:
                    continue
                for i in range(ref.shape[0]):
                    z = i + 2 * (kind == 4)
                    group = jnp.bitwise_xor(mine_ref[0], 2 * z + x)
                    rows = pl.ds(pl.multiple_of(group * size, 16), size)
                    copies.append(
                        pltpu.make_async_copy(
                            ref.at[i], whole_ref.at[:, 0, rows, :], sems.at[len(copies)]
                        )
                    )
            for copy in copies:
                copy.start()
            for copy in copies:
                copy.wait()


def assemble(mine, pieces, parts, rows):
    count, _, columns = pieces[0].shape[1:]
    return pl.pallas_call(
        assemble_kernel,
        name="assemble",
        grid_spec=pltpu.PrefetchScalarGridSpec(
            num_scalar_prefetch=1,
            grid=(parts,),
            in_specs=[pl.BlockSpec(memory_space=pl.ANY)] * len(pieces),
            out_specs=pl.BlockSpec((count, 1, rows, columns), lambda i, mine: (0, i, 0, 0)),
            scratch_shapes=[pltpu.SemaphoreType.DMA((8,))],
        ),
        out_shape=jax.ShapeDtypeStruct((count, parts, rows, columns), bf16),
        compiler_params=pltpu.CompilerParams(
            dimension_semantics=("arbitrary",), vmem_limit_bytes=20 << 20
        ),
        cost_estimate=pl.CostEstimate(
            flops=0, bytes_accessed=4 * count * parts * rows * columns, transcendentals=0
        ),
    )(mine, *pieces)


def body(
    tokens,
    cotangent,
    text_lengths,
    modality,
    masked_positions,
    joint_weight,
    joint_first,
    joint_second,
    output_weight,
    output_first,
    output_second,
    lift_weight,
    lift_first,
    lift_second,
    drop_weight,
    drop_first,
    drop_second,
    norm_params,
    norm_first,
    norm_second,
    extra_params,
    extra_first,
    extra_second,
):
    micro_count, shard_rows, model_width = tokens.shape
    block_rows = modality.shape[1]
    parts = block_rows // shard_rows
    assert micro_count == parts
    items = text_lengths.shape[1]
    width = joint_weight.shape[2]
    heads = width // HEAD_DIM
    hidden_width = lift_weight.shape[2]
    shard = joint_weight.shape[1]
    vision_rows = items * PATCH_STRIDE
    main_rows = items * ITEM_ROWS
    tail = block_rows - items * PATCHES - TEXT_MAX - (items - 1)
    tail = (tail + 47) // 48 * 48
    all_rows = main_rows + tail
    assert 4 * width == model_width and hidden_width == model_width

    shard_attend = jnp.concatenate(
        [joint_weight[0], joint_weight[1], joint_weight[2], output_weight.T], axis=1
    ).astype(bf16)[None]
    shard_lift = lift_weight.astype(bf16)
    shard_drop = jnp.swapaxes(drop_weight, 1, 2).astype(bf16)

    groups = lax.axis_size("dp")
    cube = groups == 8
    piece = model_width // 8
    order = [1, 3, 0, 2]
    if cube:
        mine = jnp.stack([lax.axis_index("dp"), lax.axis_index("mp")]).astype(jnp.int32)
    else:
        mine = jnp.zeros((2,), jnp.int32)

    def after(values, *others):
        return lax.optimization_barrier((values, others))[0]

    def swap(values, axis, bit):
        size = lax.axis_size(axis)
        return lax.ppermute(values, axis, [(i, i ^ bit) for i in range(size)])

    def exchange(values):
        return lax.all_to_all(values, "mp", split_axis=0, concat_axis=1, tiled=True)[0]

    def give_back(values):
        return lax.all_to_all(
            values.reshape(parts, shard_rows, model_width), "mp", split_axis=0, concat_axis=0, tiled=True
        )

    def gather(values):
        whole_values = lax.all_gather(values, ("mp", "dp"), axis=1, tiled=True)
        shape = (-1, parts, model_width, values.shape[2])
        return jnp.stack([whole_values.reshape(shape)[:, i] for i in order], axis=1)

    def gather_line(values):
        return jnp.stack([values] + [swap(values, "dp", bit) for bit in (2, 4, 6)])

    def gather_plane(line):
        return swap(line, "dp", 1), swap(line, "mp", 2)

    def gather_corner(along_x, along_y):
        return swap(along_x[:2], "mp", 2), swap(along_y[2:], "dp", 1)

    def gather_cores(line, along, corner):
        own = (line,) + along + corner
        return assemble(
            mine, own + tuple(swap(part, "mp", 1) for part in own), parts, model_width
        )

    def add(*terms):
        total = terms[0].astype(f32)
        for term in terms[1:]:
            total = total + term.astype(f32)
        return total

    def scatter(keep, send):
        shape = (2, 2, 4) + keep.shape[2:]
        both = jnp.stack([keep.reshape(shape), send.reshape(shape)], axis=1)
        both = jnp.transpose(both, (4, 0, 1, 3, 2, 5, 6))
        both = both.reshape(both.shape[0], parts * model_width, shape[-1])
        both = lax.psum_scatter(both, ("mp", "dp"), scatter_dimension=1, tiled=True)
        return both.astype(f32)

    def scatter_corner(keep, received):
        shape = (2, 2, 4) + keep.shape[2:]
        keep, received = keep.reshape(shape), received.reshape(shape)
        return add(keep[1, 1], received[1, 1]).astype(bf16)

    def scatter_plane(keep, received, from_x, from_y):
        shape = (2, 2, 4) + keep.shape[2:]
        keep, received = keep.reshape(shape), received.reshape(shape)
        part_x = add(keep[0, 1], received[0, 1])
        part_y = add(keep[1, 0], received[1, 0])
        part_x = jnp.concatenate([part_x[:2], add(part_x[2:], from_y)]).astype(bf16)
        part_y = jnp.concatenate([add(part_y[:2], from_x), part_y[2:]]).astype(bf16)
        return part_x, part_y

    def scatter_line(keep, received, from_x, from_y):
        shape = (2, 2, 4) + keep.shape[2:]
        keep, received = keep.reshape(shape), received.reshape(shape)
        return add(keep[0, 0], received[0, 0], from_x, from_y).astype(bf16)

    def send_corner(corner):
        return swap(corner[:2], "dp", 1), swap(corner[2:], "mp", 2)

    def send_plane(part_x, part_y):
        return swap(part_x, "dp", 1), swap(part_y, "mp", 2)

    def send_line(line):
        return tuple(swap(line[i], "dp", 2 * i) for i in (1, 2, 3))

    micro = lax.axis_index("mp")
    lengths = lax.dynamic_index_in_dim(text_lengths, micro, 0, keepdims=False)
    masked = lax.dynamic_index_in_dim(masked_positions, micro, 0, keepdims=False)
    item_ids = jnp.arange(items, dtype=jnp.int32)
    sizes = PATCHES + lengths
    ends = jnp.sum(jnp.where(item_ids[:, None] <= item_ids[None, :], sizes[:, None], 0), axis=0)
    used = jnp.sum(sizes)

    def place_of(row):
        segment = jnp.sum((row[..., None] >= ends).astype(jnp.int32), axis=-1)
        start = jnp.sum(jnp.where(row[..., None] >= ends, sizes, 0), axis=-1)
        inside = row - start
        return jnp.where(
            segment == items,
            main_rows + inside,
            jnp.where(
                inside < PATCHES,
                PATCH_STRIDE * segment + inside,
                vision_rows + TEXT_STRIDE * segment + inside - PATCHES,
            ),
        )

    place_row = place_of(jnp.arange(block_rows, dtype=jnp.int32))[None, :]
    place_column = place_of(jnp.arange(block_rows, dtype=jnp.int32))[:, None]
    targets = (vision_rows + TEXT_STRIDE * item_ids[:, None] + masked).reshape(-1)
    spots = jnp.arange(all_rows, dtype=jnp.int32)
    hidden = jnp.any(spots[:, None] == targets[None, :], axis=1).astype(jnp.int32)[:, None]
    text_spot = spots - vision_rows
    text_item = text_spot // TEXT_STRIDE
    text_end = jnp.sum(jnp.where(text_item[:, None] == item_ids, lengths, 0), axis=1)
    valid = jnp.where(
        text_spot < 0, spots % PATCH_STRIDE < PATCHES, text_spot - text_item * TEXT_STRIDE < text_end
    )
    valid = valid.astype(f32)[:, None]
    meta = jnp.concatenate([lengths, (block_rows - used)[None]])

    def rows_of(count, kind):
        return ((count, model_width), kind, whole(count, model_width))

    def plain(values):
        return (values, whole(*values.shape))

    def heads_out():
        return [
            ((2, all_rows, 3 * width), bf16, stepped(1, all_rows, 3 * width)),
            ((2, all_rows, width), bf16, stepped(1, all_rows, width)),
            (
                (2, items, heads, ITEM_ROWS, ITEM_ROWS),
                bf16,
                stepped(1, items, heads, ITEM_ROWS, ITEM_ROWS),
            ),
        ]

    def part_weight(values, first, count=2):
        return (values, stepped_pair(count, 1, *values.shape[2:], first=first))

    def grad_out(count):
        shape = (2, 8, count, piece, model_width)
        return (shape, bf16, stepped(1, *shape[1:]))

    head_sizes = dict(items=items, heads=heads)
    row_sizes = dict(main_rows=main_rows, all_rows=all_rows)

    def attention(raw, weights):
        return call(
            functools.partial(attention_kernel, **head_sizes, **row_sizes),
            "attention",
            2,
            [plain(raw), plain(place_row), plain(hidden), plain(norm_params), plain(extra_params)]
            + [(weights, stepped(1, model_width, model_width))],
            [rows_of(all_rows, f32), rows_of(all_rows, bf16), rows_of(all_rows, f32)] + heads_out(),
            [],
            ATTENTION_US,
            (meta,),
        )

    def attention_end(normed, block_input, residual, weights):
        return call(
            functools.partial(attention_end_kernel, **head_sizes, **row_sizes),
            "attention_end",
            2,
            [plain(normed), plain(block_input), plain(residual), plain(valid), plain(norm_params)]
            + [(weights, stepped(1, model_width, model_width, first=2))],
            [rows_of(all_rows, f32)] + heads_out() + [rows_of(all_rows, bf16), rows_of(1, f32)],
            [],
            ATTENTION_US,
            (meta,),
        )

    def lift(feed_input, weights):
        shape = (parts, all_rows, hidden_width)
        return call(
            functools.partial(lift_kernel, vision_rows=vision_rows, all_rows=all_rows),
            "lift",
            parts,
            [plain(feed_input), part_weight(weights, 0)],
            [(shape, bf16, stepped(1, *shape[1:]))] * 2,
            [],
            LIFT_US,
        )

    def place_grad(raw):
        return call(
            functools.partial(place_grad_kernel, vision_rows=vision_rows),
            "place_grad",
            1,
            [plain(raw), plain(place_row)],
            [rows_of(main_rows, bf16), rows_of(2, f32)],
            [],
            5,
        )

    def drop_weight_grad(grad_rows, acted, first):
        return call(
            functools.partial(drop_weight_kernel, vision_rows=vision_rows),
            "drop_weight_grad",
            2,
            [plain(grad_rows), (acted, stepped(1, main_rows, hidden_width, first=first))],
            [grad_out(2)],
            [],
            DROP_WEIGHT_US,
            (mine,),
        )[0]

    def expert_ins(grad_rows, slope, feed_input, drop_weights, lift_weights, first):
        return [
            plain(grad_rows),
            (slope, stepped(1, main_rows, hidden_width, first=first)),
            (feed_input, whole(main_rows, model_width)),
            part_weight(drop_weights, first),
            part_weight(lift_weights, first),
        ]

    def expert_back(*args):
        return call(
            functools.partial(expert_back_kernel, vision_rows=vision_rows),
            "expert_back",
            2,
            expert_ins(*args, 0),
            [grad_out(2), rows_of(main_rows, f32)],
            [pltpu.VMEM((main_rows, hidden_width), bf16)],
            EXPERT_BACK_US,
            (mine,),
        )

    def expert_back_end(before, residual, *args):
        return call(
            functools.partial(expert_back_end_kernel, vision_rows=vision_rows),
            "expert_back_end",
            2,
            expert_ins(*args, 2)
            + [plain(before), (residual, whole(main_rows, model_width)), plain(norm_params)],
            [grad_out(2), rows_of(main_rows, f32), rows_of(main_rows, bf16), rows_of(2, f32)],
            [pltpu.VMEM((main_rows, hidden_width), bf16)],
            EXPERT_BACK_US,
            (mine,),
        )

    def heads_ins(grad_attended, joint_rows, mixed, probs, normed, weights, first):
        return [
            plain(grad_attended),
            (joint_rows, stepped(1, main_rows, 3 * width)),
            (mixed, stepped(1, main_rows, width)),
            (probs, stepped(1, *probs.shape[1:])),
            (normed, whole(main_rows, model_width)),
            (weights, stepped(1, model_width, model_width, first=first)),
        ]

    heads_scratch = [
        pltpu.VMEM((main_rows, width), bf16),
        pltpu.VMEM((main_rows, 3 * width), bf16),
    ]

    def attention_back(*args):
        return call(
            functools.partial(attention_back_kernel, **head_sizes),
            "attention_back",
            2,
            heads_ins(*args, 0),
            [grad_out(1), rows_of(main_rows, f32)],
            heads_scratch,
            ATTENTION_BACK_US,
            (mine,),
        )

    def attention_back_end(before, grad_residual, block_input, *args):
        return call(
            functools.partial(attention_back_end_kernel, **head_sizes),
            "attention_back_end",
            2,
            heads_ins(*args, 2)
            + [
                plain(before),
                plain(grad_residual),
                (block_input, whole(main_rows, model_width)),
                (hidden, whole(main_rows, 1)),
                plain(place_column),
                plain(norm_params),
            ],
            [grad_out(1), rows_of(block_rows, bf16), rows_of(2, f32), rows_of(1, f32)],
            [pltpu.VMEM((main_rows, model_width), f32)] + heads_scratch,
            ATTENTION_BACK_US,
            (mine,),
        )

    def drop(acted, residual, weights):
        return call(
            functools.partial(drop_kernel, vision_rows=vision_rows, all_rows=all_rows),
            "drop",
            parts,
            [(acted, stepped(1, all_rows, hidden_width)), plain(residual), plain(valid)]
            + [plain(place_column), plain(extra_params), part_weight(weights, 0)],
            [rows_of(block_rows, bf16), rows_of(2, f32)],
            [pltpu.VMEM((all_rows, model_width), f32)],
            DROP_US,
        )

    raw_tokens = exchange(tokens)
    if cube:
        line_attend = gather_line(shard_attend)
        plane_attend = gather_plane(line_attend)
        line_lift = gather_line(after(shard_lift, line_attend))
        corner_attend = gather_corner(*plane_attend)
        line_drop = gather_line(after(shard_drop, line_lift))
        attend_all = gather_cores(line_attend, plane_attend, corner_attend)[0]
        plane_lift = gather_plane(after(line_lift, corner_attend))
    else:
        attend_all = gather(shard_attend)[0]

    block_input, normed, residual, *heads_first = attention(raw_tokens, attend_all)
    if cube:
        plane_lift, residual = after((plane_lift, residual))
        corner_lift = gather_corner(*plane_lift)
        raw_grad = exchange(after(cotangent.astype(bf16), plane_lift))
    else:
        raw_grad = exchange(cotangent.astype(bf16))
    residual, *heads_second, feed_input, attended_square = attention_end(
        normed, block_input, residual, attend_all
    )
    if cube:
        corner_lift, feed_input = after((corner_lift, feed_input))
        plane_drop = gather_plane(after(line_drop, corner_lift))
        lift_all = gather_cores(line_lift, plane_lift, corner_lift)
    else:
        lift_all = gather(shard_lift)
    acted, slope = lift(feed_input, lift_all)
    if cube:
        plane_drop, acted, slope, raw_grad = after((plane_drop, acted, slope, raw_grad))
        corner_drop = gather_corner(*plane_drop)
    grad_rows, grad_bias = place_grad(raw_grad)
    drop_send = drop_weight_grad(grad_rows, acted, 0)
    if cube:
        drop_received = swap(drop_send, "mp", 1)
    drop_keep = drop_weight_grad(grad_rows, after(acted, drop_send), 2)
    if cube:
        corner_drop, drop_keep = after((corner_drop, drop_keep))
        drop_all = gather_cores(line_drop, plane_drop, corner_drop)
        drop_all, drop_received = after((drop_all, drop_received))
        corner = scatter_corner(drop_keep, drop_received)
        corner, grad_rows = after((corner, grad_rows))
        from_corner = send_corner(corner)
    else:
        drop_all = gather(shard_drop)
        drop_grad = scatter(drop_keep, drop_send)

    lift_send, grad_feed = expert_back(grad_rows, slope, feed_input, drop_all, lift_all)
    if cube:
        lift_received = swap(lift_send, "mp", 1)
        from_corner, grad_feed = after((from_corner, grad_feed))
        plane = scatter_plane(drop_keep, drop_received, *from_corner)
        plane, grad_feed = after((plane, grad_feed))
        from_plane = send_plane(*plane)
    lift_keep, grad_residual, grad_attended, grad_norm_second = expert_back_end(
        grad_feed, residual, grad_rows, slope, feed_input, drop_all, lift_all
    )
    if cube:
        lift_received, from_plane, grad_attended = after((lift_received, from_plane, grad_attended))
        line = scatter_line(drop_keep, drop_received, *from_plane)
        lift_corner = scatter_corner(lift_keep, lift_received)
        line, lift_corner, grad_attended = after((line, lift_corner, grad_attended))
        from_line = send_line(line)
        from_corner = send_corner(lift_corner)
    else:
        lift_grad = scatter(lift_keep, lift_send)

    attend_send, grad_normed = attention_back(grad_attended, *heads_first, normed, attend_all)
    if cube:
        attend_received = swap(attend_send, "mp", 1)
        from_line, from_corner, grad_normed = after((from_line, from_corner, grad_normed))
        drop_grad = add(line[0], *from_line)
        plane = scatter_plane(lift_keep, lift_received, *from_corner)
        plane, grad_normed = after((plane, grad_normed))
        from_plane = send_plane(*plane)
    attend_keep, grad_raw, grad_norm_first, grad_mask = attention_back_end(
        grad_normed, grad_residual, block_input, grad_attended, *heads_second, normed, attend_all
    )
    if cube:
        attend_received, from_plane, attend_keep = after((attend_received, from_plane, attend_keep))
        line = scatter_line(lift_keep, lift_received, *from_plane)
        attend_corner = scatter_corner(attend_keep, attend_received)
        line, attend_corner, acted = after((line, attend_corner, acted))
        from_line = send_line(line)
        from_corner = send_corner(attend_corner)
    input_grad = give_back(grad_raw).astype(f32)
    raw_out, feed_square = drop(acted, residual, drop_all)
    block_output = give_back(raw_out).astype(f32)
    if cube:
        from_line, from_corner, raw_out = after((from_line, from_corner, raw_out))
        lift_grad = add(line[0], *from_line)
        from_plane = send_plane(*scatter_plane(attend_keep, attend_received, *from_corner))
        line = scatter_line(attend_keep, attend_received, *from_plane)
        attend_grad = add(line[0], *send_line(line))[0]
    else:
        attend_grad = scatter(attend_keep, attend_send)[0]

    squares = jnp.stack(
        [jnp.sum(feed_square[0]), jnp.sum(attended_square), jnp.sum(feed_square[1]), used.astype(f32)]
    )
    small = jnp.concatenate(
        [
            grad_norm_first,
            grad_norm_second,
            grad_bias,
            grad_mask,
            jnp.pad(squares, (0, model_width - 4))[None],
        ],
        axis=0,
    )
    if cube:
        for axis, bit in (("mp", 1), ("mp", 2), ("dp", 1), ("dp", 2), ("dp", 4)):
            small = small + swap(small, axis, bit)
    else:
        small = lax.psum(small, ("dp", "mp"))
    norm_total, extra_total = small[:4], small[4:7]
    rms_values = jnp.sqrt(small[7, :3] / (small[7, 3] * model_width))

    joint_grad = jnp.stack([attend_grad[:, k * width : (k + 1) * width] for k in range(3)])
    output_grad = attend_grad[:, 3 * width :].T
    drop_grad = jnp.swapaxes(drop_grad, 1, 2)
    results = [block_output, input_grad, rms_values]
    results += adamw(joint_weight, joint_first, joint_second, joint_grad, matrix_rate, weight_decay)
    results += adamw(output_weight, output_first, output_second, output_grad, matrix_rate, weight_decay)
    results += adamw(lift_weight, lift_first, lift_second, lift_grad, matrix_rate, weight_decay)
    results += adamw(drop_weight, drop_first, drop_second, drop_grad, matrix_rate, weight_decay)
    results += adamw(norm_params, norm_first, norm_second, norm_total, vector_rate, 0.0)
    results += adamw(extra_params, extra_first, extra_second, extra_total, vector_rate, 0.0)
    return tuple(results)


def solution(mesh):
    rows = P(None, ("dp", "mp"), None)
    joint, output, lift, drop = (
        P(None, "dp", "mp"),
        P("mp", "dp"),
        P(None, "dp", "mp"),
        P(None, "mp", "dp"),
    )
    return jax.shard_map(
        body,
        mesh=mesh,
        in_specs=(rows, rows, P(None, "dp"), P(None, "dp"), P(None, "dp", None))
        + (joint,) * 3
        + (output,) * 3
        + (lift,) * 3
        + (drop,) * 3
        + (P(),) * 6,
        out_specs=(rows, rows, P())
        + (joint,) * 4
        + (output,) * 4
        + (lift,) * 4
        + (drop,) * 4
        + (P(),) * 8,
        check_vma=False,
    )
```

```python
import functools

import jax
import jax.numpy as jnp
from jax import lax
from jax.experimental import pallas as pl
from jax.experimental.pallas import tpu as pltpu
from jax.sharding import PartitionSpec as P

HEAD_DIM = 64
PATCHES = 197
TEXT_MAX = 40
STEP = 7

norm_epsilon = 1e-06
masked_score = -1000000000.0
first_decay = 0.9
second_decay = 0.98
adam_epsilon = 1e-06
matrix_rate = 0.04
vector_rate = 0.5
weight_decay = 0.01

PATCH_STRIDE = 208
TEXT_STRIDE = 48
ITEM_ROWS = PATCH_STRIDE + TEXT_STRIDE

bf16 = jnp.bfloat16
f32 = jnp.float32
VMEM_LIMIT = 58 * 1024 * 1024
ATTENTION_US = 38
LIFT_US = 16
DROP_WEIGHT_US = 7
EXPERT_BACK_US = 17
ATTENTION_BACK_US = 19
DROP_US = 17


def adamw(weight, first_state, second_state, gradient, step_rate, decay_rate):
    first_new = first_decay * first_state + (1.0 - first_decay) * gradient
    second_new = second_decay * second_state + (1.0 - second_decay) * gradient * gradient
    first_hat = first_new / (1.0 - first_decay**STEP)
    second_hat = second_new / (1.0 - second_decay**STEP)
    weight_new = weight - step_rate * (
        first_hat / (jnp.sqrt(second_hat) + adam_epsilon) + decay_rate * weight
    )
    return (weight_new, first_new, second_new, weight_new.astype(bf16))


def dot(left, right, left_dim, right_dim):
    return lax.dot_general(
        left,
        right,
        (((left_dim,), (right_dim,)), ((), ())),
        preferred_element_type=f32,
    )


def loop(count, body):
    lax.fori_loop(0, count, lambda i, c: (body(i), c)[1], 0)


def rows_at(index, size):
    return pl.ds(pl.multiple_of(index * size, 16), size)


def norm_forward(values, gain, shift):
    centred = values - jnp.mean(values, axis=-1, keepdims=True)
    spread = jnp.mean(centred * centred, axis=-1, keepdims=True)
    return centred * lax.rsqrt(spread + norm_epsilon) * gain + shift


def norm_backward(values, gain, grad):
    centred = values - jnp.mean(values, axis=-1, keepdims=True)
    spread = jnp.mean(centred * centred, axis=-1, keepdims=True)
    scale = lax.rsqrt(spread + norm_epsilon)
    hat = centred * scale
    grad_hat = grad * gain
    grad_values = scale * (
        grad_hat
        - jnp.mean(grad_hat, axis=-1, keepdims=True)
        - hat * jnp.mean(grad_hat * hat, axis=-1, keepdims=True)
    )
    grad_gain = jnp.sum(grad * hat, axis=0, keepdims=True)
    grad_shift = jnp.sum(grad, axis=0, keepdims=True)
    return grad_values, grad_gain, grad_shift


def one_hot(row_place, first_row, count):
    place = lax.broadcasted_iota(jnp.int32, (count, row_place.shape[1]), 0) + first_row
    return (place == row_place).astype(bf16)


def relative_block(mine, block):
    other = jnp.bitwise_xor(mine, block)
    return jnp.bitwise_and(other, 1) * 4 + jnp.right_shift(other, 1)


def piece_copies(pieces, mine, place_of, sems):
    even, *odd = pieces
    blocks = [(even, i, 2 * i) for i in range(4)]
    z = 0
    for ref in odd:
        for i in range(ref.shape[0]):
            blocks.append((ref, i, 2 * z + 1))
            z += 1
    size = even.shape[2]
    copies = []
    for index, (ref, i, block) in enumerate(blocks):
        first = jnp.bitwise_xor(mine, block) * size
        rows = pl.ds(pl.multiple_of(first, 16), size)
        copies.append(pltpu.make_async_copy(ref.at[i], place_of(rows), sems.at[index]))
    return copies


def step_copies(pieces, mine, weight_ref, sems):
    by_step = []
    for step in range(4):
        even, odd, high, front, back = pieces[5 * (1 - step // 2) :][:5]
        parts = (high, front, back) if step % 2 else (even, odd)
        place_of = lambda rows, step=step: weight_ref.at[:, step, rows, :]
        by_step.append(piece_copies(parts, mine, place_of, sems.at[step]))
    return by_step


def start_all(by_step):
    for copies in by_step:
        for copy in copies:
            copy.start()


def out_copy(weight_ref, out_ref, out_sems, step):
    return pltpu.make_async_copy(weight_ref.at[:, step], out_ref.at[:, step], out_sems.at[step])


def wait_step(by_step, weight_ref, out_ref, out_sems):
    for step, copies in enumerate(by_step):

        @pl.when(pl.program_id(0) == step)
        def _():
            for copy in copies:
                copy.wait()
            out_copy(weight_ref, out_ref, out_sems, step).start()


def wait_out(weight_ref, out_ref, out_sems):
    for step in range(4):
        out_copy(weight_ref, out_ref, out_sems, step).wait()


def store_grad(grad_ref, mine, index, first, rows, value):
    value = value.astype(bf16)
    size = grad_ref.shape[-2]
    for part in range(rows // size):
        place = relative_block(mine, first // size + part)
        grad_ref[0, place, index] = value[part * size : (part + 1) * size]


def attend(queries, keys, values, allowed):
    scores = [dot(key, query, 1, 1) for query, key in zip(queries, keys)]
    scores = [jnp.where(mask, score, masked_score) for mask, score in zip(allowed, scores)]
    tops = [jnp.max(score, axis=0, keepdims=True) for score in scores]
    weights = [jnp.exp(score - top) for score, top in zip(scores, tops)]
    totals = [jnp.sum(weight, axis=0, keepdims=True) for weight in weights]
    weights = [(weight * (1.0 / total)).astype(bf16) for weight, total in zip(weights, totals)]
    return weights, [dot(value, weight, 0, 0) for value, weight in zip(values, weights)]


def item_slices(items, i):
    first = items * PATCH_STRIDE + i * TEXT_STRIDE
    return slice(i * PATCH_STRIDE, (i + 1) * PATCH_STRIDE), slice(first, first + TEXT_STRIDE)


def item_rows(ref, index, items, i):
    patch_rows, text_rows = item_slices(items, i)
    return jnp.concatenate([ref[index + (patch_rows,)], ref[index + (text_rows,)]], axis=0)


def head_columns(rows, kind, heads, h):
    first = (kind * heads + h) * HEAD_DIM
    return rows[:, first : first + HEAD_DIM]


def attention_kernel(
    meta_ref, raw_ref, place_ref, hidden_ref, valid_ref, norm_ref, extra_ref, *refs, **sizes
):
    pieces, outs = refs[:10], refs[10:]
    block_ref, normed_ref, residual_ref, feed_ref, square_ref = outs[:5]
    out_ref, joint_ref, mixed_ref, probs_ref, weight_ref, sems, out_sems = outs[5:]
    items, main_rows, all_rows = sizes["items"], sizes["main_rows"], sizes["all_rows"]
    step = pl.program_id(0)
    by_step = step_copies(pieces, meta_ref[items + 1], weight_ref, sems)

    @pl.when(step == 0)
    def _():
        start_all(by_step)

        def chunk(first, size):
            rows = pl.ds(first, size)
            picked = dot(one_hot(place_ref[...], first, size), raw_ref[...], 1, 0)
            picked = jnp.where(hidden_ref[rows, :] > 0, extra_ref[2:3, :], picked)
            block_ref[rows, :] = picked
            residual_ref[rows, :] = picked
            normed_ref[rows, :] = norm_forward(picked, norm_ref[0:1, :], norm_ref[1:2, :]).astype(bf16)

        loop(items, lambda i: chunk(pl.multiple_of(i * ITEM_ROWS, 16), ITEM_ROWS))
        chunk(main_rows, all_rows - main_rows)

    wait_step(by_step, weight_ref, out_ref, out_sems)
    attend_heads(
        meta_ref, weight_ref.at[0, step], normed_ref, residual_ref, joint_ref, mixed_ref, probs_ref, **sizes
    )

    @pl.when(step == pl.num_programs(0) - 1)
    def _():
        square_ref[...] = jnp.zeros_like(square_ref)

        def chunk(rows):
            residual = residual_ref[rows, :]
            feed_ref[rows, :] = norm_forward(residual, norm_ref[2:3, :], norm_ref[3:4, :]).astype(bf16)
            attended = (residual - block_ref[rows, :]) * valid_ref[rows, :]
            square_ref[...] += jnp.sum(attended * attended, axis=0, keepdims=True)

        loop(items, lambda i: chunk(rows_at(i, ITEM_ROWS)))
        chunk(pl.ds(main_rows, all_rows - main_rows))
        wait_out(weight_ref, out_ref, out_sems)


def attend_heads(
    meta_ref,
    weight_ref,
    normed_ref,
    residual_ref,
    joint_ref,
    mixed_ref,
    probs_ref,
    *,
    items,
    heads,
    main_rows,
    all_rows,
):
    width = heads * HEAD_DIM
    tail_rows = all_rows - main_rows

    def project(rows):
        joint = dot(normed_ref[rows, :], weight_ref[:, : 3 * width], 1, 0)
        joint_ref[0, rows, :width] = (joint[:, :width].astype(bf16).astype(f32) * HEAD_DIM**-0.5).astype(bf16)
        joint_ref[0, rows, width:] = joint[:, width:].astype(bf16)

    project(pl.ds(0, all_rows))

    key_row = lax.broadcasted_iota(jnp.int32, (ITEM_ROWS, 1), 0)
    blocks = [item_rows(joint_ref, (0,), items, i) for i in range(items)]
    masks = [
        (key_row < PATCHES)
        | ((key_row >= PATCH_STRIDE) & (key_row < PATCH_STRIDE + meta_ref[i]))
        for i in range(items)
    ]
    blocks.append(joint_ref[0, main_rows:, :])
    masks.append(lax.broadcasted_iota(jnp.int32, (tail_rows, 1), 0) < meta_ref[items])
    pairs = [(i, h) for i in range(items + 1) for h in range(heads)]
    weights, outs = attend(
        *[[head_columns(blocks[i], kind, heads, h) for i, h in pairs] for kind in range(3)],
        [masks[i] for i, _ in pairs],
    )
    for (i, h), weight in zip(pairs, weights):
        if i < items:
            probs_ref[0, i, h] = weight
    for i in range(items + 1):
        mixed = jnp.concatenate(outs[i * heads : (i + 1) * heads], axis=0).T.astype(bf16)
        if i == items:
            mixed_ref[0, main_rows:, :] = mixed
        else:
            patch_rows, text_rows = item_slices(items, i)
            mixed_ref[0, patch_rows, :] = mixed[:PATCH_STRIDE]
            mixed_ref[0, text_rows, :] = mixed[PATCH_STRIDE:]

    def add_output(rows):
        residual_ref[rows, :] += dot(mixed_ref[0, rows, :], weight_ref[:, 3 * width :], 1, 1)

    add_output(pl.ds(0, all_rows))


def attention_back_kernel(
    mine_ref,
    grad_attended_ref,
    joint_ref,
    mixed_ref,
    probs_ref,
    normed_ref,
    weight_ref,
    grad_weight_ref,
    grad_normed_ref,
    grad_mixed_ref,
    grad_joint_ref,
    **sizes,
):
    @pl.when(pl.program_id(0) == 0)
    def _():
        grad_normed_ref[...] = jnp.zeros_like(grad_normed_ref)

    heads_back(
        mine_ref,
        grad_attended_ref,
        joint_ref,
        mixed_ref,
        probs_ref,
        normed_ref,
        weight_ref,
        grad_weight_ref,
        grad_normed_ref,
        grad_mixed_ref,
        grad_joint_ref,
        **sizes,
    )


def attention_back_end_kernel(
    mine_ref,
    grad_attended_ref,
    joint_ref,
    mixed_ref,
    probs_ref,
    normed_ref,
    weight_ref,
    before_ref,
    grad_weight_ref,
    grad_normed_ref,
    grad_mixed_ref,
    grad_joint_ref,
    **sizes,
):
    @pl.when(pl.program_id(0) == 0)
    def _():
        grad_normed_ref[...] = before_ref[...]

    heads_back(
        mine_ref,
        grad_attended_ref,
        joint_ref,
        mixed_ref,
        probs_ref,
        normed_ref,
        weight_ref,
        grad_weight_ref,
        grad_normed_ref,
        grad_mixed_ref,
        grad_joint_ref,
        **sizes,
    )


def input_grad_kernel(
    grad_normed_ref,
    grad_residual_ref,
    block_ref,
    hidden_ref,
    place_ref,
    norm_ref,
    grad_raw_ref,
    grad_norm_ref,
    grad_mask_ref,
    grad_block_ref,
):
    grad_norm_ref[...] = jnp.zeros_like(grad_norm_ref)
    grad_mask_ref[...] = jnp.zeros_like(grad_mask_ref)

    def chunk(i):
        rows = rows_at(i, ITEM_ROWS)
        grad, gain, shift = norm_backward(block_ref[rows, :], norm_ref[0:1, :], grad_normed_ref[rows, :])
        grad_norm_ref[0:1, :] += gain
        grad_norm_ref[1:2, :] += shift
        grad = grad + grad_residual_ref[rows, :]
        hidden = hidden_ref[rows, :] > 0
        grad_mask_ref[...] += jnp.sum(jnp.where(hidden, grad, 0.0), axis=0, keepdims=True)
        grad_block_ref[rows, :] = jnp.where(hidden, 0.0, grad).astype(bf16)

    loop(grad_normed_ref.shape[0] // ITEM_ROWS, chunk)
    unplace(place_ref, grad_block_ref, grad_raw_ref, grad_block_ref.shape[0])


def heads_back(
    mine_ref,
    grad_attended_ref,
    joint_ref,
    mixed_ref,
    probs_ref,
    normed_ref,
    weight_ref,
    grad_weight_ref,
    grad_normed_ref,
    grad_mixed_ref,
    grad_joint_ref,
    *,
    items,
    heads,
):
    width = heads * HEAD_DIM
    half = HEAD_DIM**-0.5

    grad_mixed_ref[...] = dot(grad_attended_ref[...], weight_ref[0, :, 3 * width :], 1, 0).astype(bf16)

    blocks = [item_rows(joint_ref, (0,), items, i) for i in range(items)]
    outs = [item_rows(grad_mixed_ref, (), items, i) for i in range(items)]
    products = [
        (outs[i].astype(f32) * item_rows(mixed_ref, (0,), items, i).astype(f32)).T for i in range(items)
    ]
    pairs = [(i, h) for i in range(items) for h in range(heads)]
    queries, keys, values = [
        [head_columns(blocks[i], kind, heads, h) for i, h in pairs] for kind in range(3)
    ]
    grad_outs = [head_columns(outs[i], 0, heads, h) for i, h in pairs]
    weights = [probs_ref[0, i, h] for i, h in pairs]
    grad_probs = [dot(value, grad_out, 1, 1) for value, grad_out in zip(values, grad_outs)]
    means = [
        jnp.sum(products[i][h * HEAD_DIM : (h + 1) * HEAD_DIM], axis=0, keepdims=True) for i, h in pairs
    ]
    grad_scores = [
        (weight.astype(f32) * (grad - mean)).astype(bf16)
        for weight, grad, mean in zip(weights, grad_probs, means)
    ]
    grad_values = [dot(weight, grad_out, 1, 0).astype(bf16) for weight, grad_out in zip(weights, grad_outs)]
    grad_keys = [dot(score, query, 1, 0).astype(bf16) for score, query in zip(grad_scores, queries)]
    grad_queries = [dot(key, score, 0, 0) * half for key, score in zip(keys, grad_scores)]
    for i in range(items):
        own = slice(i * heads, (i + 1) * heads)
        grad_query = jnp.concatenate(grad_queries[own], axis=0).T.astype(bf16)
        grad_joint = jnp.concatenate([grad_query] + grad_keys[own] + grad_values[own], axis=1)
        patch_rows, text_rows = item_slices(items, i)
        grad_joint_ref[patch_rows, :] = grad_joint[:PATCH_STRIDE]
        grad_joint_ref[text_rows, :] = grad_joint[PATCH_STRIDE:]

    model_width = weight_ref.shape[1]
    for first in range(0, model_width, 384):
        cols = slice(first, first + 384)
        grad_weight = jnp.concatenate(
            [
                dot(normed_ref[:, cols], grad_joint_ref[...], 0, 0),
                dot(grad_attended_ref[:, cols], mixed_ref[0], 0, 0),
            ],
            axis=1,
        )
        store_grad(grad_weight_ref, mine_ref[0], 0, first, 384, grad_weight)

    grad_normed_ref[...] += dot(grad_joint_ref[...], weight_ref[0, :, : 3 * width], 1, 1)


def unplace(place_ref, source_ref, raw_ref, source_rows):
    source = source_ref[...].astype(bf16)
    raw_rows = raw_ref.shape[0]
    size = 240 if raw_rows % 240 == 0 else raw_rows

    def chunk(i):
        rows = rows_at(i, size)
        place = lax.broadcasted_iota(jnp.int32, (size, source_rows), 1)
        pick = (place == place_ref[rows, :]).astype(bf16)
        raw_ref[rows, :] = dot(pick, source, 1, 0).astype(bf16)

    loop(raw_rows // size, chunk)


def lift_kernel(mine_ref, feed_ref, *refs, vision_rows, all_rows):
    pieces, (acted_ref, slope_ref, out_ref, weight_ref, sems, out_sems) = refs[:10], refs[10:]
    by_step = step_copies(pieces, mine_ref[0], weight_ref, sems)

    @pl.when(pl.program_id(0) == 0)
    def _():
        start_all(by_step)

    wait_step(by_step, weight_ref, out_ref, out_sems)

    def piece(rows, expert):
        lifted = dot(feed_ref[rows, :], weight_ref[expert, pl.program_id(0)], 1, 0)
        cumulative = 0.5 * (1.0 + lax.erf(lifted * (0.5**0.5)))
        density = jnp.exp(-0.5 * lifted * lifted) * ((2.0 * jnp.pi) ** -0.5)
        acted_ref[0, rows, :] = (lifted * cumulative).astype(bf16)
        slope_ref[0, rows, :] = (cumulative + lifted * density).astype(bf16)

    loop(2, lambda i: piece(rows_at(i, vision_rows // 2), 0))
    piece(pl.ds(vision_rows, all_rows - vision_rows), 1)

    @pl.when(pl.program_id(0) == pl.num_programs(0) - 1)
    def _():
        wait_out(weight_ref, out_ref, out_sems)


def place_grad_kernel(raw_ref, place_ref, grad_ref, grad_bias_ref, *, vision_rows):
    def chunk(i):
        rows = rows_at(i, ITEM_ROWS)
        pick = one_hot(place_ref[...], i * ITEM_ROWS, ITEM_ROWS)
        grad_ref[rows, :] = dot(pick, raw_ref[...], 1, 0).astype(bf16)

    loop(grad_ref.shape[0] // ITEM_ROWS, chunk)
    grad_bias_ref[0:1, :] = jnp.sum(grad_ref[:vision_rows, :].astype(f32), axis=0, keepdims=True)
    grad_bias_ref[1:2, :] = jnp.sum(grad_ref[vision_rows:, :].astype(f32), axis=0, keepdims=True)


def expert_weight_grad(grad_weight_ref, mine, left_ref, right, vision_rows):
    rows_total, width = left_ref.shape
    for expert, rows in ((0, slice(0, vision_rows)), (1, slice(vision_rows, rows_total))):
        for first in range(0, width, 384):
            grad_weight = dot(left_ref[rows, first : first + 384], right(rows), 0, 0)
            store_grad(grad_weight_ref, mine, expert, first, 384, grad_weight)


def drop_weight_kernel(mine_ref, grad_ref, acted_ref, grad_weight_ref, *, vision_rows):
    expert_weight_grad(
        grad_weight_ref, mine_ref[0], grad_ref, lambda rows: acted_ref[0, rows, :], vision_rows
    )


def drop_kernel(
    mine_ref,
    acted_ref,
    residual_ref,
    valid_ref,
    place_ref,
    extra_ref,
    weight_ref,
    raw_ref,
    square_ref,
    total_ref,
    *,
    vision_rows,
    all_rows,
):
    step = pl.program_id(0)
    text = all_rows - vision_rows

    @pl.when(step == 0)
    def _():
        total_ref[:vision_rows, :] = jnp.broadcast_to(extra_ref[0:1, :], (vision_rows, total_ref.shape[1]))
        total_ref[vision_rows:, :] = jnp.broadcast_to(extra_ref[1:2, :], (text, total_ref.shape[1]))

    def piece(rows, expert):
        total_ref[rows, :] += dot(acted_ref[0, rows, :], weight_ref[expert, 0], 1, 1)

    piece(pl.ds(0, vision_rows), 0)
    piece(pl.ds(vision_rows, text), 1)

    @pl.when(step == pl.num_programs(0) - 1)
    def _():
        square_ref[...] = jnp.zeros_like(square_ref)

        def finish(rows, expert):
            fed = total_ref[rows, :]
            out = residual_ref[rows, :] + fed
            valid = valid_ref[rows, :]
            square_ref[0:1, :] += jnp.sum(valid * out * out, axis=0, keepdims=True)
            square_ref[1:2, :] += jnp.sum(valid * fed * fed, axis=0, keepdims=True)
            total_ref[rows, :] = out

        loop(vision_rows // PATCH_STRIDE, lambda i: finish(rows_at(i, PATCH_STRIDE), 0))
        loop(3, lambda i: finish(pl.ds(pl.multiple_of(vision_rows + i * (text // 3), 16), text // 3), 1))
        unplace(place_ref, total_ref, raw_ref, all_rows)


def expert_back_step(
    mine_ref, grad_ref, slope_ref, feed_ref, drop_ref, lift_ref, grad_weight_ref, total_ref, lifted_ref, vision_rows
):
    def piece(rows, expert):
        grad_acted = dot(grad_ref[rows, :], drop_ref[expert, 0], 1, 0)
        grad_lifted = (grad_acted * slope_ref[0, rows, :].astype(f32)).astype(bf16)
        lifted_ref[rows, :] = grad_lifted
        total_ref[rows, :] += dot(grad_lifted, lift_ref[expert, 0], 1, 1)

    piece(pl.ds(0, vision_rows), 0)
    piece(pl.ds(vision_rows, grad_ref.shape[0] - vision_rows), 1)
    expert_weight_grad(
        grad_weight_ref, mine_ref[0], feed_ref, lambda rows: lifted_ref[rows, :], vision_rows
    )


def expert_back_kernel(
    mine_ref,
    grad_ref,
    slope_ref,
    feed_ref,
    drop_ref,
    lift_ref,
    grad_weight_ref,
    total_ref,
    lifted_ref,
    *,
    vision_rows,
):
    @pl.when(pl.program_id(0) == 0)
    def _():
        total_ref[...] = jnp.zeros_like(total_ref)

    expert_back_step(
        mine_ref, grad_ref, slope_ref, feed_ref, drop_ref, lift_ref, grad_weight_ref, total_ref, lifted_ref, vision_rows
    )


def expert_back_end_kernel(
    mine_ref,
    grad_ref,
    slope_ref,
    feed_ref,
    drop_ref,
    lift_ref,
    before_ref,
    residual_ref,
    norm_ref,
    grad_weight_ref,
    grad_residual_ref,
    grad_attended_ref,
    grad_norm_ref,
    lifted_ref,
    *,
    vision_rows,
):
    @pl.when(pl.program_id(0) == 0)
    def _():
        grad_residual_ref[...] = before_ref[...]

    expert_back_step(
        mine_ref,
        grad_ref,
        slope_ref,
        feed_ref,
        drop_ref,
        lift_ref,
        grad_weight_ref,
        grad_residual_ref,
        lifted_ref,
        vision_rows,
    )

    @pl.when(pl.program_id(0) == pl.num_programs(0) - 1)
    def _():
        grad_norm_ref[...] = jnp.zeros_like(grad_norm_ref)

        def chunk(i):
            rows = rows_at(i, ITEM_ROWS)
            grad, gain, shift = norm_backward(
                residual_ref[rows, :], norm_ref[2:3, :], grad_residual_ref[rows, :]
            )
            grad_norm_ref[0:1, :] += gain
            grad_norm_ref[1:2, :] += shift
            grad = grad + grad_ref[rows, :].astype(f32)
            grad_residual_ref[rows, :] = grad
            grad_attended_ref[rows, :] = grad.astype(bf16)

        loop(grad_ref.shape[0] // ITEM_ROWS, chunk)


def whole(*shape):
    return pl.BlockSpec(shape, lambda *_: (0,) * len(shape))


def stepped(*shape, first=0):
    return pl.BlockSpec(shape, lambda i, *_: (i + first,) + (0,) * (len(shape) - 1))


def stepped_pair(*shape, first=0):
    return pl.BlockSpec(shape, lambda i, *_: (0, i + first) + (0,) * (len(shape) - 2))


def part_of(step, mine):
    return jnp.bitwise_xor(mine[1], (step % 2) * 2 + 1 - step // 2)


def part_pair(*shape, first=0):
    return pl.BlockSpec(
        shape, lambda i, mine: (0, part_of(i + first, mine)) + (0,) * (len(shape) - 2)
    )


def anywhere(values):
    return (values, pl.BlockSpec(memory_space=pl.ANY))


def call(kernel, name, steps, ins, outs, scratch, microseconds, scalars=(), aliases=None):
    return pl.pallas_call(
        kernel,
        name=name,
        grid_spec=pltpu.PrefetchScalarGridSpec(
            num_scalar_prefetch=len(scalars),
            grid=(steps,),
            in_specs=[block for _, block in ins],
            out_specs=[block for _, _, block in outs],
            scratch_shapes=scratch,
        ),
        out_shape=[jax.ShapeDtypeStruct(shape, kind) for shape, kind, _ in outs],
        input_output_aliases=aliases or {},
        compiler_params=pltpu.CompilerParams(
            dimension_semantics=("arbitrary",), vmem_limit_bytes=VMEM_LIMIT
        ),
        cost_estimate=pl.CostEstimate(
            flops=int(microseconds * 1e9), bytes_accessed=int(microseconds * 1e6), transcendentals=0
        ),
    )(*scalars, *[array for array, _ in ins])


def body(
    tokens,
    cotangent,
    text_lengths,
    modality,
    masked_positions,
    joint_weight,
    joint_first,
    joint_second,
    output_weight,
    output_first,
    output_second,
    lift_weight,
    lift_first,
    lift_second,
    drop_weight,
    drop_first,
    drop_second,
    norm_params,
    norm_first,
    norm_second,
    extra_params,
    extra_first,
    extra_second,
):
    micro_count, shard_rows, model_width = tokens.shape
    block_rows = modality.shape[1]
    parts = block_rows // shard_rows
    assert micro_count == parts
    items = text_lengths.shape[1]
    width = joint_weight.shape[2]
    heads = width // HEAD_DIM
    hidden_width = lift_weight.shape[2]
    shard = joint_weight.shape[1]
    vision_rows = items * PATCH_STRIDE
    main_rows = items * ITEM_ROWS
    tail = block_rows - items * PATCHES - TEXT_MAX - (items - 1)
    tail = (tail + 47) // 48 * 48
    all_rows = main_rows + tail
    assert 4 * width == model_width and hidden_width == model_width

    shard_attend = jnp.concatenate(
        [joint_weight[0], joint_weight[1], joint_weight[2], output_weight.T], axis=1
    ).astype(bf16)[None]
    shard_lift = lift_weight.astype(bf16)
    shard_drop = jnp.swapaxes(drop_weight, 1, 2).astype(bf16)

    groups = lax.axis_size("dp")
    cube = groups == 8
    piece = model_width // 8
    if cube:
        mine = jnp.stack([lax.axis_index("dp"), lax.axis_index("mp")]).astype(jnp.int32)
    else:
        mine = jnp.zeros((2,), jnp.int32)

    def after(values, *others):
        return lax.optimization_barrier((values, others))[0]

    def swap(values, axis, bit):
        size = lax.axis_size(axis)
        return lax.ppermute(values, axis, [(i, i ^ bit) for i in range(size)])

    def exchange(values):
        return lax.all_to_all(values, "mp", split_axis=0, concat_axis=1, tiled=True)[0]

    def give_back(values):
        return lax.all_to_all(
            values.reshape(parts, shard_rows, model_width), "mp", split_axis=0, concat_axis=0, tiled=True
        )

    def gather(values):
        whole_values = lax.all_gather(values, ("mp", "dp"), axis=1, tiled=True)
        return whole_values.reshape(-1, parts, model_width, values.shape[2])

    def gather_pieces(values):
        whole_values = jnp.swapaxes(gather(values).reshape(-1, parts, 4, 2, piece, model_width), 0, 3)
        pieces = []
        for core in range(2):
            low, high = whole_values[:, core], whole_values[:, 2 + core]
            pieces += [low[0], low[1], high[0], high[1, :2], high[1, 2:]]
        return pieces

    def gather_line(values):
        return jnp.stack([values] + [swap(values, "dp", bit) for bit in (2, 4, 6)])

    def gather_plane(line):
        return swap(line, "dp", 1), swap(line, "mp", 2)

    def gather_corner(along_x, along_y):
        return swap(along_x[:2], "mp", 2), swap(along_y[2:], "dp", 1)

    def gather_cores(line, along, corner):
        own = (line,) + along + corner
        return own + tuple(swap(part, "mp", 1) for part in own)

    def add(*terms):
        total = terms[0].astype(f32)
        for term in terms[1:]:
            total = total + term.astype(f32)
        return total

    def scatter(keep, send):
        shape = (2, 2, 4) + keep.shape[2:]
        both = jnp.stack([keep.reshape(shape), send.reshape(shape)], axis=1)
        both = jnp.transpose(both, (4, 0, 1, 3, 2, 5, 6))
        return reduce(both.reshape(both.shape[0], parts * model_width, shape[-1]))

    def reduce(values):
        values = lax.psum_scatter(values, ("mp", "dp"), scatter_dimension=1, tiled=True)
        return values.astype(f32)

    def scatter_corner(keep, received):
        shape = (2, 2, 4) + keep.shape[2:]
        keep, received = keep.reshape(shape), received.reshape(shape)
        return add(keep[1, 1], received[1, 1]).astype(bf16)

    def scatter_plane(keep, received, from_x, from_y):
        shape = (2, 2, 4) + keep.shape[2:]
        keep, received = keep.reshape(shape), received.reshape(shape)
        part_x = add(keep[0, 1], received[0, 1])
        part_y = add(keep[1, 0], received[1, 0])
        part_x = jnp.concatenate([part_x[:2], add(part_x[2:], from_y)]).astype(bf16)
        part_y = jnp.concatenate([add(part_y[:2], from_x), part_y[2:]]).astype(bf16)
        return part_x, part_y

    def scatter_line(keep, received, from_x, from_y):
        shape = (2, 2, 4) + keep.shape[2:]
        keep, received = keep.reshape(shape), received.reshape(shape)
        return add(keep[0, 0], received[0, 0], from_x, from_y).astype(bf16)

    def send_corner(corner):
        return swap(corner[:2], "dp", 1), swap(corner[2:], "mp", 2)

    def send_plane(part_x, part_y):
        return swap(part_x, "dp", 1), swap(part_y, "mp", 2)

    def send_line(line):
        return tuple(swap(line[i], "dp", 2 * i) for i in (1, 2, 3))

    micro = lax.axis_index("mp")
    lengths = lax.dynamic_index_in_dim(text_lengths, micro, 0, keepdims=False)
    masked = lax.dynamic_index_in_dim(masked_positions, micro, 0, keepdims=False)
    item_ids = jnp.arange(items, dtype=jnp.int32)
    sizes = PATCHES + lengths
    ends = jnp.sum(jnp.where(item_ids[:, None] <= item_ids[None, :], sizes[:, None], 0), axis=0)
    used = jnp.sum(sizes)

    def place_of(row):
        segment = jnp.sum((row[..., None] >= ends).astype(jnp.int32), axis=-1)
        start = jnp.sum(jnp.where(row[..., None] >= ends, sizes, 0), axis=-1)
        inside = row - start
        return jnp.where(
            segment == items,
            main_rows + inside,
            jnp.where(
                inside < PATCHES,
                PATCH_STRIDE * segment + inside,
                vision_rows + TEXT_STRIDE * segment + inside - PATCHES,
            ),
        )

    place_row = place_of(jnp.arange(block_rows, dtype=jnp.int32))[None, :]
    place_column = place_of(jnp.arange(block_rows, dtype=jnp.int32))[:, None]
    targets = (vision_rows + TEXT_STRIDE * item_ids[:, None] + masked).reshape(-1)
    spots = jnp.arange(all_rows, dtype=jnp.int32)
    hidden = jnp.any(spots[:, None] == targets[None, :], axis=1).astype(jnp.int32)[:, None]
    text_spot = spots - vision_rows
    text_item = text_spot // TEXT_STRIDE
    text_end = jnp.sum(jnp.where(text_item[:, None] == item_ids, lengths, 0), axis=1)
    valid = jnp.where(
        text_spot < 0, spots % PATCH_STRIDE < PATCHES, text_spot - text_item * TEXT_STRIDE < text_end
    )
    valid = valid.astype(f32)[:, None]
    meta = jnp.concatenate([lengths, (block_rows - used)[None], mine[:1]])

    def rows_of(count, kind):
        return ((count, model_width), kind, whole(count, model_width))

    def plain(values):
        return (values, whole(*values.shape))

    def heads_out():
        shapes = [
            (parts, all_rows, 3 * width),
            (parts, all_rows, width),
            (parts, items, heads, ITEM_ROWS, ITEM_ROWS),
        ]
        return [(shape, bf16, stepped(1, *shape[1:])) for shape in shapes]

    def whole_weight(count):
        shape = (count, parts, model_width, model_width)
        return (shape, bf16, pl.BlockSpec(memory_space=pl.ANY)), [
            pltpu.VMEM(shape, bf16),
            pltpu.SemaphoreType.DMA((parts, 8)),
            pltpu.SemaphoreType.DMA((parts,)),
        ]

    def part_weight(values, first, count=2):
        return (values, stepped_pair(count, 1, *values.shape[2:], first=first))

    def grad_out(count):
        shape = (2, 8, count, piece, model_width)
        return (shape, bf16, stepped(1, *shape[1:]))

    head_sizes = dict(items=items, heads=heads)
    row_sizes = dict(main_rows=main_rows, all_rows=all_rows)

    def attention(raw, pieces):
        weight_out, scratch = whole_weight(1)
        block_input, normed, residual, feed_input, squared, weights, *made = call(
            functools.partial(attention_kernel, **head_sizes, **row_sizes),
            "attention",
            parts,
            [plain(raw), plain(place_row), plain(hidden), plain(valid), plain(norm_params)]
            + [plain(extra_params)]
            + [anywhere(values) for values in pieces],
            [rows_of(all_rows, f32), rows_of(all_rows, bf16), rows_of(all_rows, f32)]
            + [rows_of(all_rows, bf16), rows_of(1, f32), weight_out]
            + heads_out(),
            scratch,
            ATTENTION_US,
            (meta,),
        )
        return block_input, normed, residual, feed_input, squared, [weights[0], *made]

    def lift(feed_input, pieces):
        shape = (parts, all_rows, hidden_width)
        weight_out, scratch = whole_weight(2)
        return call(
            functools.partial(lift_kernel, vision_rows=vision_rows, all_rows=all_rows),
            "lift",
            parts,
            [plain(feed_input)] + [anywhere(values) for values in pieces],
            [(shape, bf16, stepped(1, *shape[1:]))] * 2 + [weight_out],
            scratch,
            LIFT_US,
            (mine,),
        )

    def place_grad(raw):
        return call(
            functools.partial(place_grad_kernel, vision_rows=vision_rows),
            "place_grad",
            1,
            [plain(raw), plain(place_row)],
            [rows_of(main_rows, bf16), rows_of(2, f32)],
            [],
            5,
        )

    def drop_weight_grad(grad_rows, acted, first):
        return call(
            functools.partial(drop_weight_kernel, vision_rows=vision_rows),
            "drop_weight_grad",
            2,
            [plain(grad_rows), (acted, stepped(1, main_rows, hidden_width, first=first))],
            [grad_out(2)],
            [],
            DROP_WEIGHT_US,
            (mine,),
        )[0]

    def expert_ins(grad_rows, slope, feed_input, drop_weights, lift_weights, first):
        return [
            plain(grad_rows),
            (slope, stepped(1, main_rows, hidden_width, first=first)),
            (feed_input, whole(main_rows, model_width)),
            (drop_weights, part_pair(2, 1, *drop_weights.shape[2:], first=first)),
            part_weight(lift_weights, first),
        ]

    def expert_back(*args):
        return call(
            functools.partial(expert_back_kernel, vision_rows=vision_rows),
            "expert_back",
            2,
            expert_ins(*args, 0),
            [grad_out(2), rows_of(main_rows, f32)],
            [pltpu.VMEM((main_rows, hidden_width), bf16)],
            EXPERT_BACK_US,
            (mine,),
        )

    def expert_back_end(before, residual, *args):
        return call(
            functools.partial(expert_back_end_kernel, vision_rows=vision_rows),
            "expert_back_end",
            2,
            expert_ins(*args, 2)
            + [plain(before), (residual, whole(main_rows, model_width)), plain(norm_params)],
            [grad_out(2), rows_of(main_rows, f32), rows_of(main_rows, bf16), rows_of(2, f32)],
            [pltpu.VMEM((main_rows, hidden_width), bf16)],
            EXPERT_BACK_US,
            (mine,),
        )

    def heads_ins(grad_attended, normed, weights, joint_rows, mixed, probs, first):
        return [
            plain(grad_attended),
            (joint_rows, stepped(1, main_rows, 3 * width, first=first)),
            (mixed, stepped(1, main_rows, width, first=first)),
            (probs, stepped(1, *probs.shape[1:], first=first)),
            (normed, whole(main_rows, model_width)),
            (weights, stepped(1, model_width, model_width, first=first)),
        ]

    heads_scratch = [
        pltpu.VMEM((main_rows, width), bf16),
        pltpu.VMEM((main_rows, 3 * width), bf16),
    ]

    def attention_back(*args):
        return call(
            functools.partial(attention_back_kernel, **head_sizes),
            "attention_back",
            2,
            heads_ins(*args, 0),
            [grad_out(1), rows_of(main_rows, f32)],
            heads_scratch,
            ATTENTION_BACK_US,
            (mine,),
        )

    def attention_back_end(before, *args):
        return call(
            functools.partial(attention_back_end_kernel, **head_sizes),
            "attention_back_end",
            2,
            heads_ins(*args, 2) + [plain(before)],
            [grad_out(1), rows_of(main_rows, f32)],
            heads_scratch,
            ATTENTION_BACK_US,
            (mine,),
        )

    def finish_input_grad(grad_normed, grad_residual, block_input):
        return call(
            input_grad_kernel,
            "input_grad",
            1,
            [
                plain(grad_normed),
                plain(grad_residual),
                (block_input, whole(main_rows, model_width)),
                (hidden, whole(main_rows, 1)),
                plain(place_column),
                plain(norm_params),
            ],
            [rows_of(block_rows, bf16), rows_of(2, f32), rows_of(1, f32)],
            [pltpu.VMEM((main_rows, model_width), bf16)],
            9,
        )

    def drop(acted, residual, weights):
        return call(
            functools.partial(drop_kernel, vision_rows=vision_rows, all_rows=all_rows),
            "drop",
            parts,
            [(acted, stepped(1, all_rows, hidden_width)), plain(residual), plain(valid)]
            + [plain(place_column), plain(extra_params)]
            + [(weights, part_pair(2, 1, *weights.shape[2:]))],
            [rows_of(block_rows, bf16), rows_of(2, f32)],
            [pltpu.VMEM((all_rows, model_width), f32)],
            DROP_US,
            (mine,),
        )

    raw_tokens = exchange(tokens)
    if cube:
        line_attend, raw_tokens = after((gather_line(shard_attend), raw_tokens))
        line_lift = gather_line(after(shard_lift, line_attend))
        plane_attend = gather_plane(line_attend)
        corner_attend = gather_corner(*plane_attend)
        attend_pieces = gather_cores(line_attend, plane_attend, corner_attend)
        line_lift, raw_tokens = after((line_lift, raw_tokens))
        drop_all = gather(after(shard_drop, line_lift, corner_attend))
        plane_lift = gather_plane(line_lift)
        raw_grad = exchange(after(cotangent.astype(bf16), line_lift))
    else:
        attend_pieces = gather_pieces(shard_attend)
        drop_all = gather(shard_drop)
        raw_grad = exchange(cotangent.astype(bf16))

    block_input, normed, residual, feed_input, attended_square, made = attention(raw_tokens, attend_pieces)
    raw_grad, feed_input = after((raw_grad, feed_input))
    if cube:
        plane_lift, feed_input = after((plane_lift, feed_input))
        corner_lift = gather_corner(*plane_lift)
    grad_rows, grad_bias = place_grad(raw_grad)
    if cube:
        corner_lift, grad_rows = after((corner_lift, grad_rows))
        lift_pieces = gather_cores(line_lift, plane_lift, corner_lift)
    else:
        lift_pieces = gather_pieces(shard_lift)
    acted, slope, lift_all = lift(feed_input, lift_pieces)
    drop_send = drop_weight_grad(grad_rows, acted, 0)
    if cube:
        drop_received = swap(drop_send, "mp", 1)
    drop_keep = drop_weight_grad(grad_rows, after(acted, drop_send), 2)
    if cube:
        drop_received, drop_keep = after((drop_received, drop_keep))
        corner = scatter_corner(drop_keep, drop_received)
        corner, grad_rows = after((corner, grad_rows))
        from_corner = send_corner(corner)
    else:
        drop_grad = scatter(drop_keep, drop_send)

    lift_send, grad_feed = expert_back(grad_rows, slope, feed_input, drop_all, lift_all)
    if cube:
        lift_received = swap(lift_send, "mp", 1)
        from_corner, grad_feed = after((from_corner, grad_feed))
        plane = scatter_plane(drop_keep, drop_received, *from_corner)
        plane, grad_feed = after((plane, grad_feed))
        from_plane = send_plane(*plane)
    lift_keep, grad_residual, grad_attended, grad_norm_second = expert_back_end(
        grad_feed, residual, grad_rows, slope, feed_input, drop_all, lift_all
    )
    if cube:
        lift_received, from_plane, grad_attended = after((lift_received, from_plane, grad_attended))
        lift_corner = scatter_corner(lift_keep, lift_received)
        drop_line = scatter_line(drop_keep, drop_received, *from_plane)
        lift_corner, drop_line, acted = after((lift_corner, drop_line, acted))
        from_corner = send_corner(lift_corner)
        from_line = send_line(drop_line)
    else:
        lift_grad = scatter(lift_keep, lift_send)
    raw_out, feed_square = drop(acted, residual, drop_all)
    if cube:
        from_corner, raw_out = after((from_corner, raw_out))
        plane = scatter_plane(lift_keep, lift_received, *from_corner)
        from_line, plane, grad_attended = after((from_line, plane, grad_attended))
        drop_grad = add(drop_line[0], *from_line)
        from_plane = send_plane(*plane)

    attend_send, grad_normed = attention_back(grad_attended, normed, *made)
    if cube:
        attend_received = swap(attend_send, "mp", 1)
        from_plane, raw_out, grad_normed = after((from_plane, raw_out, grad_normed))
        lift_line = scatter_line(lift_keep, lift_received, *from_plane)
        lift_line, grad_normed = after((lift_line, grad_normed))
        from_line = send_line(lift_line)
    block_output = give_back(raw_out)
    attend_keep, grad_normed = attention_back_end(grad_normed, grad_attended, normed, *made)
    if cube:
        attend_received, from_line, attend_keep = after((attend_received, from_line, attend_keep))
        corner = scatter_corner(attend_keep, attend_received)
        corner, block_output, grad_normed = after((corner, block_output, grad_normed))
        from_corner = send_corner(corner)
    block_output = block_output.astype(f32)
    grad_raw, grad_norm_first, grad_mask = finish_input_grad(grad_normed, grad_residual, block_input)
    if cube:
        from_corner, grad_raw = after((from_corner, grad_raw))
        plane = scatter_plane(attend_keep, attend_received, *from_corner)
        from_plane = send_plane(*plane)
        lift_grad = add(lift_line[0], *from_line)
        from_plane, grad_raw = after((from_plane, grad_raw))
        line = scatter_line(attend_keep, attend_received, *from_plane)
        attend_grad = add(line[0], *send_line(line))[0]
    else:
        attend_grad = scatter(attend_keep, attend_send)[0]
    input_grad = give_back(grad_raw).astype(f32)

    squares = jnp.stack(
        [jnp.sum(feed_square[0]), jnp.sum(attended_square), jnp.sum(feed_square[1]), used.astype(f32)]
    )
    small = jnp.concatenate(
        [
            grad_norm_first,
            grad_norm_second,
            grad_bias,
            grad_mask,
            jnp.pad(squares, (0, model_width - 4))[None],
        ],
        axis=0,
    )
    if cube:
        small = after(small, plane)
        for axis, bit in (("mp", 1), ("dp", 2), ("dp", 4)):
            small = small + swap(small, axis, bit)
        small = after(small, line)
        for axis, bit in (("mp", 2), ("dp", 1)):
            small = small + swap(small, axis, bit)
    else:
        small = lax.psum(small, ("dp", "mp"))
    norm_total, extra_total = small[:4], small[4:7]
    rms_values = jnp.sqrt(small[7, :3] / (small[7, 3] * model_width))

    joint_grad = jnp.stack([attend_grad[:, k * width : (k + 1) * width] for k in range(3)])
    output_grad = attend_grad[:, 3 * width :].T
    drop_grad = jnp.swapaxes(drop_grad, 1, 2)
    results = [block_output, input_grad, rms_values]
    results += adamw(joint_weight, joint_first, joint_second, joint_grad, matrix_rate, weight_decay)
    results += adamw(output_weight, output_first, output_second, output_grad, matrix_rate, weight_decay)
    results += adamw(lift_weight, lift_first, lift_second, lift_grad, matrix_rate, weight_decay)
    results += adamw(drop_weight, drop_first, drop_second, drop_grad, matrix_rate, weight_decay)
    results += adamw(norm_params, norm_first, norm_second, norm_total, vector_rate, 0.0)
    results += adamw(extra_params, extra_first, extra_second, extra_total, vector_rate, 0.0)
    return tuple(results)


def solution(mesh):
    rows = P(None, ("dp", "mp"), None)
    joint, output, lift, drop = (
        P(None, "dp", "mp"),
        P("mp", "dp"),
        P(None, "dp", "mp"),
        P(None, "mp", "dp"),
    )
    return jax.shard_map(
        body,
        mesh=mesh,
        in_specs=(rows, rows, P(None, "dp"), P(None, "dp"), P(None, "dp", None))
        + (joint,) * 3
        + (output,) * 3
        + (lift,) * 3
        + (drop,) * 3
        + (P(),) * 6,
        out_specs=(rows, rows, P())
        + (joint,) * 4
        + (output,) * 4
        + (lift,) * 4
        + (drop,) * 4
        + (P(),) * 8,
        check_vma=False,
    )
```

```python
import functools

import jax
import jax.numpy as jnp
from jax import lax
from jax.experimental import pallas as pl
from jax.experimental.pallas import tpu as pltpu
from jax.sharding import PartitionSpec as P

HEAD_DIM = 64
PATCHES = 197
TEXT_MAX = 40
STEP = 7

norm_epsilon = 1e-06
masked_score = -1000000000.0
first_decay = 0.9
second_decay = 0.98
adam_epsilon = 1e-06
matrix_rate = 0.04
vector_rate = 0.5
weight_decay = 0.01

PATCH_STRIDE = 208
TEXT_STRIDE = 48
ITEM_ROWS = PATCH_STRIDE + TEXT_STRIDE

bf16 = jnp.bfloat16
f32 = jnp.float32
VMEM_LIMIT = 58 * 1024 * 1024
ATTENTION_US = 18
LIFT_US = 16
DROP_WEIGHT_US = 7
EXPERT_BACK_US = 17
ATTENTION_BACK_US = 19
DROP_US = 17


def adamw(weight, first_state, second_state, gradient, step_rate, decay_rate):
    first_new = first_decay * first_state + (1.0 - first_decay) * gradient
    second_new = second_decay * second_state + (1.0 - second_decay) * gradient * gradient
    first_hat = first_new / (1.0 - first_decay**STEP)
    second_hat = second_new / (1.0 - second_decay**STEP)
    weight_new = weight - step_rate * (
        first_hat / (jnp.sqrt(second_hat) + adam_epsilon) + decay_rate * weight
    )
    return (weight_new, first_new, second_new, weight_new.astype(bf16))


def dot(left, right, left_dim, right_dim):
    return lax.dot_general(
        left,
        right,
        (((left_dim,), (right_dim,)), ((), ())),
        preferred_element_type=f32,
    )


def loop(count, body):
    lax.fori_loop(0, count, lambda i, c: (body(i), c)[1], 0)


def rows_at(index, size):
    return pl.ds(pl.multiple_of(index * size, 16), size)


def norm_forward(values, gain, shift):
    centred = values - jnp.mean(values, axis=-1, keepdims=True)
    spread = jnp.mean(centred * centred, axis=-1, keepdims=True)
    return centred * lax.rsqrt(spread + norm_epsilon) * gain + shift


def norm_backward(values, gain, grad):
    centred = values - jnp.mean(values, axis=-1, keepdims=True)
    spread = jnp.mean(centred * centred, axis=-1, keepdims=True)
    scale = lax.rsqrt(spread + norm_epsilon)
    hat = centred * scale
    grad_hat = grad * gain
    grad_values = scale * (
        grad_hat
        - jnp.mean(grad_hat, axis=-1, keepdims=True)
        - hat * jnp.mean(grad_hat * hat, axis=-1, keepdims=True)
    )
    grad_gain = jnp.sum(grad * hat, axis=0, keepdims=True)
    grad_shift = jnp.sum(grad, axis=0, keepdims=True)
    return grad_values, grad_gain, grad_shift


def one_hot(row_place, first_row, count):
    place = lax.broadcasted_iota(jnp.int32, (count, row_place.shape[1]), 0) + first_row
    return (place == row_place).astype(bf16)


def relative_block(mine, block):
    other = jnp.bitwise_xor(mine, block)
    return jnp.bitwise_and(other, 1) * 4 + jnp.right_shift(other, 1)


def piece_copies(pieces, mine, place_of, sems):
    even, *odd = pieces
    blocks = [(even, i, 2 * i) for i in range(4)]
    z = 0
    for ref in odd:
        for i in range(ref.shape[0]):
            blocks.append((ref, i, 2 * z + 1))
            z += 1
    size = even.shape[2]
    copies = []
    for index, (ref, i, block) in enumerate(blocks):
        first = jnp.bitwise_xor(mine, block) * size
        rows = pl.ds(pl.multiple_of(first, 16), size)
        copies.append(pltpu.make_async_copy(ref.at[i], place_of(rows), sems.at[index]))
    return copies


def step_parts(pieces):
    parts = []
    for step in range(2 * len(pieces) // 5):
        even, odd, high, front, back = pieces[len(pieces) - 5 - 5 * (step // 2) :][:5]
        parts.append((high, front, back) if step % 2 else (even, odd))
    return parts


def step_copies(parts, mine, weight_ref, sems):
    by_step = []
    for step, pieces in enumerate(parts):
        place_of = lambda rows, step=step: weight_ref.at[:, step, rows, :]
        by_step.append(piece_copies(pieces, mine, place_of, sems.at[step]))
    return by_step


def start_all(by_step):
    for copies in by_step:
        for copy in copies:
            copy.start()


def out_copy(weight_ref, out_ref, out_sems, step, places):
    return pltpu.make_async_copy(
        weight_ref.at[:, step], out_ref.at[:, places[step]], out_sems.at[step]
    )


def wait_step(by_step, weight_ref, out_ref, out_sems, places):
    for step, copies in enumerate(by_step):

        @pl.when(pl.program_id(0) == step)
        def _():
            for copy in copies:
                copy.wait()
            out_copy(weight_ref, out_ref, out_sems, step, places).start()


def wait_out(weight_ref, out_ref, out_sems, places):
    for step in range(weight_ref.shape[1]):
        out_copy(weight_ref, out_ref, out_sems, step, places).wait()


def store_grad(grad_ref, mine, index, first, rows, value):
    value = value.astype(bf16)
    size = grad_ref.shape[-2]
    for part in range(rows // size):
        place = relative_block(mine, first // size + part)
        grad_ref[0, place, index] = value[part * size : (part + 1) * size]


def attend(queries, keys, values, allowed):
    scores = [dot(key, query, 1, 1) for query, key in zip(queries, keys)]
    scores = [jnp.where(mask, score, masked_score) for mask, score in zip(allowed, scores)]
    tops = [jnp.max(score, axis=0, keepdims=True) for score in scores]
    weights = [jnp.exp(score - top) for score, top in zip(scores, tops)]
    totals = [jnp.sum(weight, axis=0, keepdims=True) for weight in weights]
    weights = [(weight * (1.0 / total)).astype(bf16) for weight, total in zip(weights, totals)]
    return weights, [dot(value, weight, 0, 0) for value, weight in zip(values, weights)]


def item_slices(items, i):
    first = items * PATCH_STRIDE + i * TEXT_STRIDE
    return slice(i * PATCH_STRIDE, (i + 1) * PATCH_STRIDE), slice(first, first + TEXT_STRIDE)


def item_rows(ref, index, items, i):
    patch_rows, text_rows = item_slices(items, i)
    return jnp.concatenate([ref[index + (patch_rows,)], ref[index + (text_rows,)]], axis=0)


def head_columns(rows, kind, heads, h):
    first = (kind * heads + h) * HEAD_DIM
    return rows[:, first : first + HEAD_DIM]


def attention_kernel(meta_ref, raw_ref, place_ref, hidden_ref, norm_ref, extra_ref, *refs, **sizes):
    parts, outs = (refs[:2], refs[2:4]), refs[4:]
    block_ref, normed_ref, residual_ref, out_ref, joint_ref, mixed_ref, probs_ref = outs[:7]
    weight_ref, sems, out_sems = outs[7:]
    items, main_rows, all_rows = sizes["items"], sizes["main_rows"], sizes["all_rows"]
    step = pl.program_id(0)
    by_step = step_copies(parts, meta_ref[items + 1], weight_ref, sems)

    @pl.when(step == 0)
    def _():
        start_all(by_step)

        def chunk(first, size):
            rows = pl.ds(first, size)
            picked = dot(one_hot(place_ref[...], first, size), raw_ref[...], 1, 0)
            picked = jnp.where(hidden_ref[rows, :] > 0, extra_ref[2:3, :], picked)
            block_ref[rows, :] = picked
            residual_ref[rows, :] = picked
            normed_ref[rows, :] = norm_forward(picked, norm_ref[0:1, :], norm_ref[1:2, :]).astype(bf16)

        loop(items, lambda i: chunk(pl.multiple_of(i * ITEM_ROWS, 16), ITEM_ROWS))
        chunk(main_rows, all_rows - main_rows)

    wait_step(by_step, weight_ref, out_ref, out_sems, (0, 2))
    attend_heads(
        meta_ref, weight_ref.at[0, step], normed_ref, residual_ref, joint_ref, mixed_ref, probs_ref, **sizes
    )

    @pl.when(step == pl.num_programs(0) - 1)
    def _():
        wait_out(weight_ref, out_ref, out_sems, (0, 2))


def attention_end_kernel(meta_ref, normed_ref, block_ref, before_ref, valid_ref, norm_ref, *refs, **sizes):
    parts, outs = (refs[:3], refs[3:6]), refs[10:]
    residual_ref, feed_ref, square_ref, out_ref, joint_ref, mixed_ref, probs_ref = outs[:7]
    weight_ref, sems, out_sems = outs[7:]
    items, main_rows, all_rows = sizes["items"], sizes["main_rows"], sizes["all_rows"]
    step = pl.program_id(0)
    by_step = step_copies(parts, meta_ref[items + 1], weight_ref, sems)

    @pl.when(step == 0)
    def _():
        start_all(by_step)
        residual_ref[...] = before_ref[...]

    wait_step(by_step, weight_ref, out_ref, out_sems, (1, 3))
    attend_heads(
        meta_ref, weight_ref.at[0, step], normed_ref, residual_ref, joint_ref, mixed_ref, probs_ref, **sizes
    )

    @pl.when(step == pl.num_programs(0) - 1)
    def _():
        square_ref[...] = jnp.zeros_like(square_ref)

        def chunk(rows):
            residual = residual_ref[rows, :]
            feed_ref[rows, :] = norm_forward(residual, norm_ref[2:3, :], norm_ref[3:4, :]).astype(bf16)
            attended = (residual - block_ref[rows, :]) * valid_ref[rows, :]
            square_ref[...] += jnp.sum(attended * attended, axis=0, keepdims=True)

        loop(items, lambda i: chunk(rows_at(i, ITEM_ROWS)))
        chunk(pl.ds(main_rows, all_rows - main_rows))
        wait_out(weight_ref, out_ref, out_sems, (1, 3))


def attend_heads(
    meta_ref,
    weight_ref,
    normed_ref,
    residual_ref,
    joint_ref,
    mixed_ref,
    probs_ref,
    *,
    items,
    heads,
    main_rows,
    all_rows,
):
    width = heads * HEAD_DIM
    tail_rows = all_rows - main_rows

    def project(rows):
        joint = dot(normed_ref[rows, :], weight_ref[:, : 3 * width], 1, 0)
        joint_ref[0, rows, :width] = (joint[:, :width].astype(bf16).astype(f32) * HEAD_DIM**-0.5).astype(bf16)
        joint_ref[0, rows, width:] = joint[:, width:].astype(bf16)

    project(pl.ds(0, all_rows))

    key_row = lax.broadcasted_iota(jnp.int32, (ITEM_ROWS, 1), 0)
    blocks = [item_rows(joint_ref, (0,), items, i) for i in range(items)]
    masks = [
        (key_row < PATCHES)
        | ((key_row >= PATCH_STRIDE) & (key_row < PATCH_STRIDE + meta_ref[i]))
        for i in range(items)
    ]
    blocks.append(joint_ref[0, main_rows:, :])
    masks.append(lax.broadcasted_iota(jnp.int32, (tail_rows, 1), 0) < meta_ref[items])
    pairs = [(i, h) for i in range(items + 1) for h in range(heads)]
    weights, outs = attend(
        *[[head_columns(blocks[i], kind, heads, h) for i, h in pairs] for kind in range(3)],
        [masks[i] for i, _ in pairs],
    )
    for (i, h), weight in zip(pairs, weights):
        if i < items:
            probs_ref[0, i, h] = weight
    for i in range(items + 1):
        mixed = jnp.concatenate(outs[i * heads : (i + 1) * heads], axis=0).T.astype(bf16)
        if i == items:
            mixed_ref[0, main_rows:, :] = mixed
        else:
            patch_rows, text_rows = item_slices(items, i)
            mixed_ref[0, patch_rows, :] = mixed[:PATCH_STRIDE]
            mixed_ref[0, text_rows, :] = mixed[PATCH_STRIDE:]

    def add_output(rows):
        residual_ref[rows, :] += dot(mixed_ref[0, rows, :], weight_ref[:, 3 * width :], 1, 1)

    add_output(pl.ds(0, all_rows))


def attention_back_kernel(
    mine_ref,
    grad_attended_ref,
    joint_ref,
    mixed_ref,
    probs_ref,
    normed_ref,
    weight_ref,
    grad_weight_ref,
    grad_normed_ref,
    grad_mixed_ref,
    grad_joint_ref,
    **sizes,
):
    @pl.when(pl.program_id(0) == 0)
    def _():
        grad_normed_ref[...] = jnp.zeros_like(grad_normed_ref)

    heads_back(
        mine_ref,
        grad_attended_ref,
        joint_ref,
        mixed_ref,
        probs_ref,
        normed_ref,
        weight_ref,
        grad_weight_ref,
        grad_normed_ref,
        grad_mixed_ref,
        grad_joint_ref,
        **sizes,
    )


def attention_back_end_kernel(
    mine_ref,
    grad_attended_ref,
    joint_ref,
    mixed_ref,
    probs_ref,
    normed_ref,
    weight_ref,
    before_ref,
    grad_weight_ref,
    grad_normed_ref,
    grad_mixed_ref,
    grad_joint_ref,
    **sizes,
):
    @pl.when(pl.program_id(0) == 0)
    def _():
        grad_normed_ref[...] = before_ref[...]

    heads_back(
        mine_ref,
        grad_attended_ref,
        joint_ref,
        mixed_ref,
        probs_ref,
        normed_ref,
        weight_ref,
        grad_weight_ref,
        grad_normed_ref,
        grad_mixed_ref,
        grad_joint_ref,
        **sizes,
    )


def input_grad_kernel(
    grad_normed_ref,
    grad_residual_ref,
    block_ref,
    hidden_ref,
    place_ref,
    norm_ref,
    grad_raw_ref,
    grad_norm_ref,
    grad_mask_ref,
    grad_block_ref,
):
    grad_norm_ref[...] = jnp.zeros_like(grad_norm_ref)
    grad_mask_ref[...] = jnp.zeros_like(grad_mask_ref)

    def chunk(i):
        rows = rows_at(i, ITEM_ROWS)
        grad, gain, shift = norm_backward(block_ref[rows, :], norm_ref[0:1, :], grad_normed_ref[rows, :])
        grad_norm_ref[0:1, :] += gain
        grad_norm_ref[1:2, :] += shift
        grad = grad + grad_residual_ref[rows, :]
        hidden = hidden_ref[rows, :] > 0
        grad_mask_ref[...] += jnp.sum(jnp.where(hidden, grad, 0.0), axis=0, keepdims=True)
        grad_block_ref[rows, :] = jnp.where(hidden, 0.0, grad).astype(bf16)

    loop(grad_normed_ref.shape[0] // ITEM_ROWS, chunk)
    unplace(place_ref, grad_block_ref, grad_raw_ref, grad_block_ref.shape[0])


def heads_back(
    mine_ref,
    grad_attended_ref,
    joint_ref,
    mixed_ref,
    probs_ref,
    normed_ref,
    weight_ref,
    grad_weight_ref,
    grad_normed_ref,
    grad_mixed_ref,
    grad_joint_ref,
    *,
    items,
    heads,
):
    width = heads * HEAD_DIM
    half = HEAD_DIM**-0.5

    grad_mixed_ref[...] = dot(grad_attended_ref[...], weight_ref[0, :, 3 * width :], 1, 0).astype(bf16)

    blocks = [item_rows(joint_ref, (0,), items, i) for i in range(items)]
    outs = [item_rows(grad_mixed_ref, (), items, i) for i in range(items)]
    products = [
        (outs[i].astype(f32) * item_rows(mixed_ref, (0,), items, i).astype(f32)).T for i in range(items)
    ]
    pairs = [(i, h) for i in range(items) for h in range(heads)]
    queries, keys, values = [
        [head_columns(blocks[i], kind, heads, h) for i, h in pairs] for kind in range(3)
    ]
    grad_outs = [head_columns(outs[i], 0, heads, h) for i, h in pairs]
    weights = [probs_ref[0, i, h] for i, h in pairs]
    grad_probs = [dot(value, grad_out, 1, 1) for value, grad_out in zip(values, grad_outs)]
    means = [
        jnp.sum(products[i][h * HEAD_DIM : (h + 1) * HEAD_DIM], axis=0, keepdims=True) for i, h in pairs
    ]
    grad_scores = [
        (weight.astype(f32) * (grad - mean)).astype(bf16)
        for weight, grad, mean in zip(weights, grad_probs, means)
    ]
    grad_values = [dot(weight, grad_out, 1, 0).astype(bf16) for weight, grad_out in zip(weights, grad_outs)]
    grad_keys = [dot(score, query, 1, 0).astype(bf16) for score, query in zip(grad_scores, queries)]
    grad_queries = [dot(key, score, 0, 0) * half for key, score in zip(keys, grad_scores)]
    for i in range(items):
        own = slice(i * heads, (i + 1) * heads)
        grad_query = jnp.concatenate(grad_queries[own], axis=0).T.astype(bf16)
        grad_joint = jnp.concatenate([grad_query] + grad_keys[own] + grad_values[own], axis=1)
        patch_rows, text_rows = item_slices(items, i)
        grad_joint_ref[patch_rows, :] = grad_joint[:PATCH_STRIDE]
        grad_joint_ref[text_rows, :] = grad_joint[PATCH_STRIDE:]

    model_width = weight_ref.shape[1]
    for first in range(0, model_width, 384):
        cols = slice(first, first + 384)
        grad_weight = jnp.concatenate(
            [
                dot(normed_ref[:, cols], grad_joint_ref[...], 0, 0),
                dot(grad_attended_ref[:, cols], mixed_ref[0], 0, 0),
            ],
            axis=1,
        )
        store_grad(grad_weight_ref, mine_ref[0], 0, first, 384, grad_weight)

    grad_normed_ref[...] += dot(grad_joint_ref[...], weight_ref[0, :, : 3 * width], 1, 1)


def unplace(place_ref, source_ref, raw_ref, source_rows):
    source = source_ref[...].astype(bf16)
    raw_rows = raw_ref.shape[0]
    size = 240 if raw_rows % 240 == 0 else raw_rows

    def chunk(i):
        rows = rows_at(i, size)
        place = lax.broadcasted_iota(jnp.int32, (size, source_rows), 1)
        pick = (place == place_ref[rows, :]).astype(bf16)
        raw_ref[rows, :] = dot(pick, source, 1, 0).astype(bf16)

    loop(raw_rows // size, chunk)


def lift_kernel(mine_ref, feed_ref, *refs, vision_rows, all_rows):
    pieces, (acted_ref, slope_ref, out_ref, weight_ref, sems, out_sems) = refs[:10], refs[10:]
    by_step = step_copies(step_parts(pieces), mine_ref[0], weight_ref, sems)

    @pl.when(pl.program_id(0) == 0)
    def _():
        start_all(by_step)

    wait_step(by_step, weight_ref, out_ref, out_sems, (0, 1, 2, 3))

    def piece(rows, expert):
        lifted = dot(feed_ref[rows, :], weight_ref[expert, pl.program_id(0)], 1, 0)
        cumulative = 0.5 * (1.0 + lax.erf(lifted * (0.5**0.5)))
        density = jnp.exp(-0.5 * lifted * lifted) * ((2.0 * jnp.pi) ** -0.5)
        acted_ref[0, rows, :] = (lifted * cumulative).astype(bf16)
        slope_ref[0, rows, :] = (cumulative + lifted * density).astype(bf16)

    loop(2, lambda i: piece(rows_at(i, vision_rows // 2), 0))
    piece(pl.ds(vision_rows, all_rows - vision_rows), 1)

    @pl.when(pl.program_id(0) == pl.num_programs(0) - 1)
    def _():
        wait_out(weight_ref, out_ref, out_sems, (0, 1, 2, 3))


def place_grad_kernel(raw_ref, place_ref, grad_ref, grad_bias_ref, *, vision_rows):
    def chunk(i):
        rows = rows_at(i, ITEM_ROWS)
        pick = one_hot(place_ref[...], i * ITEM_ROWS, ITEM_ROWS)
        grad_ref[rows, :] = dot(pick, raw_ref[...], 1, 0).astype(bf16)

    loop(grad_ref.shape[0] // ITEM_ROWS, chunk)
    grad_bias_ref[0:1, :] = jnp.sum(grad_ref[:vision_rows, :].astype(f32), axis=0, keepdims=True)
    grad_bias_ref[1:2, :] = jnp.sum(grad_ref[vision_rows:, :].astype(f32), axis=0, keepdims=True)


def expert_weight_grad(grad_weight_ref, mine, left_ref, right, vision_rows):
    rows_total, width = left_ref.shape
    for expert, rows in ((0, slice(0, vision_rows)), (1, slice(vision_rows, rows_total))):
        for first in range(0, width, 384):
            grad_weight = dot(left_ref[rows, first : first + 384], right(rows), 0, 0)
            store_grad(grad_weight_ref, mine, expert, first, 384, grad_weight)


def drop_weight_kernel(mine_ref, grad_ref, acted_ref, grad_weight_ref, *, vision_rows):
    expert_weight_grad(
        grad_weight_ref, mine_ref[0], grad_ref, lambda rows: acted_ref[0, rows, :], vision_rows
    )


def drop_kernel(
    acted_ref,
    residual_ref,
    valid_ref,
    place_ref,
    extra_ref,
    weight_ref,
    raw_ref,
    square_ref,
    total_ref,
    *,
    vision_rows,
    all_rows,
):
    step = pl.program_id(0)
    text = all_rows - vision_rows

    @pl.when(step == 0)
    def _():
        total_ref[:vision_rows, :] = jnp.broadcast_to(extra_ref[0:1, :], (vision_rows, total_ref.shape[1]))
        total_ref[vision_rows:, :] = jnp.broadcast_to(extra_ref[1:2, :], (text, total_ref.shape[1]))

    def piece(rows, expert):
        total_ref[rows, :] += dot(acted_ref[0, rows, :], weight_ref[expert, 0], 1, 1)

    piece(pl.ds(0, vision_rows), 0)
    piece(pl.ds(vision_rows, text), 1)

    @pl.when(step == pl.num_programs(0) - 1)
    def _():
        square_ref[...] = jnp.zeros_like(square_ref)

        def finish(rows, expert):
            fed = total_ref[rows, :]
            out = residual_ref[rows, :] + fed
            valid = valid_ref[rows, :]
            square_ref[0:1, :] += jnp.sum(valid * out * out, axis=0, keepdims=True)
            square_ref[1:2, :] += jnp.sum(valid * fed * fed, axis=0, keepdims=True)
            total_ref[rows, :] = out

        loop(vision_rows // PATCH_STRIDE, lambda i: finish(rows_at(i, PATCH_STRIDE), 0))
        loop(3, lambda i: finish(pl.ds(pl.multiple_of(vision_rows + i * (text // 3), 16), text // 3), 1))
        unplace(place_ref, total_ref, raw_ref, all_rows)


def expert_back_step(
    mine_ref, grad_ref, slope_ref, feed_ref, lift_ref, drop_ref, grad_weight_ref, total_ref, lifted_ref, vision_rows
):
    step = pl.program_id(0)

    def piece(rows, expert):
        grad_acted = dot(grad_ref[rows, :], drop_ref[expert, step], 1, 0)
        grad_lifted = (grad_acted * slope_ref[0, rows, :].astype(f32)).astype(bf16)
        lifted_ref[rows, :] = grad_lifted
        total_ref[rows, :] += dot(grad_lifted, lift_ref[expert, 0], 1, 1)

    piece(pl.ds(0, vision_rows), 0)
    piece(pl.ds(vision_rows, grad_ref.shape[0] - vision_rows), 1)
    expert_weight_grad(
        grad_weight_ref, mine_ref[0], feed_ref, lambda rows: lifted_ref[rows, :], vision_rows
    )


def expert_back_kernel(mine_ref, grad_ref, slope_ref, feed_ref, lift_ref, *refs, vision_rows):
    pieces, (grad_weight_ref, out_ref, total_ref) = refs[:5], refs[5:8]
    lifted_ref, drop_ref, sems, out_sems = refs[8:]
    by_step = step_copies(step_parts(pieces), mine_ref[0], drop_ref, sems)

    @pl.when(pl.program_id(0) == 0)
    def _():
        start_all(by_step)
        total_ref[...] = jnp.zeros_like(total_ref)

    wait_step(by_step, drop_ref, out_ref, out_sems, (0, 1))
    expert_back_step(
        mine_ref, grad_ref, slope_ref, feed_ref, lift_ref, drop_ref, grad_weight_ref, total_ref, lifted_ref, vision_rows
    )

    @pl.when(pl.program_id(0) == pl.num_programs(0) - 1)
    def _():
        wait_out(drop_ref, out_ref, out_sems, (0, 1))


def expert_back_end_kernel(mine_ref, grad_ref, slope_ref, feed_ref, lift_ref, *refs, vision_rows):
    pieces, (_, before_ref, residual_ref, norm_ref) = refs[:5], refs[5:9]
    grad_weight_ref, out_ref, grad_residual_ref, grad_attended_ref, grad_norm_ref = refs[9:14]
    lifted_ref, drop_ref, sems, out_sems = refs[14:]
    by_step = step_copies(step_parts(pieces), mine_ref[0], drop_ref, sems)

    @pl.when(pl.program_id(0) == 0)
    def _():
        start_all(by_step)
        grad_residual_ref[...] = before_ref[...]

    wait_step(by_step, drop_ref, out_ref, out_sems, (2, 3))
    expert_back_step(
        mine_ref,
        grad_ref,
        slope_ref,
        feed_ref,
        lift_ref,
        drop_ref,
        grad_weight_ref,
        grad_residual_ref,
        lifted_ref,
        vision_rows,
    )

    @pl.when(pl.program_id(0) == pl.num_programs(0) - 1)
    def _():
        grad_norm_ref[...] = jnp.zeros_like(grad_norm_ref)

        def chunk(i):
            rows = rows_at(i, ITEM_ROWS)
            grad, gain, shift = norm_backward(
                residual_ref[rows, :], norm_ref[2:3, :], grad_residual_ref[rows, :]
            )
            grad_norm_ref[0:1, :] += gain
            grad_norm_ref[1:2, :] += shift
            grad = grad + grad_ref[rows, :].astype(f32)
            grad_residual_ref[rows, :] = grad
            grad_attended_ref[rows, :] = grad.astype(bf16)

        loop(grad_ref.shape[0] // ITEM_ROWS, chunk)
        wait_out(drop_ref, out_ref, out_sems, (2, 3))


def whole(*shape):
    return pl.BlockSpec(shape, lambda *_: (0,) * len(shape))


def stepped(*shape, first=0):
    return pl.BlockSpec(shape, lambda i, *_: (i + first,) + (0,) * (len(shape) - 1))


def stepped_pair(*shape, first=0):
    return pl.BlockSpec(shape, lambda i, *_: (0, i + first) + (0,) * (len(shape) - 2))


def every_other(*shape, first=0):
    return pl.BlockSpec(shape, lambda i, *_: (2 * i + first,) + (0,) * (len(shape) - 1))


def anywhere(values):
    return (values, pl.BlockSpec(memory_space=pl.ANY))


def call(kernel, name, steps, ins, outs, scratch, microseconds, scalars=(), aliases=None):
    return pl.pallas_call(
        kernel,
        name=name,
        grid_spec=pltpu.PrefetchScalarGridSpec(
            num_scalar_prefetch=len(scalars),
            grid=(steps,),
            in_specs=[block for _, block in ins],
            out_specs=[block for _, _, block in outs],
            scratch_shapes=scratch,
        ),
        out_shape=[jax.ShapeDtypeStruct(shape, kind) for shape, kind, _ in outs],
        input_output_aliases=aliases or {},
        compiler_params=pltpu.CompilerParams(
            dimension_semantics=("arbitrary",), vmem_limit_bytes=VMEM_LIMIT
        ),
        cost_estimate=pl.CostEstimate(
            flops=int(microseconds * 1e9), bytes_accessed=int(microseconds * 1e6), transcendentals=0
        ),
    )(*scalars, *[array for array, _ in ins])


def body(
    tokens,
    cotangent,
    text_lengths,
    modality,
    masked_positions,
    joint_weight,
    joint_first,
    joint_second,
    output_weight,
    output_first,
    output_second,
    lift_weight,
    lift_first,
    lift_second,
    drop_weight,
    drop_first,
    drop_second,
    norm_params,
    norm_first,
    norm_second,
    extra_params,
    extra_first,
    extra_second,
):
    micro_count, shard_rows, model_width = tokens.shape
    block_rows = modality.shape[1]
    parts = block_rows // shard_rows
    assert micro_count == parts
    items = text_lengths.shape[1]
    width = joint_weight.shape[2]
    heads = width // HEAD_DIM
    hidden_width = lift_weight.shape[2]
    shard = joint_weight.shape[1]
    vision_rows = items * PATCH_STRIDE
    main_rows = items * ITEM_ROWS
    tail = block_rows - items * PATCHES - TEXT_MAX - (items - 1)
    tail = (tail + 47) // 48 * 48
    all_rows = main_rows + tail
    assert 4 * width == model_width and hidden_width == model_width

    shard_attend = jnp.concatenate(
        [joint_weight[0], joint_weight[1], joint_weight[2], output_weight.T], axis=1
    ).astype(bf16)[None]
    shard_lift = lift_weight.astype(bf16)
    shard_drop = jnp.swapaxes(drop_weight, 1, 2).astype(bf16)

    groups = lax.axis_size("dp")
    cube = groups == 8
    piece = model_width // 8
    if cube:
        mine = jnp.stack([lax.axis_index("dp"), lax.axis_index("mp")]).astype(jnp.int32)
    else:
        mine = jnp.zeros((2,), jnp.int32)

    def together(*values):
        return lax.optimization_barrier(values)

    def swap(values, axis, bit):
        size = lax.axis_size(axis)
        return lax.ppermute(values, axis, [(i, i ^ bit) for i in range(size)])

    def exchange(values):
        return lax.all_to_all(values, "mp", split_axis=0, concat_axis=1, tiled=True)[0]

    def give_back(values):
        return lax.all_to_all(
            values.reshape(parts, shard_rows, model_width), "mp", split_axis=0, concat_axis=0, tiled=True
        )

    def gather(values):
        whole_values = lax.all_gather(values, ("mp", "dp"), axis=1, tiled=True)
        return whole_values.reshape(-1, parts, model_width, values.shape[2])

    def gather_pieces(values):
        whole_values = jnp.swapaxes(gather(values).reshape(-1, parts, 4, 2, piece, model_width), 0, 3)
        pieces = []
        for core in range(2):
            low, high = whole_values[:, core], whole_values[:, 2 + core]
            pieces += [low[0], low[1], high[0], high[1, :2], high[1, 2:]]
        return pieces

    def line_parts(values):
        return (values,) + tuple(swap(values, "dp", bit) for bit in (2, 4, 6))

    def gather_line(values):
        return jnp.stack(line_parts(values))

    def gather_plane(line):
        return swap(line, "dp", 1), swap(line, "mp", 2)

    def gather_corner(along_x, along_y):
        return swap(along_x[:2], "mp", 2), swap(along_y[2:], "dp", 1)

    def over_cores(*pieces):
        return tuple(swap(part, "mp", 1) for part in pieces)

    def add(*terms):
        total = terms[0].astype(f32)
        for term in terms[1:]:
            total = total + term.astype(f32)
        return total

    def scatter(keep, send):
        shape = (2, 2, 4) + keep.shape[2:]
        both = jnp.stack([keep.reshape(shape), send.reshape(shape)], axis=1)
        both = jnp.transpose(both, (4, 0, 1, 3, 2, 5, 6))
        return reduce(both.reshape(both.shape[0], parts * model_width, shape[-1]))

    def reduce(values):
        values = lax.psum_scatter(values, ("mp", "dp"), scatter_dimension=1, tiled=True)
        return values.astype(f32)

    def quarters(keep, received, *others):
        keep, received, others = together(keep, received, others)
        shape = (2, 2, 4) + keep.shape[2:]
        keep, received = keep.reshape(shape), received.reshape(shape)
        return (lambda y, x: add(keep[y, x], received[y, x])), others

    def scatter_corner(keep, received):
        quarter, _ = quarters(keep, received)
        return quarter(1, 1).astype(bf16)

    def scatter_plane(keep, received, from_x, from_y):
        quarter, (from_x, from_y) = quarters(keep, received, from_x, from_y)
        part_x, part_y = quarter(0, 1), quarter(1, 0)
        part_x = jnp.concatenate([part_x[:2], add(part_x[2:], from_y)]).astype(bf16)
        part_y = jnp.concatenate([add(part_y[:2], from_x), part_y[2:]]).astype(bf16)
        return part_x, part_y

    def scatter_line(keep, received, from_x, from_y):
        quarter, (from_x, from_y) = quarters(keep, received, from_x, from_y)
        return add(quarter(0, 0), from_x, from_y).astype(bf16)

    def send_corner(corner):
        return swap(corner[:2], "dp", 1), swap(corner[2:], "mp", 2)

    def send_plane(part_x, part_y):
        return swap(part_x, "dp", 1), swap(part_y, "mp", 2)

    def send_line(line):
        return tuple(swap(line[i], "dp", 2 * i) for i in (1, 2, 3))

    micro = lax.axis_index("mp")
    lengths = lax.dynamic_index_in_dim(text_lengths, micro, 0, keepdims=False)
    masked = lax.dynamic_index_in_dim(masked_positions, micro, 0, keepdims=False)
    item_ids = jnp.arange(items, dtype=jnp.int32)
    sizes = PATCHES + lengths
    ends = jnp.sum(jnp.where(item_ids[:, None] <= item_ids[None, :], sizes[:, None], 0), axis=0)
    used = jnp.sum(sizes)

    def place_of(row):
        segment = jnp.sum((row[..., None] >= ends).astype(jnp.int32), axis=-1)
        start = jnp.sum(jnp.where(row[..., None] >= ends, sizes, 0), axis=-1)
        inside = row - start
        return jnp.where(
            segment == items,
            main_rows + inside,
            jnp.where(
                inside < PATCHES,
                PATCH_STRIDE * segment + inside,
                vision_rows + TEXT_STRIDE * segment + inside - PATCHES,
            ),
        )

    place_row = place_of(jnp.arange(block_rows, dtype=jnp.int32))[None, :]
    place_column = place_of(jnp.arange(block_rows, dtype=jnp.int32))[:, None]
    targets = (vision_rows + TEXT_STRIDE * item_ids[:, None] + masked).reshape(-1)
    spots = jnp.arange(all_rows, dtype=jnp.int32)
    hidden = jnp.any(spots[:, None] == targets[None, :], axis=1).astype(jnp.int32)[:, None]
    text_spot = spots - vision_rows
    text_item = text_spot // TEXT_STRIDE
    text_end = jnp.sum(jnp.where(text_item[:, None] == item_ids, lengths, 0), axis=1)
    valid = jnp.where(
        text_spot < 0, spots % PATCH_STRIDE < PATCHES, text_spot - text_item * TEXT_STRIDE < text_end
    )
    valid = valid.astype(f32)[:, None]
    meta = jnp.concatenate([lengths, (block_rows - used)[None], mine[:1]])

    def rows_of(count, kind):
        return ((count, model_width), kind, whole(count, model_width))

    def plain(values):
        return (values, whole(*values.shape))

    def heads_out(first):
        shapes = [
            (parts, all_rows, 3 * width),
            (parts, all_rows, width),
            (parts, items, heads, ITEM_ROWS, ITEM_ROWS),
        ]
        return [(shape, bf16, every_other(1, *shape[1:], first=first)) for shape in shapes]

    def whole_weight(count):
        return ((count, parts, model_width, model_width), bf16, pl.BlockSpec(memory_space=pl.ANY))

    def weight_scratch(count, steps):
        return [
            pltpu.VMEM((count, steps, model_width, model_width), bf16),
            pltpu.SemaphoreType.DMA((steps, 8)),
            pltpu.SemaphoreType.DMA((steps,)),
        ]

    def part_weight(values, first, count=2):
        return (values, stepped_pair(count, 1, *values.shape[2:], first=first))

    def grad_out(count):
        shape = (2, 8, count, piece, model_width)
        return (shape, bf16, stepped(1, *shape[1:]))

    head_sizes = dict(items=items, heads=heads)
    row_sizes = dict(main_rows=main_rows, all_rows=all_rows)

    def attention(raw, pieces):
        return call(
            functools.partial(attention_kernel, **head_sizes, **row_sizes),
            "attention",
            2,
            [plain(raw), plain(place_row), plain(hidden), plain(norm_params), plain(extra_params)]
            + [anywhere(values) for values in pieces],
            [rows_of(all_rows, f32), rows_of(all_rows, bf16), rows_of(all_rows, f32), whole_weight(1)]
            + heads_out(0),
            weight_scratch(1, 2),
            ATTENTION_US,
            (meta,),
        )

    def attention_end(normed, block_input, residual, pieces, made):
        return call(
            functools.partial(attention_end_kernel, **head_sizes, **row_sizes),
            "attention_end",
            2,
            [plain(normed), plain(block_input), plain(residual), plain(valid), plain(norm_params)]
            + [anywhere(values) for values in pieces]
            + [anywhere(values) for values in made],
            [rows_of(all_rows, f32), rows_of(all_rows, bf16), rows_of(1, f32), whole_weight(1)]
            + heads_out(1),
            weight_scratch(1, 2),
            ATTENTION_US,
            (meta,),
            {12 + i: 3 + i for i in range(4)},
        )

    def lift(feed_input, pieces):
        shape = (parts, all_rows, hidden_width)
        return call(
            functools.partial(lift_kernel, vision_rows=vision_rows, all_rows=all_rows),
            "lift",
            parts,
            [plain(feed_input)] + [anywhere(values) for values in pieces],
            [(shape, bf16, stepped(1, *shape[1:]))] * 2 + [whole_weight(2)],
            weight_scratch(2, parts),
            LIFT_US,
            (mine,),
        )

    def place_grad(raw):
        return call(
            functools.partial(place_grad_kernel, vision_rows=vision_rows),
            "place_grad",
            1,
            [plain(raw), plain(place_row)],
            [rows_of(main_rows, bf16), rows_of(2, f32)],
            [],
            5,
        )

    def drop_weight_grad(grad_rows, acted, first):
        return call(
            functools.partial(drop_weight_kernel, vision_rows=vision_rows),
            "drop_weight_grad",
            2,
            [plain(grad_rows), (acted, stepped(1, main_rows, hidden_width, first=first))],
            [grad_out(2)],
            [],
            DROP_WEIGHT_US,
            (mine,),
        )[0]

    def expert_ins(grad_rows, slope, feed_input, lift_weights, pieces, first):
        return [
            plain(grad_rows),
            (slope, stepped(1, main_rows, hidden_width, first=first)),
            (feed_input, whole(main_rows, model_width)),
            part_weight(lift_weights, first),
        ] + [anywhere(values) for values in pieces]

    drop_out = whole_weight(2)
    expert_scratch = [pltpu.VMEM((main_rows, hidden_width), bf16)] + weight_scratch(2, 2)

    def expert_back(pieces, *args):
        return call(
            functools.partial(expert_back_kernel, vision_rows=vision_rows),
            "expert_back",
            2,
            expert_ins(*args, pieces[5:], 0),
            [grad_out(2), drop_out, rows_of(main_rows, f32)],
            expert_scratch,
            EXPERT_BACK_US,
            (mine,),
        )

    def expert_back_end(made, before, residual, pieces, *args):
        return call(
            functools.partial(expert_back_end_kernel, vision_rows=vision_rows),
            "expert_back_end",
            2,
            expert_ins(*args, pieces[:5], 2)
            + [anywhere(made), plain(before), (residual, whole(main_rows, model_width))]
            + [plain(norm_params)],
            [grad_out(2), drop_out, rows_of(main_rows, f32), rows_of(main_rows, bf16)]
            + [rows_of(2, f32)],
            expert_scratch,
            EXPERT_BACK_US,
            (mine,),
            {10: 1},
        )

    def heads_ins(grad_attended, normed, weights, joint_rows, mixed, probs, first):
        return [
            plain(grad_attended),
            (joint_rows, stepped(1, main_rows, 3 * width, first=first)),
            (mixed, stepped(1, main_rows, width, first=first)),
            (probs, stepped(1, *probs.shape[1:], first=first)),
            (normed, whole(main_rows, model_width)),
            (weights, stepped(1, model_width, model_width, first=first)),
        ]

    heads_scratch = [
        pltpu.VMEM((main_rows, width), bf16),
        pltpu.VMEM((main_rows, 3 * width), bf16),
    ]

    def attention_back(*args):
        return call(
            functools.partial(attention_back_kernel, **head_sizes),
            "attention_back",
            2,
            heads_ins(*args, 0),
            [grad_out(1), rows_of(main_rows, f32)],
            heads_scratch,
            ATTENTION_BACK_US,
            (mine,),
        )

    def attention_back_end(before, *args):
        return call(
            functools.partial(attention_back_end_kernel, **head_sizes),
            "attention_back_end",
            2,
            heads_ins(*args, 2) + [plain(before)],
            [grad_out(1), rows_of(main_rows, f32)],
            heads_scratch,
            ATTENTION_BACK_US,
            (mine,),
        )

    def finish_input_grad(grad_normed, grad_residual, block_input):
        return call(
            input_grad_kernel,
            "input_grad",
            1,
            [
                plain(grad_normed),
                plain(grad_residual),
                (block_input, whole(main_rows, model_width)),
                (hidden, whole(main_rows, 1)),
                plain(place_column),
                plain(norm_params),
            ],
            [rows_of(block_rows, bf16), rows_of(2, f32), rows_of(1, f32)],
            [pltpu.VMEM((main_rows, model_width), bf16)],
            9,
        )

    def drop(acted, residual, weights):
        return call(
            functools.partial(drop_kernel, vision_rows=vision_rows, all_rows=all_rows),
            "drop",
            parts,
            [(acted, stepped(1, all_rows, hidden_width)), plain(residual), plain(valid)]
            + [plain(place_column), plain(extra_params)]
            + [part_weight(weights, 0)],
            [rows_of(block_rows, bf16), rows_of(2, f32)],
            [pltpu.VMEM((all_rows, model_width), f32)],
            DROP_US,
        )

    tables = (place_row, place_column, hidden, valid, meta)
    raw_tokens = exchange(tokens)
    if cube:
        line, tables = together(gather_line(shard_attend), tables)
        place_row, place_column, hidden, valid, meta = tables
        even, high = gather_plane(line)
        even, high, raw_tokens, shard_lift, cotangent = together(
            even, high, raw_tokens, shard_lift, cotangent
        )
        corner = gather_corner(even, high)
        line_lift = line_parts(shard_lift)
        raw_grad = exchange(cotangent.astype(bf16))
        early = over_cores(line, even) + (line, even)
    else:
        pieces = gather_pieces(shard_attend)
        early = [pieces[i] for i in (5, 6, 0, 1)]
        late = [pieces[i] for i in (7, 8, 9, 2, 3, 4)]
        raw_grad = exchange(cotangent.astype(bf16))

    block_input, normed, residual, *made = attention(raw_tokens, early)
    if cube:
        corner, line_lift, raw_grad, residual = together(corner, line_lift, raw_grad, residual)
        late = (high,) + corner
        late = over_cores(*late) + late
        line_lift, shard_drop = together(jnp.stack(line_lift), shard_drop)
        plane_lift = gather_plane(line_lift)
        line_drop = line_parts(shard_drop)
    residual, feed_input, attended_square, *made = attention_end(normed, block_input, residual, late, made)
    made[0] = made[0][0]
    if cube:
        plane_lift, line_drop, raw_grad, feed_input = together(plane_lift, line_drop, raw_grad, feed_input)
        corner_lift = gather_corner(*plane_lift)
        lift_others = over_cores(line_lift, *plane_lift)
    grad_rows, grad_bias = place_grad(raw_grad)
    if cube:
        corner_lift, lift_others, line_drop, grad_rows = together(
            corner_lift, lift_others, line_drop, grad_rows
        )
        lift_pieces = (line_lift,) + plane_lift + corner_lift
        lift_pieces += lift_others + over_cores(*corner_lift)
        line_drop = jnp.stack(line_drop)
        plane_drop = gather_plane(line_drop)
    else:
        lift_pieces = gather_pieces(shard_lift)
    acted, slope, lift_all = lift(feed_input, lift_pieces)
    if cube:
        plane_drop, acted = together(plane_drop, acted)
        corner_drop = gather_corner(*plane_drop)
        drop_others = over_cores(line_drop, *plane_drop)
    drop_send = drop_weight_grad(grad_rows, acted, 0)
    if cube:
        corner_drop, drop_others, drop_send, acted = together(corner_drop, drop_others, drop_send, acted)
        drop_received = swap(drop_send, "mp", 1)
        drop_pieces = (line_drop,) + plane_drop + corner_drop
        drop_pieces += drop_others + over_cores(*corner_drop)
    drop_keep = drop_weight_grad(grad_rows, acted, 2)
    if cube:
        drop_pieces, drop_received, drop_keep = together(drop_pieces, drop_received, drop_keep)
        corner, grad_rows = together(scatter_corner(drop_keep, drop_received), grad_rows)
        from_corner = send_corner(corner)
    else:
        drop_pieces = gather_pieces(shard_drop)
        drop_grad = scatter(drop_keep, drop_send)

    lift_send, drop_all, grad_feed = expert_back(drop_pieces, grad_rows, slope, feed_input, lift_all)
    if cube:
        from_corner, grad_feed = together(from_corner, grad_feed)
        plane = scatter_plane(drop_keep, drop_received, *from_corner)
        plane, lift_send, grad_feed = together(plane, lift_send, grad_feed)
        from_plane = send_plane(*plane)
        lift_received = swap(lift_send, "mp", 1)
    lift_keep, drop_all, grad_residual, grad_attended, grad_norm_second = expert_back_end(
        drop_all, grad_feed, residual, drop_pieces, grad_rows, slope, feed_input, lift_all
    )
    if cube:
        lift_received, from_plane, grad_attended = together(lift_received, from_plane, grad_attended)
        lift_corner = scatter_corner(lift_keep, lift_received)
        drop_line = scatter_line(drop_keep, drop_received, *from_plane)
        lift_corner, drop_line, acted = together(lift_corner, drop_line, acted)
        from_corner = send_corner(lift_corner)
        from_drop_line = send_line(drop_line)
    else:
        lift_grad = scatter(lift_keep, lift_send)
    raw_out, feed_square = drop(acted, residual, drop_all)
    if cube:
        from_corner, raw_out = together(from_corner, raw_out)
        plane = scatter_plane(lift_keep, lift_received, *from_corner)
        from_drop_line, plane, grad_attended = together(from_drop_line, plane, grad_attended)
        from_plane = send_plane(*plane)

    attend_send, grad_normed = attention_back(grad_attended, normed, *made)
    if cube:
        attend_received = swap(attend_send, "mp", 1)
        from_plane, raw_out, grad_normed = together(from_plane, raw_out, grad_normed)
        lift_line = scatter_line(lift_keep, lift_received, *from_plane)
        lift_line, grad_normed = together(lift_line, grad_normed)
        from_lift_line = send_line(lift_line)
    block_output = give_back(raw_out)
    attend_keep, grad_normed = attention_back_end(grad_normed, grad_attended, normed, *made)
    squares = jnp.stack(
        [jnp.sum(feed_square[0]), jnp.sum(attended_square), jnp.sum(feed_square[1]), used.astype(f32)]
    )
    squares = jnp.pad(squares, (0, model_width - 4))[None]
    if cube:
        attend_received, from_lift_line, squares, attend_keep = together(
            attend_received, from_lift_line, squares, attend_keep
        )
        corner = scatter_corner(attend_keep, attend_received)
        corner, block_output, grad_normed = together(corner, block_output, grad_normed)
        from_corner = send_corner(corner)
    block_output = block_output.astype(f32)
    grad_raw, grad_norm_first, grad_mask = finish_input_grad(grad_normed, grad_residual, block_input)
    small = (grad_norm_first, grad_norm_second, grad_bias, grad_mask, squares)
    if cube:
        from_corner, small, grad_raw = together(from_corner, small, grad_raw)
        plane = scatter_plane(attend_keep, attend_received, *from_corner)
        plane, small, grad_raw, block_output = together(plane, small, grad_raw, block_output)
        line = scatter_line(attend_keep, attend_received, *send_plane(*plane))
        line, small, grad_raw, drop_line, lift_line = together(line, small, grad_raw, drop_line, lift_line)
        attend_grad = add(line[0], *send_line(line))[0]
        drop_grad = add(drop_line[0], *from_drop_line)
        lift_grad = add(lift_line[0], *from_lift_line)
    else:
        attend_grad = scatter(attend_keep, attend_send)[0]
    input_grad = give_back(grad_raw).astype(f32)

    small = jnp.concatenate(small, axis=0)
    if cube:
        for axis, bit in (("mp", 1), ("dp", 1), ("mp", 2), ("dp", 2), ("dp", 4)):
            small = small + swap(small, axis, bit)
    else:
        small = lax.psum(small, ("dp", "mp"))
    norm_total, extra_total = small[:4], small[4:7]
    rms_values = jnp.sqrt(small[7, :3] / (small[7, 3] * model_width))

    joint_grad = jnp.stack([attend_grad[:, k * width : (k + 1) * width] for k in range(3)])
    output_grad = attend_grad[:, 3 * width :].T
    drop_grad = jnp.swapaxes(drop_grad, 1, 2)
    results = [block_output, input_grad, rms_values]
    results += adamw(joint_weight, joint_first, joint_second, joint_grad, matrix_rate, weight_decay)
    results += adamw(output_weight, output_first, output_second, output_grad, matrix_rate, weight_decay)
    results += adamw(lift_weight, lift_first, lift_second, lift_grad, matrix_rate, weight_decay)
    results += adamw(drop_weight, drop_first, drop_second, drop_grad, matrix_rate, weight_decay)
    results += adamw(norm_params, norm_first, norm_second, norm_total, vector_rate, 0.0)
    results += adamw(extra_params, extra_first, extra_second, extra_total, vector_rate, 0.0)
    return tuple(results)


def solution(mesh):
    rows = P(None, ("dp", "mp"), None)
    joint, output, lift, drop = (
        P(None, "dp", "mp"),
        P("mp", "dp"),
        P(None, "dp", "mp"),
        P(None, "mp", "dp"),
    )
    return jax.shard_map(
        body,
        mesh=mesh,
        in_specs=(rows, rows, P(None, "dp"), P(None, "dp"), P(None, "dp", None))
        + (joint,) * 3
        + (output,) * 3
        + (lift,) * 3
        + (drop,) * 3
        + (P(),) * 6,
        out_specs=(rows, rows, P())
        + (joint,) * 4
        + (output,) * 4
        + (lift,) * 4
        + (drop,) * 4
        + (P(),) * 8,
        check_vma=False,
    )
```

```python
import functools

import jax
import jax.numpy as jnp
from jax import lax
from jax.experimental import pallas as pl
from jax.experimental.pallas import tpu as pltpu
from jax.sharding import PartitionSpec as P

HEAD_DIM = 64
PATCHES = 197
TEXT_MAX = 40
STEP = 7

norm_epsilon = 1e-06
masked_score = -1000000000.0
first_decay = 0.9
second_decay = 0.98
adam_epsilon = 1e-06
matrix_rate = 0.04
vector_rate = 0.5
weight_decay = 0.01

PATCH_STRIDE = 208
TEXT_STRIDE = 48
ITEM_ROWS = PATCH_STRIDE + TEXT_STRIDE

bf16 = jnp.bfloat16
f32 = jnp.float32
VMEM_LIMIT = 58 * 1024 * 1024
ATTENTION_US = 18
LIFT_US = 16
DROP_WEIGHT_US = 7
EXPERT_BACK_US = 17
ATTENTION_BACK_US = 19
DROP_US = 17


def adamw(weight, first_state, second_state, gradient, step_rate, decay_rate):
    first_new = first_decay * first_state + (1.0 - first_decay) * gradient
    second_new = second_decay * second_state + (1.0 - second_decay) * gradient * gradient
    first_hat = first_new / (1.0 - first_decay**STEP)
    second_hat = second_new / (1.0 - second_decay**STEP)
    weight_new = weight - step_rate * (
        first_hat / (jnp.sqrt(second_hat) + adam_epsilon) + decay_rate * weight
    )
    return (weight_new, first_new, second_new, weight_new.astype(bf16))


def dot(left, right, left_dim, right_dim):
    return lax.dot_general(
        left,
        right,
        (((left_dim,), (right_dim,)), ((), ())),
        preferred_element_type=f32,
    )


def loop(count, body):
    lax.fori_loop(0, count, lambda i, c: (body(i), c)[1], 0)


def rows_at(index, size):
    return pl.ds(pl.multiple_of(index * size, 16), size)


def norm_forward(values, gain, shift):
    centred = values - jnp.mean(values, axis=-1, keepdims=True)
    spread = jnp.mean(centred * centred, axis=-1, keepdims=True)
    return centred * lax.rsqrt(spread + norm_epsilon) * gain + shift


def norm_backward(values, gain, grad):
    centred = values - jnp.mean(values, axis=-1, keepdims=True)
    spread = jnp.mean(centred * centred, axis=-1, keepdims=True)
    scale = lax.rsqrt(spread + norm_epsilon)
    hat = centred * scale
    grad_hat = grad * gain
    grad_values = scale * (
        grad_hat
        - jnp.mean(grad_hat, axis=-1, keepdims=True)
        - hat * jnp.mean(grad_hat * hat, axis=-1, keepdims=True)
    )
    grad_gain = jnp.sum(grad * hat, axis=0, keepdims=True)
    grad_shift = jnp.sum(grad, axis=0, keepdims=True)
    return grad_values, grad_gain, grad_shift


def one_hot(row_place, first_row, count):
    place = lax.broadcasted_iota(jnp.int32, (count, row_place.shape[1]), 0) + first_row
    return (place == row_place).astype(bf16)


def relative_block(mine, block):
    other = jnp.bitwise_xor(mine, block)
    return jnp.bitwise_and(other, 1) * 4 + jnp.right_shift(other, 1)


def piece_copies(pieces, mine, place_of, sems):
    even, *odd = pieces
    blocks = [(even, i, 2 * i) for i in range(4)]
    z = 0
    for ref in odd:
        for i in range(ref.shape[0]):
            blocks.append((ref, i, 2 * z + 1))
            z += 1
    size = even.shape[2]
    copies = []
    for index, (ref, i, block) in enumerate(blocks):
        first = jnp.bitwise_xor(mine, block) * size
        rows = pl.ds(pl.multiple_of(first, 16), size)
        copies.append(pltpu.make_async_copy(ref.at[i], place_of(rows), sems.at[index]))
    return copies


def step_parts(pieces):
    parts = []
    for step in range(2 * len(pieces) // 5):
        even, odd, high, front, back = pieces[len(pieces) - 5 - 5 * (step // 2) :][:5]
        parts.append((high, front, back) if step % 2 else (even, odd))
    return parts


def step_copies(parts, mine, weight_ref, sems):
    by_step = []
    for step, pieces in enumerate(parts):
        place_of = lambda rows, step=step: weight_ref.at[:, step, rows, :]
        by_step.append(piece_copies(pieces, mine, place_of, sems.at[step]))
    return by_step


def start_all(by_step):
    for copies in by_step:
        for copy in copies:
            copy.start()


def out_copy(weight_ref, out_ref, out_sems, step, places):
    return pltpu.make_async_copy(
        weight_ref.at[:, step], out_ref.at[:, places[step]], out_sems.at[step]
    )


def wait_step(by_step, weight_ref, out_ref, out_sems, places):
    for step, copies in enumerate(by_step):

        @pl.when(pl.program_id(0) == step)
        def _():
            for copy in copies:
                copy.wait()
            out_copy(weight_ref, out_ref, out_sems, step, places).start()


def wait_out(weight_ref, out_ref, out_sems, places):
    for step in range(weight_ref.shape[1]):
        out_copy(weight_ref, out_ref, out_sems, step, places).wait()


def store_grad(grad_ref, mine, index, first, rows, value):
    value = value.astype(bf16)
    size = grad_ref.shape[-2]
    for part in range(rows // size):
        place = relative_block(mine, first // size + part)
        grad_ref[0, place, index] = value[part * size : (part + 1) * size]


def attend(queries, keys, values, allowed):
    scores = [dot(key, query, 1, 1) for query, key in zip(queries, keys)]
    scores = [jnp.where(mask, score, masked_score) for mask, score in zip(allowed, scores)]
    tops = [jnp.max(score, axis=0, keepdims=True) for score in scores]
    weights = [jnp.exp(score - top) for score, top in zip(scores, tops)]
    totals = [jnp.sum(weight, axis=0, keepdims=True) for weight in weights]
    weights = [(weight * (1.0 / total)).astype(bf16) for weight, total in zip(weights, totals)]
    return weights, [dot(value, weight, 0, 0) for value, weight in zip(values, weights)]


def item_slices(items, i):
    first = items * PATCH_STRIDE + i * TEXT_STRIDE
    return slice(i * PATCH_STRIDE, (i + 1) * PATCH_STRIDE), slice(first, first + TEXT_STRIDE)


def item_rows(ref, index, items, i):
    patch_rows, text_rows = item_slices(items, i)
    return jnp.concatenate([ref[index + (patch_rows,)], ref[index + (text_rows,)]], axis=0)


def head_columns(rows, kind, heads, h):
    first = (kind * heads + h) * HEAD_DIM
    return rows[:, first : first + HEAD_DIM]


def attention_kernel(meta_ref, raw_ref, place_ref, hidden_ref, norm_ref, extra_ref, *refs, **sizes):
    parts, outs = (refs[:2], refs[2:4]), refs[4:]
    block_ref, normed_ref, residual_ref, out_ref, joint_ref, mixed_ref, probs_ref = outs[:7]
    weight_ref, sems, out_sems = outs[7:]
    items, main_rows, all_rows = sizes["items"], sizes["main_rows"], sizes["all_rows"]
    step = pl.program_id(0)
    by_step = step_copies(parts, meta_ref[items + 1], weight_ref, sems)

    @pl.when(step == 0)
    def _():
        start_all(by_step)

        def chunk(first, size):
            rows = pl.ds(first, size)
            picked = dot(one_hot(place_ref[...], first, size), raw_ref[...], 1, 0)
            picked = jnp.where(hidden_ref[rows, :] > 0, extra_ref[2:3, :], picked)
            block_ref[rows, :] = picked
            residual_ref[rows, :] = picked
            normed_ref[rows, :] = norm_forward(picked, norm_ref[0:1, :], norm_ref[1:2, :]).astype(bf16)

        loop(items, lambda i: chunk(pl.multiple_of(i * ITEM_ROWS, 16), ITEM_ROWS))
        chunk(main_rows, all_rows - main_rows)

    wait_step(by_step, weight_ref, out_ref, out_sems, (0, 2))
    attend_heads(
        meta_ref, weight_ref.at[0, step], normed_ref, residual_ref, joint_ref, mixed_ref, probs_ref, **sizes
    )

    @pl.when(step == pl.num_programs(0) - 1)
    def _():
        wait_out(weight_ref, out_ref, out_sems, (0, 2))


def attention_end_kernel(meta_ref, normed_ref, block_ref, before_ref, valid_ref, norm_ref, *refs, **sizes):
    parts, outs = (refs[:2], refs[2:4]), refs[8:]
    residual_ref, feed_ref, square_ref, out_ref, joint_ref, mixed_ref, probs_ref = outs[:7]
    weight_ref, sems, out_sems = outs[7:]
    items, main_rows, all_rows = sizes["items"], sizes["main_rows"], sizes["all_rows"]
    step = pl.program_id(0)
    by_step = step_copies(parts, meta_ref[items + 1], weight_ref, sems)

    @pl.when(step == 0)
    def _():
        start_all(by_step)
        residual_ref[...] = before_ref[...]

    wait_step(by_step, weight_ref, out_ref, out_sems, (1, 3))
    attend_heads(
        meta_ref, weight_ref.at[0, step], normed_ref, residual_ref, joint_ref, mixed_ref, probs_ref, **sizes
    )

    @pl.when(step == pl.num_programs(0) - 1)
    def _():
        square_ref[...] = jnp.zeros_like(square_ref)

        def chunk(rows):
            residual = residual_ref[rows, :]
            feed_ref[rows, :] = norm_forward(residual, norm_ref[2:3, :], norm_ref[3:4, :]).astype(bf16)
            attended = (residual - block_ref[rows, :]) * valid_ref[rows, :]
            square_ref[...] += jnp.sum(attended * attended, axis=0, keepdims=True)

        loop(items, lambda i: chunk(rows_at(i, ITEM_ROWS)))
        chunk(pl.ds(main_rows, all_rows - main_rows))
        wait_out(weight_ref, out_ref, out_sems, (1, 3))


def attend_heads(
    meta_ref,
    weight_ref,
    normed_ref,
    residual_ref,
    joint_ref,
    mixed_ref,
    probs_ref,
    *,
    items,
    heads,
    main_rows,
    all_rows,
):
    width = heads * HEAD_DIM
    tail_rows = all_rows - main_rows

    def project(rows):
        joint = dot(normed_ref[rows, :], weight_ref[:, : 3 * width], 1, 0)
        joint_ref[0, rows, :width] = (joint[:, :width].astype(bf16).astype(f32) * HEAD_DIM**-0.5).astype(bf16)
        joint_ref[0, rows, width:] = joint[:, width:].astype(bf16)

    project(pl.ds(0, all_rows))

    key_row = lax.broadcasted_iota(jnp.int32, (ITEM_ROWS, 1), 0)
    blocks = [item_rows(joint_ref, (0,), items, i) for i in range(items)]
    masks = [
        (key_row < PATCHES)
        | ((key_row >= PATCH_STRIDE) & (key_row < PATCH_STRIDE + meta_ref[i]))
        for i in range(items)
    ]
    blocks.append(joint_ref[0, main_rows:, :])
    masks.append(lax.broadcasted_iota(jnp.int32, (tail_rows, 1), 0) < meta_ref[items])
    pairs = [(i, h) for i in range(items + 1) for h in range(heads)]
    weights, outs = attend(
        *[[head_columns(blocks[i], kind, heads, h) for i, h in pairs] for kind in range(3)],
        [masks[i] for i, _ in pairs],
    )
    for (i, h), weight in zip(pairs, weights):
        if i < items:
            probs_ref[0, i, h] = weight
    for i in range(items + 1):
        mixed = jnp.concatenate(outs[i * heads : (i + 1) * heads], axis=0).T.astype(bf16)
        if i == items:
            mixed_ref[0, main_rows:, :] = mixed
        else:
            patch_rows, text_rows = item_slices(items, i)
            mixed_ref[0, patch_rows, :] = mixed[:PATCH_STRIDE]
            mixed_ref[0, text_rows, :] = mixed[PATCH_STRIDE:]

    def add_output(rows):
        residual_ref[rows, :] += dot(mixed_ref[0, rows, :], weight_ref[:, 3 * width :], 1, 1)

    add_output(pl.ds(0, all_rows))


def attention_back_kernel(
    mine_ref,
    grad_attended_ref,
    joint_ref,
    mixed_ref,
    probs_ref,
    normed_ref,
    weight_ref,
    grad_weight_ref,
    grad_normed_ref,
    grad_mixed_ref,
    grad_joint_ref,
    **sizes,
):
    @pl.when(pl.program_id(0) == 0)
    def _():
        grad_normed_ref[...] = jnp.zeros_like(grad_normed_ref)

    heads_back(
        mine_ref,
        grad_attended_ref,
        joint_ref,
        mixed_ref,
        probs_ref,
        normed_ref,
        weight_ref,
        grad_weight_ref,
        grad_normed_ref,
        grad_mixed_ref,
        grad_joint_ref,
        **sizes,
    )


def attention_back_end_kernel(
    mine_ref,
    grad_attended_ref,
    joint_ref,
    mixed_ref,
    probs_ref,
    normed_ref,
    weight_ref,
    before_ref,
    grad_weight_ref,
    grad_normed_ref,
    grad_mixed_ref,
    grad_joint_ref,
    **sizes,
):
    @pl.when(pl.program_id(0) == 0)
    def _():
        grad_normed_ref[...] = before_ref[...]

    heads_back(
        mine_ref,
        grad_attended_ref,
        joint_ref,
        mixed_ref,
        probs_ref,
        normed_ref,
        weight_ref,
        grad_weight_ref,
        grad_normed_ref,
        grad_mixed_ref,
        grad_joint_ref,
        **sizes,
    )


def input_grad_kernel(
    grad_normed_ref,
    grad_residual_ref,
    block_ref,
    hidden_ref,
    place_ref,
    norm_ref,
    *refs,
):
    small_refs, (grad_raw_ref, small_ref, grad_block_ref) = refs[:-3], refs[-3:]
    small_ref[...] = jnp.zeros_like(small_ref)
    first = 3
    for ref in small_refs:
        small_ref[first : first + ref.shape[0], :] = ref[...]
        first += ref.shape[0]

    def chunk(i):
        rows = rows_at(i, ITEM_ROWS)
        grad, gain, shift = norm_backward(block_ref[rows, :], norm_ref[0:1, :], grad_normed_ref[rows, :])
        small_ref[0:1, :] += gain
        small_ref[1:2, :] += shift
        grad = grad + grad_residual_ref[rows, :]
        hidden = hidden_ref[rows, :] > 0
        small_ref[2:3, :] += jnp.sum(jnp.where(hidden, grad, 0.0), axis=0, keepdims=True)
        grad_block_ref[rows, :] = jnp.where(hidden, 0.0, grad).astype(bf16)

    loop(grad_normed_ref.shape[0] // ITEM_ROWS, chunk)
    unplace(place_ref, grad_block_ref, grad_raw_ref, grad_block_ref.shape[0])


def heads_back(
    mine_ref,
    grad_attended_ref,
    joint_ref,
    mixed_ref,
    probs_ref,
    normed_ref,
    weight_ref,
    grad_weight_ref,
    grad_normed_ref,
    grad_mixed_ref,
    grad_joint_ref,
    *,
    items,
    heads,
):
    width = heads * HEAD_DIM
    half = HEAD_DIM**-0.5

    grad_mixed_ref[...] = dot(grad_attended_ref[...], weight_ref[0, :, 3 * width :], 1, 0).astype(bf16)

    blocks = [item_rows(joint_ref, (0,), items, i) for i in range(items)]
    outs = [item_rows(grad_mixed_ref, (), items, i) for i in range(items)]
    products = [
        (outs[i].astype(f32) * item_rows(mixed_ref, (0,), items, i).astype(f32)).T for i in range(items)
    ]
    pairs = [(i, h) for i in range(items) for h in range(heads)]
    queries, keys, values = [
        [head_columns(blocks[i], kind, heads, h) for i, h in pairs] for kind in range(3)
    ]
    grad_outs = [head_columns(outs[i], 0, heads, h) for i, h in pairs]
    weights = [probs_ref[0, i, h] for i, h in pairs]
    grad_probs = [dot(value, grad_out, 1, 1) for value, grad_out in zip(values, grad_outs)]
    means = [
        jnp.sum(products[i][h * HEAD_DIM : (h + 1) * HEAD_DIM], axis=0, keepdims=True) for i, h in pairs
    ]
    grad_scores = [
        (weight.astype(f32) * (grad - mean)).astype(bf16)
        for weight, grad, mean in zip(weights, grad_probs, means)
    ]
    grad_values = [dot(weight, grad_out, 1, 0).astype(bf16) for weight, grad_out in zip(weights, grad_outs)]
    grad_keys = [dot(score, query, 1, 0).astype(bf16) for score, query in zip(grad_scores, queries)]
    grad_queries = [dot(key, score, 0, 0) * half for key, score in zip(keys, grad_scores)]
    for i in range(items):
        own = slice(i * heads, (i + 1) * heads)
        grad_query = jnp.concatenate(grad_queries[own], axis=0).T.astype(bf16)
        grad_joint = jnp.concatenate([grad_query] + grad_keys[own] + grad_values[own], axis=1)
        patch_rows, text_rows = item_slices(items, i)
        grad_joint_ref[patch_rows, :] = grad_joint[:PATCH_STRIDE]
        grad_joint_ref[text_rows, :] = grad_joint[PATCH_STRIDE:]

    model_width = weight_ref.shape[1]
    for first in range(0, model_width, 384):
        cols = slice(first, first + 384)
        grad_weight = jnp.concatenate(
            [
                dot(normed_ref[:, cols], grad_joint_ref[...], 0, 0),
                dot(grad_attended_ref[:, cols], mixed_ref[0], 0, 0),
            ],
            axis=1,
        )
        store_grad(grad_weight_ref, mine_ref[0], 0, first, 384, grad_weight)

    grad_normed_ref[...] += dot(grad_joint_ref[...], weight_ref[0, :, : 3 * width], 1, 1)


def unplace(place_ref, source_ref, raw_ref, source_rows):
    source = source_ref[...].astype(bf16)
    raw_rows = raw_ref.shape[0]
    size = 240 if raw_rows % 240 == 0 else raw_rows

    def chunk(i):
        rows = rows_at(i, size)
        place = lax.broadcasted_iota(jnp.int32, (size, source_rows), 1)
        pick = (place == place_ref[rows, :]).astype(bf16)
        raw_ref[rows, :] = dot(pick, source, 1, 0).astype(bf16)

    loop(raw_rows // size, chunk)


def lift_kernel(mine_ref, feed_ref, *refs, vision_rows, all_rows):
    pieces, (acted_ref, slope_ref, out_ref, weight_ref, sems, out_sems) = refs[:10], refs[10:]
    by_step = step_copies(step_parts(pieces), mine_ref[0], weight_ref, sems)

    @pl.when(pl.program_id(0) == 0)
    def _():
        start_all(by_step)

    wait_step(by_step, weight_ref, out_ref, out_sems, (0, 1, 2, 3))

    def piece(rows, expert):
        lifted = dot(feed_ref[rows, :], weight_ref[expert, pl.program_id(0)], 1, 0)
        cumulative = 0.5 * (1.0 + lax.erf(lifted * (0.5**0.5)))
        density = jnp.exp(-0.5 * lifted * lifted) * ((2.0 * jnp.pi) ** -0.5)
        acted_ref[0, rows, :] = (lifted * cumulative).astype(bf16)
        slope_ref[0, rows, :] = (cumulative + lifted * density).astype(bf16)

    loop(2, lambda i: piece(rows_at(i, vision_rows // 2), 0))
    piece(pl.ds(vision_rows, all_rows - vision_rows), 1)

    @pl.when(pl.program_id(0) == pl.num_programs(0) - 1)
    def _():
        wait_out(weight_ref, out_ref, out_sems, (0, 1, 2, 3))


def place_grad_kernel(raw_ref, place_ref, grad_ref, grad_bias_ref, *, vision_rows):
    def chunk(i):
        rows = rows_at(i, ITEM_ROWS)
        pick = one_hot(place_ref[...], i * ITEM_ROWS, ITEM_ROWS)
        grad_ref[rows, :] = dot(pick, raw_ref[...], 1, 0).astype(bf16)

    loop(grad_ref.shape[0] // ITEM_ROWS, chunk)
    grad_bias_ref[0:1, :] = jnp.sum(grad_ref[:vision_rows, :].astype(f32), axis=0, keepdims=True)
    grad_bias_ref[1:2, :] = jnp.sum(grad_ref[vision_rows:, :].astype(f32), axis=0, keepdims=True)


def expert_weight_grad(grad_weight_ref, mine, left_ref, right, vision_rows):
    rows_total, width = left_ref.shape
    for expert, rows in ((0, slice(0, vision_rows)), (1, slice(vision_rows, rows_total))):
        for first in range(0, width, 384):
            grad_weight = dot(left_ref[rows, first : first + 384], right(rows), 0, 0)
            store_grad(grad_weight_ref, mine, expert, first, 384, grad_weight)


def drop_weight_kernel(mine_ref, grad_ref, acted_ref, grad_weight_ref, *, vision_rows):
    expert_weight_grad(
        grad_weight_ref, mine_ref[0], grad_ref, lambda rows: acted_ref[0, rows, :], vision_rows
    )


def drop_kernel(
    acted_ref,
    residual_ref,
    valid_ref,
    place_ref,
    extra_ref,
    weight_ref,
    raw_ref,
    square_ref,
    total_ref,
    *,
    vision_rows,
    all_rows,
):
    step = pl.program_id(0)
    text = all_rows - vision_rows

    @pl.when(step == 0)
    def _():
        total_ref[:vision_rows, :] = jnp.broadcast_to(extra_ref[0:1, :], (vision_rows, total_ref.shape[1]))
        total_ref[vision_rows:, :] = jnp.broadcast_to(extra_ref[1:2, :], (text, total_ref.shape[1]))

    def piece(rows, expert):
        total_ref[rows, :] += dot(acted_ref[0, rows, :], weight_ref[expert, 0], 1, 1)

    piece(pl.ds(0, vision_rows), 0)
    piece(pl.ds(vision_rows, text), 1)

    @pl.when(step == pl.num_programs(0) - 1)
    def _():
        square_ref[...] = jnp.zeros_like(square_ref)

        def finish(rows, expert):
            fed = total_ref[rows, :]
            out = residual_ref[rows, :] + fed
            valid = valid_ref[rows, :]
            square_ref[0:1, :] += jnp.sum(valid * out * out, axis=0, keepdims=True)
            square_ref[1:2, :] += jnp.sum(valid * fed * fed, axis=0, keepdims=True)
            total_ref[rows, :] = out

        loop(vision_rows // PATCH_STRIDE, lambda i: finish(rows_at(i, PATCH_STRIDE), 0))
        loop(3, lambda i: finish(pl.ds(pl.multiple_of(vision_rows + i * (text // 3), 16), text // 3), 1))
        unplace(place_ref, total_ref, raw_ref, all_rows)


def expert_back_step(
    mine_ref, grad_ref, slope_ref, feed_ref, lift_ref, drop_ref, grad_weight_ref, total_ref, lifted_ref, vision_rows
):
    step = pl.program_id(0)

    def piece(rows, expert):
        grad_acted = dot(grad_ref[rows, :], drop_ref[expert, step], 1, 0)
        grad_lifted = (grad_acted * slope_ref[0, rows, :].astype(f32)).astype(bf16)
        lifted_ref[rows, :] = grad_lifted
        total_ref[rows, :] += dot(grad_lifted, lift_ref[expert, 0], 1, 1)

    piece(pl.ds(0, vision_rows), 0)
    piece(pl.ds(vision_rows, grad_ref.shape[0] - vision_rows), 1)
    expert_weight_grad(
        grad_weight_ref, mine_ref[0], feed_ref, lambda rows: lifted_ref[rows, :], vision_rows
    )


def expert_back_kernel(mine_ref, grad_ref, slope_ref, feed_ref, lift_ref, *refs, vision_rows):
    pieces, (grad_weight_ref, out_ref, total_ref) = refs[:5], refs[5:8]
    lifted_ref, drop_ref, sems, out_sems = refs[8:]
    by_step = step_copies(step_parts(pieces), mine_ref[0], drop_ref, sems)

    @pl.when(pl.program_id(0) == 0)
    def _():
        start_all(by_step)
        total_ref[...] = jnp.zeros_like(total_ref)

    wait_step(by_step, drop_ref, out_ref, out_sems, (0, 1))
    expert_back_step(
        mine_ref, grad_ref, slope_ref, feed_ref, lift_ref, drop_ref, grad_weight_ref, total_ref, lifted_ref, vision_rows
    )

    @pl.when(pl.program_id(0) == pl.num_programs(0) - 1)
    def _():
        wait_out(drop_ref, out_ref, out_sems, (0, 1))


def expert_back_end_kernel(mine_ref, grad_ref, slope_ref, feed_ref, lift_ref, *refs, vision_rows):
    pieces, (_, before_ref, residual_ref, norm_ref) = refs[:5], refs[5:9]
    grad_weight_ref, out_ref, grad_residual_ref, grad_attended_ref, grad_norm_ref = refs[9:14]
    lifted_ref, drop_ref, sems, out_sems = refs[14:]
    by_step = step_copies(step_parts(pieces), mine_ref[0], drop_ref, sems)

    @pl.when(pl.program_id(0) == 0)
    def _():
        start_all(by_step)
        grad_residual_ref[...] = before_ref[...]

    wait_step(by_step, drop_ref, out_ref, out_sems, (2, 3))
    expert_back_step(
        mine_ref,
        grad_ref,
        slope_ref,
        feed_ref,
        lift_ref,
        drop_ref,
        grad_weight_ref,
        grad_residual_ref,
        lifted_ref,
        vision_rows,
    )

    @pl.when(pl.program_id(0) == pl.num_programs(0) - 1)
    def _():
        grad_norm_ref[...] = jnp.zeros_like(grad_norm_ref)

        def chunk(i):
            rows = rows_at(i, ITEM_ROWS)
            grad, gain, shift = norm_backward(
                residual_ref[rows, :], norm_ref[2:3, :], grad_residual_ref[rows, :]
            )
            grad_norm_ref[0:1, :] += gain
            grad_norm_ref[1:2, :] += shift
            grad = grad + grad_ref[rows, :].astype(f32)
            grad_residual_ref[rows, :] = grad
            grad_attended_ref[rows, :] = grad.astype(bf16)

        loop(grad_ref.shape[0] // ITEM_ROWS, chunk)
        wait_out(drop_ref, out_ref, out_sems, (2, 3))


def whole(*shape):
    return pl.BlockSpec(shape, lambda *_: (0,) * len(shape))


def stepped(*shape, first=0):
    return pl.BlockSpec(shape, lambda i, *_: (i + first,) + (0,) * (len(shape) - 1))


def stepped_pair(*shape, first=0):
    return pl.BlockSpec(shape, lambda i, *_: (0, i + first) + (0,) * (len(shape) - 2))


def every_other(*shape, first=0):
    return pl.BlockSpec(shape, lambda i, *_: (2 * i + first,) + (0,) * (len(shape) - 1))


def anywhere(values):
    return (values, pl.BlockSpec(memory_space=pl.ANY))


def call(kernel, name, steps, ins, outs, scratch, microseconds, scalars=(), aliases=None):
    return pl.pallas_call(
        kernel,
        name=name,
        grid_spec=pltpu.PrefetchScalarGridSpec(
            num_scalar_prefetch=len(scalars),
            grid=(steps,),
            in_specs=[block for _, block in ins],
            out_specs=[block for _, _, block in outs],
            scratch_shapes=scratch,
        ),
        out_shape=[jax.ShapeDtypeStruct(shape, kind) for shape, kind, _ in outs],
        input_output_aliases=aliases or {},
        compiler_params=pltpu.CompilerParams(
            dimension_semantics=("arbitrary",), vmem_limit_bytes=VMEM_LIMIT
        ),
        cost_estimate=pl.CostEstimate(
            flops=int(microseconds * 1e9), bytes_accessed=int(microseconds * 1e6), transcendentals=0
        ),
    )(*scalars, *[array for array, _ in ins])


def body(
    tokens,
    cotangent,
    text_lengths,
    modality,
    masked_positions,
    joint_weight,
    joint_first,
    joint_second,
    output_weight,
    output_first,
    output_second,
    lift_weight,
    lift_first,
    lift_second,
    drop_weight,
    drop_first,
    drop_second,
    norm_params,
    norm_first,
    norm_second,
    extra_params,
    extra_first,
    extra_second,
):
    micro_count, shard_rows, model_width = tokens.shape
    block_rows = modality.shape[1]
    parts = block_rows // shard_rows
    assert micro_count == parts
    items = text_lengths.shape[1]
    width = joint_weight.shape[2]
    heads = width // HEAD_DIM
    hidden_width = lift_weight.shape[2]
    shard = joint_weight.shape[1]
    vision_rows = items * PATCH_STRIDE
    main_rows = items * ITEM_ROWS
    tail = block_rows - items * PATCHES - TEXT_MAX - (items - 1)
    tail = (tail + 47) // 48 * 48
    all_rows = main_rows + tail
    assert 4 * width == model_width and hidden_width == model_width

    shard_attend = jnp.concatenate(
        [joint_weight[0], joint_weight[1], joint_weight[2], output_weight.T], axis=1
    ).astype(bf16)[None]
    shard_lift = lift_weight.astype(bf16)
    shard_drop = jnp.swapaxes(drop_weight, 1, 2).astype(bf16)

    groups = lax.axis_size("dp")
    cube = groups == 8
    piece = model_width // 8
    if cube:
        mine = jnp.stack([lax.axis_index("dp"), lax.axis_index("mp")]).astype(jnp.int32)
    else:
        mine = jnp.zeros((2,), jnp.int32)

    def together(*values):
        return lax.optimization_barrier(values)

    def swap(values, axis, bit):
        size = lax.axis_size(axis)
        return lax.ppermute(values, axis, [(i, i ^ bit) for i in range(size)])

    def exchange(values):
        return lax.all_to_all(values, "mp", split_axis=0, concat_axis=1, tiled=True)[0]

    def give_back(values):
        return lax.all_to_all(
            values.reshape(parts, shard_rows, model_width), "mp", split_axis=0, concat_axis=0, tiled=True
        )

    def gather(values):
        whole_values = lax.all_gather(values, ("mp", "dp"), axis=1, tiled=True)
        return whole_values.reshape(-1, parts, model_width, values.shape[2])

    def gather_pieces(values):
        whole_values = jnp.swapaxes(gather(values).reshape(-1, parts, 4, 2, piece, model_width), 0, 3)
        pieces = []
        for core in range(2):
            low, high = whole_values[:, core], whole_values[:, 2 + core]
            pieces += [low[0], low[1], high[0], high[1, :2], high[1, 2:]]
        return pieces

    def line_parts(values):
        return (values,) + tuple(swap(values, "dp", bit) for bit in (2, 4, 6))

    def gather_line(values):
        return jnp.stack(line_parts(values))

    def gather_plane(line):
        return swap(line, "dp", 1), swap(line, "mp", 2)

    def gather_corner(along_x, along_y):
        return swap(along_x[:2], "mp", 2), swap(along_y[2:], "dp", 1)

    def over_cores(*pieces):
        return tuple(swap(part, "mp", 1) for part in pieces)

    def add(*terms):
        total = terms[0].astype(f32)
        for term in terms[1:]:
            total = total + term.astype(f32)
        return total

    def scatter(keep, send):
        shape = (2, 2, 4) + keep.shape[2:]
        both = jnp.stack([keep.reshape(shape), send.reshape(shape)], axis=1)
        both = jnp.transpose(both, (4, 0, 1, 3, 2, 5, 6))
        return reduce(both.reshape(both.shape[0], parts * model_width, shape[-1]))

    def reduce(values):
        values = lax.psum_scatter(values, ("mp", "dp"), scatter_dimension=1, tiled=True)
        return values.astype(f32)

    def quarters(keep, received, *others):
        keep, received, others = together(keep, received, others)
        shape = (2, 2, 4) + keep.shape[2:]
        keep, received = keep.reshape(shape), received.reshape(shape)
        return (lambda y, x: add(keep[y, x], received[y, x])), others

    def scatter_corner(keep, received):
        quarter, _ = quarters(keep, received)
        return quarter(1, 1).astype(bf16)

    def scatter_plane(keep, received, from_x, from_y):
        quarter, (from_x, from_y) = quarters(keep, received, from_x, from_y)
        part_x, part_y = quarter(0, 1), quarter(1, 0)
        part_x = jnp.concatenate([part_x[:2], add(part_x[2:], from_y)]).astype(bf16)
        part_y = jnp.concatenate([add(part_y[:2], from_x), part_y[2:]]).astype(bf16)
        return part_x, part_y

    def scatter_line(keep, received, from_x, from_y):
        quarter, (from_x, from_y) = quarters(keep, received, from_x, from_y)
        return add(quarter(0, 0), from_x, from_y).astype(bf16)

    def send_corner(corner):
        return swap(corner[:2], "dp", 1), swap(corner[2:], "mp", 2)

    def send_plane(part_x, part_y):
        return swap(part_x, "dp", 1), swap(part_y, "mp", 2)

    def send_line(line):
        return tuple(swap(line[i], "dp", 2 * i) for i in (1, 2, 3))

    micro = lax.axis_index("mp")
    lengths = lax.dynamic_index_in_dim(text_lengths, micro, 0, keepdims=False)
    masked = lax.dynamic_index_in_dim(masked_positions, micro, 0, keepdims=False)
    item_ids = jnp.arange(items, dtype=jnp.int32)
    sizes = PATCHES + lengths
    ends = jnp.sum(jnp.where(item_ids[:, None] <= item_ids[None, :], sizes[:, None], 0), axis=0)
    used = jnp.sum(sizes)

    def place_of(row):
        segment = jnp.sum((row[..., None] >= ends).astype(jnp.int32), axis=-1)
        start = jnp.sum(jnp.where(row[..., None] >= ends, sizes, 0), axis=-1)
        inside = row - start
        return jnp.where(
            segment == items,
            main_rows + inside,
            jnp.where(
                inside < PATCHES,
                PATCH_STRIDE * segment + inside,
                vision_rows + TEXT_STRIDE * segment + inside - PATCHES,
            ),
        )

    places = together(place_of(jnp.arange(block_rows, dtype=jnp.int32)))[0]
    place_row, place_column = places[None, :], places[:, None]
    targets = (vision_rows + TEXT_STRIDE * item_ids[:, None] + masked).reshape(-1)
    spots = jnp.arange(all_rows, dtype=jnp.int32)
    hidden = jnp.any(spots[:, None] == targets[None, :], axis=1).astype(jnp.int32)[:, None]
    text_spot = spots - vision_rows
    text_item = text_spot // TEXT_STRIDE
    text_end = jnp.sum(jnp.where(text_item[:, None] == item_ids, lengths, 0), axis=1)
    valid = jnp.where(
        text_spot < 0, spots % PATCH_STRIDE < PATCHES, text_spot - text_item * TEXT_STRIDE < text_end
    )
    valid = valid.astype(f32)[:, None]
    meta = jnp.concatenate([lengths, (block_rows - used)[None], mine[:1]])

    def rows_of(count, kind):
        return ((count, model_width), kind, whole(count, model_width))

    def plain(values):
        return (values, whole(*values.shape))

    def heads_out(first):
        shapes = [
            (parts, all_rows, 3 * width),
            (parts, all_rows, width),
            (parts, items, heads, ITEM_ROWS, ITEM_ROWS),
        ]
        return [(shape, bf16, every_other(1, *shape[1:], first=first)) for shape in shapes]

    def whole_weight(count):
        return ((count, parts, model_width, model_width), bf16, pl.BlockSpec(memory_space=pl.ANY))

    def weight_scratch(count, steps):
        return [
            pltpu.VMEM((count, steps, model_width, model_width), bf16),
            pltpu.SemaphoreType.DMA((steps, 8)),
            pltpu.SemaphoreType.DMA((steps,)),
        ]

    def part_weight(values, first, count=2):
        return (values, stepped_pair(count, 1, *values.shape[2:], first=first))

    def grad_out(count):
        shape = (2, 8, count, piece, model_width)
        return (shape, bf16, stepped(1, *shape[1:]))

    head_sizes = dict(items=items, heads=heads)
    row_sizes = dict(main_rows=main_rows, all_rows=all_rows)

    def attention(raw, pieces):
        return call(
            functools.partial(attention_kernel, **head_sizes, **row_sizes),
            "attention",
            2,
            [plain(raw), plain(place_row), plain(hidden), plain(norm_params), plain(extra_params)]
            + [anywhere(values) for values in pieces],
            [rows_of(all_rows, f32), rows_of(all_rows, bf16), rows_of(all_rows, f32), whole_weight(1)]
            + heads_out(0),
            weight_scratch(1, 2),
            ATTENTION_US,
            (meta,),
        )

    def attention_end(normed, block_input, residual, pieces, made):
        return call(
            functools.partial(attention_end_kernel, **head_sizes, **row_sizes),
            "attention_end",
            2,
            [plain(normed), plain(block_input), plain(residual), plain(valid), plain(norm_params)]
            + [anywhere(values) for values in pieces]
            + [anywhere(values) for values in made],
            [rows_of(all_rows, f32), rows_of(all_rows, bf16), rows_of(1, f32), whole_weight(1)]
            + heads_out(1),
            weight_scratch(1, 2),
            ATTENTION_US,
            (meta,),
            {10 + i: 3 + i for i in range(4)},
        )

    def lift(feed_input, pieces):
        shape = (parts, all_rows, hidden_width)
        return call(
            functools.partial(lift_kernel, vision_rows=vision_rows, all_rows=all_rows),
            "lift",
            parts,
            [plain(feed_input)] + [anywhere(values) for values in pieces],
            [(shape, bf16, stepped(1, *shape[1:]))] * 2 + [whole_weight(2)],
            weight_scratch(2, parts),
            LIFT_US,
            (mine,),
        )

    def place_grad(raw):
        return call(
            functools.partial(place_grad_kernel, vision_rows=vision_rows),
            "place_grad",
            1,
            [plain(raw), plain(place_row)],
            [rows_of(main_rows, bf16), rows_of(2, f32)],
            [],
            5,
        )

    def drop_weight_grad(grad_rows, acted, first):
        return call(
            functools.partial(drop_weight_kernel, vision_rows=vision_rows),
            "drop_weight_grad",
            2,
            [plain(grad_rows), (acted, stepped(1, main_rows, hidden_width, first=first))],
            [grad_out(2)],
            [],
            DROP_WEIGHT_US,
            (mine,),
        )[0]

    def expert_ins(grad_rows, slope, feed_input, lift_weights, pieces, first):
        return [
            plain(grad_rows),
            (slope, stepped(1, main_rows, hidden_width, first=first)),
            (feed_input, whole(main_rows, model_width)),
            part_weight(lift_weights, first),
        ] + [anywhere(values) for values in pieces]

    drop_out = whole_weight(2)
    expert_scratch = [pltpu.VMEM((main_rows, hidden_width), bf16)] + weight_scratch(2, 2)

    def expert_back(pieces, *args):
        return call(
            functools.partial(expert_back_kernel, vision_rows=vision_rows),
            "expert_back",
            2,
            expert_ins(*args, pieces[5:], 0),
            [grad_out(2), drop_out, rows_of(main_rows, f32)],
            expert_scratch,
            EXPERT_BACK_US,
            (mine,),
        )

    def expert_back_end(made, before, residual, pieces, *args):
        return call(
            functools.partial(expert_back_end_kernel, vision_rows=vision_rows),
            "expert_back_end",
            2,
            expert_ins(*args, pieces[:5], 2)
            + [anywhere(made), plain(before), (residual, whole(main_rows, model_width))]
            + [plain(norm_params)],
            [grad_out(2), drop_out, rows_of(main_rows, f32), rows_of(main_rows, bf16)]
            + [rows_of(2, f32)],
            expert_scratch,
            EXPERT_BACK_US,
            (mine,),
            {10: 1},
        )

    def heads_ins(grad_attended, normed, weights, joint_rows, mixed, probs, first):
        return [
            plain(grad_attended),
            (joint_rows, stepped(1, main_rows, 3 * width, first=first)),
            (mixed, stepped(1, main_rows, width, first=first)),
            (probs, stepped(1, *probs.shape[1:], first=first)),
            (normed, whole(main_rows, model_width)),
            (weights, stepped(1, model_width, model_width, first=first)),
        ]

    heads_scratch = [
        pltpu.VMEM((main_rows, width), bf16),
        pltpu.VMEM((main_rows, 3 * width), bf16),
    ]

    def attention_back(*args):
        return call(
            functools.partial(attention_back_kernel, **head_sizes),
            "attention_back",
            2,
            heads_ins(*args, 0),
            [grad_out(1), rows_of(main_rows, f32)],
            heads_scratch,
            ATTENTION_BACK_US,
            (mine,),
        )

    def attention_back_end(before, *args):
        return call(
            functools.partial(attention_back_end_kernel, **head_sizes),
            "attention_back_end",
            2,
            heads_ins(*args, 2) + [plain(before)],
            [grad_out(1), rows_of(main_rows, f32)],
            heads_scratch,
            ATTENTION_BACK_US,
            (mine,),
        )

    def finish_input_grad(grad_normed, grad_residual, block_input, *sums):
        return call(
            input_grad_kernel,
            "input_grad",
            1,
            [
                plain(grad_normed),
                plain(grad_residual),
                (block_input, whole(main_rows, model_width)),
                (hidden, whole(main_rows, 1)),
                plain(place_column),
                plain(norm_params),
            ]
            + [plain(values) for values in sums],
            [rows_of(block_rows, bf16), rows_of(16, f32)],
            [pltpu.VMEM((main_rows, model_width), bf16)],
            9,
        )

    def drop(acted, residual, weights):
        return call(
            functools.partial(drop_kernel, vision_rows=vision_rows, all_rows=all_rows),
            "drop",
            parts,
            [(acted, stepped(1, all_rows, hidden_width)), plain(residual), plain(valid)]
            + [plain(place_column), plain(extra_params)]
            + [part_weight(weights, 0)],
            [rows_of(block_rows, bf16), rows_of(2, f32)],
            [pltpu.VMEM((all_rows, model_width), f32)],
            DROP_US,
        )

    used_row = jnp.where(jnp.arange(model_width)[None, :] == 0, used.astype(f32), 0.0)
    tables = (place_row, place_column, hidden, valid, meta)
    raw_tokens = exchange(tokens)
    if cube:
        line = gather_line(shard_attend)
        even, high = gather_plane(line)
        even, high, raw_tokens, shard_lift, cotangent, tables = together(
            even, high, raw_tokens, shard_lift, cotangent, tables
        )
        place_row, place_column, hidden, valid, meta = tables
        corner = swap(high, "dp", 1)
        line_lift = line_parts(shard_lift)
        raw_grad = exchange(cotangent.astype(bf16))
        early = over_cores(line, even) + (line, even)
    else:
        pieces = gather_pieces(shard_attend)
        early = [pieces[i] for i in (5, 6, 0, 1)]
        late = [pieces[7], jnp.concatenate(pieces[8:10]), pieces[2], jnp.concatenate(pieces[3:5])]
        raw_grad = exchange(cotangent.astype(bf16))

    block_input, normed, residual, *made = attention(raw_tokens, early)
    if cube:
        corner, line_lift, raw_grad, residual = together(corner, line_lift, raw_grad, residual)
        late = over_cores(high, corner) + (high, corner)
        line_lift, shard_drop = together(jnp.stack(line_lift), shard_drop)
        plane_lift = gather_plane(line_lift)
        line_drop = line_parts(shard_drop)
    residual, feed_input, attended_square, *made = attention_end(normed, block_input, residual, late, made)
    made[0] = made[0][0]
    if cube:
        plane_lift, line_drop, raw_grad, feed_input = together(plane_lift, line_drop, raw_grad, feed_input)
        corner_lift = gather_corner(*plane_lift)
        lift_others = over_cores(line_lift, *plane_lift)
    grad_rows, grad_bias = place_grad(raw_grad)
    if cube:
        corner_lift, lift_others, line_drop, grad_rows = together(
            corner_lift, lift_others, line_drop, grad_rows
        )
        lift_pieces = (line_lift,) + plane_lift + corner_lift
        lift_pieces += lift_others + over_cores(*corner_lift)
        line_drop = jnp.stack(line_drop)
        plane_drop = gather_plane(line_drop)
    else:
        lift_pieces = gather_pieces(shard_lift)
    acted, slope, lift_all = lift(feed_input, lift_pieces)
    if cube:
        plane_drop, acted = together(plane_drop, acted)
        corner_drop = gather_corner(*plane_drop)
        drop_others = over_cores(line_drop, *plane_drop)
    drop_send = drop_weight_grad(grad_rows, acted, 0)
    if cube:
        corner_drop, drop_others, drop_send, acted = together(corner_drop, drop_others, drop_send, acted)
        drop_received = swap(drop_send, "mp", 1)
        drop_pieces = (line_drop,) + plane_drop + corner_drop
        drop_pieces += drop_others + over_cores(*corner_drop)
    drop_keep = drop_weight_grad(grad_rows, acted, 2)
    if cube:
        drop_pieces, drop_received, drop_keep = together(drop_pieces, drop_received, drop_keep)
        corner, grad_rows = together(scatter_corner(drop_keep, drop_received), grad_rows)
        from_corner = send_corner(corner)
    else:
        drop_pieces = gather_pieces(shard_drop)
        drop_grad = scatter(drop_keep, drop_send)

    lift_send, drop_all, grad_feed = expert_back(drop_pieces, grad_rows, slope, feed_input, lift_all)
    if cube:
        from_corner, grad_feed = together(from_corner, grad_feed)
        plane = scatter_plane(drop_keep, drop_received, *from_corner)
        plane, lift_send, grad_feed = together(plane, lift_send, grad_feed)
        from_plane = send_plane(*plane)
        lift_received = swap(lift_send, "mp", 1)
    lift_keep, drop_all, grad_residual, grad_attended, grad_norm_second = expert_back_end(
        drop_all, grad_feed, residual, drop_pieces, grad_rows, slope, feed_input, lift_all
    )
    if cube:
        lift_received, from_plane, grad_attended = together(lift_received, from_plane, grad_attended)
        corner = scatter_corner(lift_keep, lift_received)
        drop_line = scatter_line(drop_keep, drop_received, *from_plane)
        corner, drop_line, acted = together(corner, drop_line, acted)
        from_corner = send_corner(corner)
        from_drop_line = send_line(drop_line)
    else:
        lift_grad = scatter(lift_keep, lift_send)
    raw_out, squares = drop(acted, residual, drop_all)
    if cube:
        from_corner, raw_out = together(from_corner, raw_out)
        plane = scatter_plane(lift_keep, lift_received, *from_corner)
        from_drop_line, plane, grad_attended = together(from_drop_line, plane, grad_attended)
        from_plane = send_plane(*plane)

    attend_send, grad_normed = attention_back(grad_attended, normed, *made)
    if cube:
        attend_received = swap(attend_send, "mp", 1)
        from_plane, raw_out, grad_normed = together(from_plane, raw_out, grad_normed)
        lift_line = scatter_line(lift_keep, lift_received, *from_plane)
        lift_line, grad_normed = together(lift_line, grad_normed)
        from_lift_line = send_line(lift_line)
    block_output = give_back(raw_out)
    attend_keep, grad_normed = attention_back_end(grad_normed, grad_attended, normed, *made)
    if cube:
        attend_received, from_lift_line, attend_keep = together(
            attend_received, from_lift_line, attend_keep
        )
        corner = scatter_corner(attend_keep, attend_received)
        corner, block_output, grad_normed = together(corner, block_output, grad_normed)
        from_corner = send_corner(corner)
    block_output = block_output.astype(f32)
    grad_raw, small = finish_input_grad(
        grad_normed,
        grad_residual,
        block_input,
        *(grad_norm_second, grad_bias, squares, attended_square, used_row),
    )
    if cube:
        from_corner, small, grad_raw = together(from_corner, small, grad_raw)
        plane = scatter_plane(attend_keep, attend_received, *from_corner)
        plane, small, grad_raw, block_output = together(plane, small, grad_raw, block_output)
        from_plane = send_plane(*plane)
        for axis, bit in (("mp", 1), ("dp", 1)):
            small = small + swap(small, axis, bit)
        line = scatter_line(attend_keep, attend_received, *from_plane)
        line, small, grad_raw, drop_line, lift_line = together(line, small, grad_raw, drop_line, lift_line)
        attend_grad = add(line[0], *send_line(line))[0]
        drop_grad = add(drop_line[0], *from_drop_line)
        lift_grad = add(lift_line[0], *from_lift_line)
    else:
        attend_grad = scatter(attend_keep, attend_send)[0]
    input_grad = give_back(grad_raw).astype(f32)

    if cube:
        for axis, bit in (("mp", 2), ("dp", 2), ("dp", 4)):
            small = small + swap(small, axis, bit)
    else:
        small = lax.psum(small, ("dp", "mp"))
    norm_total = jnp.concatenate([small[0:2], small[3:5]])
    extra_total = jnp.concatenate([small[5:7], small[2:3]])
    sums = jnp.sum(small[7:11], axis=1)
    rms_values = jnp.sqrt(jnp.stack([sums[0], sums[2], sums[1]]) / (sums[3] * model_width))

    joint_grad = jnp.stack([attend_grad[:, k * width : (k + 1) * width] for k in range(3)])
    output_grad = attend_grad[:, 3 * width :].T
    drop_grad = jnp.swapaxes(drop_grad, 1, 2)
    results = [block_output, input_grad, rms_values]
    results += adamw(joint_weight, joint_first, joint_second, joint_grad, matrix_rate, weight_decay)
    results += adamw(output_weight, output_first, output_second, output_grad, matrix_rate, weight_decay)
    results += adamw(lift_weight, lift_first, lift_second, lift_grad, matrix_rate, weight_decay)
    results += adamw(drop_weight, drop_first, drop_second, drop_grad, matrix_rate, weight_decay)
    results += adamw(norm_params, norm_first, norm_second, norm_total, vector_rate, 0.0)
    results += adamw(extra_params, extra_first, extra_second, extra_total, vector_rate, 0.0)
    return tuple(results)


def solution(mesh):
    rows = P(None, ("dp", "mp"), None)
    joint, output, lift, drop = (
        P(None, "dp", "mp"),
        P("mp", "dp"),
        P(None, "dp", "mp"),
        P(None, "mp", "dp"),
    )
    return jax.shard_map(
        body,
        mesh=mesh,
        in_specs=(rows, rows, P(None, "dp"), P(None, "dp"), P(None, "dp", None))
        + (joint,) * 3
        + (output,) * 3
        + (lift,) * 3
        + (drop,) * 3
        + (P(),) * 6,
        out_specs=(rows, rows, P())
        + (joint,) * 4
        + (output,) * 4
        + (lift,) * 4
        + (drop,) * 4
        + (P(),) * 8,
        check_vma=False,
    )
```

```python
import functools

import jax
import jax.numpy as jnp
from jax import lax
from jax.experimental import pallas as pl
from jax.experimental.pallas import tpu as pltpu
from jax.sharding import PartitionSpec as P

HEAD_DIM = 64
PATCHES = 197
TEXT_MAX = 40
STEP = 7

norm_epsilon = 1e-06
masked_score = -1000000000.0
first_decay = 0.9
second_decay = 0.98
adam_epsilon = 1e-06
matrix_rate = 0.04
vector_rate = 0.5
weight_decay = 0.01

PATCH_STRIDE = 208
TEXT_STRIDE = 48
ITEM_ROWS = PATCH_STRIDE + TEXT_STRIDE

bf16 = jnp.bfloat16
f32 = jnp.float32
VMEM_LIMIT = 58 * 1024 * 1024
ATTENTION_US = 18
LIFT_US = 16
DROP_WEIGHT_US = 7
EXPERT_BACK_US = 17
ATTENTION_BACK_US = 19
DROP_US = 17


def adamw(weight, first_state, second_state, gradient, step_rate, decay_rate):
    first_new = first_decay * first_state + (1.0 - first_decay) * gradient
    second_new = second_decay * second_state + (1.0 - second_decay) * gradient * gradient
    first_hat = first_new / (1.0 - first_decay**STEP)
    second_hat = second_new / (1.0 - second_decay**STEP)
    weight_new = weight - step_rate * (
        first_hat / (jnp.sqrt(second_hat) + adam_epsilon) + decay_rate * weight
    )
    return (weight_new, first_new, second_new, weight_new.astype(bf16))


def dot(left, right, left_dim, right_dim):
    return lax.dot_general(
        left,
        right,
        (((left_dim,), (right_dim,)), ((), ())),
        preferred_element_type=f32,
    )


def loop(count, body):
    lax.fori_loop(0, count, lambda i, c: (body(i), c)[1], 0)


def rows_at(index, size):
    return pl.ds(pl.multiple_of(index * size, 16), size)


def norm_forward(values, gain, shift):
    centred = values - jnp.mean(values, axis=-1, keepdims=True)
    spread = jnp.mean(centred * centred, axis=-1, keepdims=True)
    return centred * lax.rsqrt(spread + norm_epsilon) * gain + shift


def norm_backward(values, gain, grad):
    centred = values - jnp.mean(values, axis=-1, keepdims=True)
    spread = jnp.mean(centred * centred, axis=-1, keepdims=True)
    scale = lax.rsqrt(spread + norm_epsilon)
    hat = centred * scale
    grad_hat = grad * gain
    grad_values = scale * (
        grad_hat
        - jnp.mean(grad_hat, axis=-1, keepdims=True)
        - hat * jnp.mean(grad_hat * hat, axis=-1, keepdims=True)
    )
    grad_gain = jnp.sum(grad * hat, axis=0, keepdims=True)
    grad_shift = jnp.sum(grad, axis=0, keepdims=True)
    return grad_values, grad_gain, grad_shift


def one_hot(row_place, first_row, count):
    place = lax.broadcasted_iota(jnp.int32, (count, row_place.shape[1]), 0) + first_row
    return (place == row_place).astype(bf16)


def relative_block(mine, block):
    other = jnp.bitwise_xor(mine, block)
    return jnp.bitwise_and(other, 1) * 4 + jnp.right_shift(other, 1)


def piece_copies(pieces, mine, place_of, sems):
    even, *odd = pieces
    blocks = [(even, i, 2 * i) for i in range(4)]
    z = 0
    for ref in odd:
        for i in range(ref.shape[0]):
            blocks.append((ref, i, 2 * z + 1))
            z += 1
    size = even.shape[2]
    copies = []
    for index, (ref, i, block) in enumerate(blocks):
        first = jnp.bitwise_xor(mine, block) * size
        rows = pl.ds(pl.multiple_of(first, 16), size)
        copies.append(pltpu.make_async_copy(ref.at[i], place_of(rows), sems.at[index]))
    return copies


def step_parts(pieces):
    parts = []
    for step in range(2 * len(pieces) // 5):
        even, odd, high, front, back = pieces[len(pieces) - 5 - 5 * (step // 2) :][:5]
        parts.append((high, front, back) if step % 2 else (even, odd))
    return parts


def step_copies(parts, mine, weight_ref, sems):
    by_step = []
    for step, pieces in enumerate(parts):
        place_of = lambda rows, step=step: weight_ref.at[:, step, rows, :]
        by_step.append(piece_copies(pieces, mine, place_of, sems.at[step]))
    return by_step


def start_all(by_step):
    for copies in by_step:
        for copy in copies:
            copy.start()


def out_copy(weight_ref, out_ref, out_sems, step, places):
    return pltpu.make_async_copy(
        weight_ref.at[:, step], out_ref.at[:, places[step]], out_sems.at[step]
    )


def wait_step(by_step, weight_ref, out_ref, out_sems, places):
    for step, copies in enumerate(by_step):

        @pl.when(pl.program_id(0) == step)
        def _():
            for copy in copies:
                copy.wait()
            out_copy(weight_ref, out_ref, out_sems, step, places).start()


def wait_out(weight_ref, out_ref, out_sems, places):
    for step in range(weight_ref.shape[1]):
        out_copy(weight_ref, out_ref, out_sems, step, places).wait()


def store_grad(grad_ref, mine, index, first, rows, value):
    value = value.astype(bf16)
    size = grad_ref.shape[-2]
    for part in range(rows // size):
        place = relative_block(mine, first // size + part)
        grad_ref[0, place, index] = value[part * size : (part + 1) * size]


def attend(queries, keys, values, allowed):
    scores = [dot(key, query, 1, 1) for query, key in zip(queries, keys)]
    scores = [jnp.where(mask, score, masked_score) for mask, score in zip(allowed, scores)]
    tops = [jnp.max(score, axis=0, keepdims=True) for score in scores]
    weights = [jnp.exp(score - top) for score, top in zip(scores, tops)]
    totals = [jnp.sum(weight, axis=0, keepdims=True) for weight in weights]
    weights = [(weight * (1.0 / total)).astype(bf16) for weight, total in zip(weights, totals)]
    return weights, [dot(value, weight, 0, 0) for value, weight in zip(values, weights)]


def item_slices(items, i):
    first = items * PATCH_STRIDE + i * TEXT_STRIDE
    return slice(i * PATCH_STRIDE, (i + 1) * PATCH_STRIDE), slice(first, first + TEXT_STRIDE)


def item_rows(ref, index, items, i):
    patch_rows, text_rows = item_slices(items, i)
    return jnp.concatenate([ref[index + (patch_rows,)], ref[index + (text_rows,)]], axis=0)


def head_columns(rows, kind, heads, h):
    first = (kind * heads + h) * HEAD_DIM
    return rows[:, first : first + HEAD_DIM]


def attention_kernel(meta_ref, raw_ref, place_ref, hidden_ref, norm_ref, extra_ref, *refs, **sizes):
    parts, outs = (refs[:2], refs[2:4]), refs[4:]
    block_ref, normed_ref, residual_ref, out_ref, joint_ref, mixed_ref, probs_ref = outs[:7]
    weight_ref, sems, out_sems = outs[7:]
    items, main_rows, all_rows = sizes["items"], sizes["main_rows"], sizes["all_rows"]
    step = pl.program_id(0)
    by_step = step_copies(parts, meta_ref[items + 1], weight_ref, sems)

    @pl.when(step == 0)
    def _():
        start_all(by_step)

        def chunk(first, size):
            rows = pl.ds(first, size)
            picked = dot(one_hot(place_ref[...], first, size), raw_ref[...], 1, 0)
            picked = jnp.where(hidden_ref[rows, :] > 0, extra_ref[2:3, :], picked)
            block_ref[rows, :] = picked
            residual_ref[rows, :] = picked
            normed_ref[rows, :] = norm_forward(picked, norm_ref[0:1, :], norm_ref[1:2, :]).astype(bf16)

        loop(items, lambda i: chunk(pl.multiple_of(i * ITEM_ROWS, 16), ITEM_ROWS))
        chunk(main_rows, all_rows - main_rows)

    wait_step(by_step, weight_ref, out_ref, out_sems, (0, 2))
    attend_heads(
        meta_ref, weight_ref.at[0, step], normed_ref, residual_ref, joint_ref, mixed_ref, probs_ref, **sizes
    )

    @pl.when(step == pl.num_programs(0) - 1)
    def _():
        wait_out(weight_ref, out_ref, out_sems, (0, 2))


def attention_end_kernel(meta_ref, normed_ref, block_ref, before_ref, valid_ref, norm_ref, *refs, **sizes):
    parts, outs = (refs[:2], refs[2:4]), refs[8:]
    residual_ref, feed_ref, square_ref, out_ref, joint_ref, mixed_ref, probs_ref = outs[:7]
    weight_ref, sems, out_sems = outs[7:]
    items, main_rows, all_rows = sizes["items"], sizes["main_rows"], sizes["all_rows"]
    step = pl.program_id(0)
    by_step = step_copies(parts, meta_ref[items + 1], weight_ref, sems)

    @pl.when(step == 0)
    def _():
        start_all(by_step)
        residual_ref[...] = before_ref[...]

    wait_step(by_step, weight_ref, out_ref, out_sems, (1, 3))
    attend_heads(
        meta_ref, weight_ref.at[0, step], normed_ref, residual_ref, joint_ref, mixed_ref, probs_ref, **sizes
    )

    @pl.when(step == pl.num_programs(0) - 1)
    def _():
        square_ref[...] = jnp.zeros_like(square_ref)

        def chunk(rows):
            residual = residual_ref[rows, :]
            feed_ref[rows, :] = norm_forward(residual, norm_ref[2:3, :], norm_ref[3:4, :]).astype(bf16)
            attended = (residual - block_ref[rows, :]) * valid_ref[rows, :]
            square_ref[...] += jnp.sum(attended * attended, axis=0, keepdims=True)

        loop(items, lambda i: chunk(rows_at(i, ITEM_ROWS)))
        chunk(pl.ds(main_rows, all_rows - main_rows))
        wait_out(weight_ref, out_ref, out_sems, (1, 3))


def attend_heads(
    meta_ref,
    weight_ref,
    normed_ref,
    residual_ref,
    joint_ref,
    mixed_ref,
    probs_ref,
    *,
    items,
    heads,
    main_rows,
    all_rows,
):
    width = heads * HEAD_DIM
    tail_rows = all_rows - main_rows

    def project(rows):
        joint = dot(normed_ref[rows, :], weight_ref[:, : 3 * width], 1, 0)
        joint_ref[0, rows, :width] = (joint[:, :width].astype(bf16).astype(f32) * HEAD_DIM**-0.5).astype(bf16)
        joint_ref[0, rows, width:] = joint[:, width:].astype(bf16)

    project(pl.ds(0, all_rows))

    key_row = lax.broadcasted_iota(jnp.int32, (ITEM_ROWS, 1), 0)
    blocks = [item_rows(joint_ref, (0,), items, i) for i in range(items)]
    masks = [
        (key_row < PATCHES)
        | ((key_row >= PATCH_STRIDE) & (key_row < PATCH_STRIDE + meta_ref[i]))
        for i in range(items)
    ]
    blocks.append(joint_ref[0, main_rows:, :])
    masks.append(lax.broadcasted_iota(jnp.int32, (tail_rows, 1), 0) < meta_ref[items])
    pairs = [(i, h) for i in range(items + 1) for h in range(heads)]
    weights, outs = attend(
        *[[head_columns(blocks[i], kind, heads, h) for i, h in pairs] for kind in range(3)],
        [masks[i] for i, _ in pairs],
    )
    for (i, h), weight in zip(pairs, weights):
        if i < items:
            probs_ref[0, i, h] = weight
    for i in range(items + 1):
        mixed = jnp.concatenate(outs[i * heads : (i + 1) * heads], axis=0).T.astype(bf16)
        if i == items:
            mixed_ref[0, main_rows:, :] = mixed
        else:
            patch_rows, text_rows = item_slices(items, i)
            mixed_ref[0, patch_rows, :] = mixed[:PATCH_STRIDE]
            mixed_ref[0, text_rows, :] = mixed[PATCH_STRIDE:]

    def add_output(rows):
        residual_ref[rows, :] += dot(mixed_ref[0, rows, :], weight_ref[:, 3 * width :], 1, 1)

    add_output(pl.ds(0, all_rows))


def attention_back_kernel(
    mine_ref,
    grad_attended_ref,
    joint_ref,
    mixed_ref,
    probs_ref,
    normed_ref,
    weight_ref,
    grad_weight_ref,
    grad_normed_ref,
    grad_mixed_ref,
    grad_joint_ref,
    **sizes,
):
    @pl.when(pl.program_id(0) == 0)
    def _():
        grad_normed_ref[...] = jnp.zeros_like(grad_normed_ref)

    heads_back(
        mine_ref,
        grad_attended_ref,
        joint_ref,
        mixed_ref,
        probs_ref,
        normed_ref,
        weight_ref,
        grad_weight_ref,
        grad_normed_ref,
        grad_mixed_ref,
        grad_joint_ref,
        **sizes,
    )


def attention_back_end_kernel(
    mine_ref,
    grad_attended_ref,
    joint_ref,
    mixed_ref,
    probs_ref,
    normed_ref,
    weight_ref,
    before_ref,
    grad_weight_ref,
    grad_normed_ref,
    grad_mixed_ref,
    grad_joint_ref,
    **sizes,
):
    @pl.when(pl.program_id(0) == 0)
    def _():
        grad_normed_ref[...] = before_ref[...]

    heads_back(
        mine_ref,
        grad_attended_ref,
        joint_ref,
        mixed_ref,
        probs_ref,
        normed_ref,
        weight_ref,
        grad_weight_ref,
        grad_normed_ref,
        grad_mixed_ref,
        grad_joint_ref,
        **sizes,
    )


def input_grad_kernel(
    grad_normed_ref,
    grad_residual_ref,
    block_ref,
    hidden_ref,
    place_ref,
    norm_ref,
    *refs,
):
    small_refs, (grad_raw_ref, small_ref, grad_block_ref) = refs[:-3], refs[-3:]
    step = pl.program_id(0)

    @pl.when(step == 0)
    def _():
        small_ref[...] = jnp.zeros_like(small_ref)
        first = 3
        for ref in small_refs:
            small_ref[first : first + ref.shape[0], :] = ref[...]
            first += ref.shape[0]

    grad, gain, shift = norm_backward(block_ref[...], norm_ref[0:1, :], grad_normed_ref[...])
    small_ref[0:1, :] += gain
    small_ref[1:2, :] += shift
    grad = grad + grad_residual_ref[...]
    hidden = hidden_ref[...] > 0
    small_ref[2:3, :] += jnp.sum(jnp.where(hidden, grad, 0.0), axis=0, keepdims=True)
    grad_block_ref[rows_at(step, ITEM_ROWS), :] = jnp.where(hidden, 0.0, grad).astype(bf16)

    @pl.when(step == pl.num_programs(0) - 1)
    def _():
        unplace(place_ref, grad_block_ref, grad_raw_ref, grad_block_ref.shape[0])


def heads_back(
    mine_ref,
    grad_attended_ref,
    joint_ref,
    mixed_ref,
    probs_ref,
    normed_ref,
    weight_ref,
    grad_weight_ref,
    grad_normed_ref,
    grad_mixed_ref,
    grad_joint_ref,
    *,
    items,
    heads,
):
    width = heads * HEAD_DIM
    half = HEAD_DIM**-0.5

    grad_mixed_ref[...] = dot(grad_attended_ref[...], weight_ref[0, :, 3 * width :], 1, 0).astype(bf16)

    blocks = [item_rows(joint_ref, (0,), items, i) for i in range(items)]
    outs = [item_rows(grad_mixed_ref, (), items, i) for i in range(items)]
    products = [
        (outs[i].astype(f32) * item_rows(mixed_ref, (0,), items, i).astype(f32)).T for i in range(items)
    ]
    pairs = [(i, h) for i in range(items) for h in range(heads)]
    queries, keys, values = [
        [head_columns(blocks[i], kind, heads, h) for i, h in pairs] for kind in range(3)
    ]
    grad_outs = [head_columns(outs[i], 0, heads, h) for i, h in pairs]
    weights = [probs_ref[0, i, h] for i, h in pairs]
    grad_probs = [dot(value, grad_out, 1, 1) for value, grad_out in zip(values, grad_outs)]
    means = [
        jnp.sum(products[i][h * HEAD_DIM : (h + 1) * HEAD_DIM], axis=0, keepdims=True) for i, h in pairs
    ]
    grad_scores = [
        (weight.astype(f32) * (grad - mean)).astype(bf16)
        for weight, grad, mean in zip(weights, grad_probs, means)
    ]
    grad_values = [dot(weight, grad_out, 1, 0).astype(bf16) for weight, grad_out in zip(weights, grad_outs)]
    grad_keys = [dot(score, query, 1, 0).astype(bf16) for score, query in zip(grad_scores, queries)]
    grad_queries = [dot(key, score, 0, 0) * half for key, score in zip(keys, grad_scores)]
    for i in range(items):
        own = slice(i * heads, (i + 1) * heads)
        grad_query = jnp.concatenate(grad_queries[own], axis=0).T.astype(bf16)
        grad_joint = jnp.concatenate([grad_query] + grad_keys[own] + grad_values[own], axis=1)
        patch_rows, text_rows = item_slices(items, i)
        grad_joint_ref[patch_rows, :] = grad_joint[:PATCH_STRIDE]
        grad_joint_ref[text_rows, :] = grad_joint[PATCH_STRIDE:]

    model_width = weight_ref.shape[1]
    for first in range(0, model_width, 384):
        cols = slice(first, first + 384)
        grad_weight = jnp.concatenate(
            [
                dot(normed_ref[:, cols], grad_joint_ref[...], 0, 0),
                dot(grad_attended_ref[:, cols], mixed_ref[0], 0, 0),
            ],
            axis=1,
        )
        store_grad(grad_weight_ref, mine_ref[0], 0, first, 384, grad_weight)

    grad_normed_ref[...] += dot(grad_joint_ref[...], weight_ref[0, :, : 3 * width], 1, 1)


def unplace(place_ref, source_ref, raw_ref, source_rows):
    source = source_ref[...].astype(bf16)
    raw_rows = raw_ref.shape[0]
    size = 240 if raw_rows % 240 == 0 else raw_rows

    def chunk(i):
        rows = rows_at(i, size)
        place = lax.broadcasted_iota(jnp.int32, (size, source_rows), 1)
        pick = (place == place_ref[rows, :]).astype(bf16)
        raw_ref[rows, :] = dot(pick, source, 1, 0).astype(bf16)

    loop(raw_rows // size, chunk)


def lift_kernel(mine_ref, feed_ref, *refs, vision_rows, all_rows):
    pieces, (acted_ref, slope_ref, out_ref, weight_ref, sems, out_sems) = refs[:10], refs[10:]
    by_step = step_copies(step_parts(pieces), mine_ref[0], weight_ref, sems)

    @pl.when(pl.program_id(0) == 0)
    def _():
        start_all(by_step)

    wait_step(by_step, weight_ref, out_ref, out_sems, (0, 1, 2, 3))

    def piece(rows, expert):
        lifted = dot(feed_ref[rows, :], weight_ref[expert, pl.program_id(0)], 1, 0)
        cumulative = 0.5 * (1.0 + lax.erf(lifted * (0.5**0.5)))
        density = jnp.exp(-0.5 * lifted * lifted) * ((2.0 * jnp.pi) ** -0.5)
        acted_ref[0, rows, :] = (lifted * cumulative).astype(bf16)
        slope_ref[0, rows, :] = (cumulative + lifted * density).astype(bf16)

    loop(2, lambda i: piece(rows_at(i, vision_rows // 2), 0))
    piece(pl.ds(vision_rows, all_rows - vision_rows), 1)

    @pl.when(pl.program_id(0) == pl.num_programs(0) - 1)
    def _():
        wait_out(weight_ref, out_ref, out_sems, (0, 1, 2, 3))


def place_grad_kernel(raw_ref, place_ref, grad_ref, grad_bias_ref, *, vision_rows):
    def chunk(i):
        rows = rows_at(i, ITEM_ROWS)
        pick = one_hot(place_ref[...], i * ITEM_ROWS, ITEM_ROWS)
        grad_ref[rows, :] = dot(pick, raw_ref[...], 1, 0).astype(bf16)

    loop(grad_ref.shape[0] // ITEM_ROWS, chunk)
    grad_bias_ref[0:1, :] = jnp.sum(grad_ref[:vision_rows, :].astype(f32), axis=0, keepdims=True)
    grad_bias_ref[1:2, :] = jnp.sum(grad_ref[vision_rows:, :].astype(f32), axis=0, keepdims=True)


def expert_weight_grad(grad_weight_ref, mine, left_ref, right, vision_rows):
    rows_total, width = left_ref.shape
    for expert, rows in ((0, slice(0, vision_rows)), (1, slice(vision_rows, rows_total))):
        for first in range(0, width, 384):
            grad_weight = dot(left_ref[rows, first : first + 384], right(rows), 0, 0)
            store_grad(grad_weight_ref, mine, expert, first, 384, grad_weight)


def drop_weight_kernel(mine_ref, grad_ref, acted_ref, grad_weight_ref, *, vision_rows):
    expert_weight_grad(
        grad_weight_ref, mine_ref[0], grad_ref, lambda rows: acted_ref[0, rows, :], vision_rows
    )


def drop_kernel(
    acted_ref,
    residual_ref,
    valid_ref,
    place_ref,
    extra_ref,
    weight_ref,
    raw_ref,
    square_ref,
    total_ref,
    *,
    vision_rows,
    all_rows,
):
    step = pl.program_id(0)
    text = all_rows - vision_rows

    @pl.when(step == 0)
    def _():
        total_ref[:vision_rows, :] = jnp.broadcast_to(extra_ref[0:1, :], (vision_rows, total_ref.shape[1]))
        total_ref[vision_rows:, :] = jnp.broadcast_to(extra_ref[1:2, :], (text, total_ref.shape[1]))

    def piece(rows, expert):
        total_ref[rows, :] += dot(acted_ref[0, rows, :], weight_ref[expert, 0], 1, 1)

    piece(pl.ds(0, vision_rows), 0)
    piece(pl.ds(vision_rows, text), 1)

    @pl.when(step == pl.num_programs(0) - 1)
    def _():
        square_ref[...] = jnp.zeros_like(square_ref)

        def finish(rows, expert):
            fed = total_ref[rows, :]
            out = residual_ref[rows, :] + fed
            valid = valid_ref[rows, :]
            square_ref[0:1, :] += jnp.sum(valid * out * out, axis=0, keepdims=True)
            square_ref[1:2, :] += jnp.sum(valid * fed * fed, axis=0, keepdims=True)
            total_ref[rows, :] = out

        loop(vision_rows // PATCH_STRIDE, lambda i: finish(rows_at(i, PATCH_STRIDE), 0))
        loop(3, lambda i: finish(pl.ds(pl.multiple_of(vision_rows + i * (text // 3), 16), text // 3), 1))
        unplace(place_ref, total_ref, raw_ref, all_rows)


def expert_back_step(
    mine_ref, grad_ref, slope_ref, feed_ref, lift_ref, drop_ref, grad_weight_ref, total_ref, lifted_ref, vision_rows
):
    step = pl.program_id(0)

    def piece(rows, expert):
        grad_acted = dot(grad_ref[rows, :], drop_ref[expert, step], 1, 0)
        grad_lifted = (grad_acted * slope_ref[0, rows, :].astype(f32)).astype(bf16)
        lifted_ref[rows, :] = grad_lifted
        total_ref[rows, :] += dot(grad_lifted, lift_ref[expert, 0], 1, 1)

    piece(pl.ds(0, vision_rows), 0)
    piece(pl.ds(vision_rows, grad_ref.shape[0] - vision_rows), 1)
    expert_weight_grad(
        grad_weight_ref, mine_ref[0], feed_ref, lambda rows: lifted_ref[rows, :], vision_rows
    )


def expert_back_kernel(mine_ref, grad_ref, slope_ref, feed_ref, lift_ref, *refs, vision_rows):
    pieces, (grad_weight_ref, out_ref, total_ref) = refs[:5], refs[5:8]
    lifted_ref, drop_ref, sems, out_sems = refs[8:]
    by_step = step_copies(step_parts(pieces), mine_ref[0], drop_ref, sems)

    @pl.when(pl.program_id(0) == 0)
    def _():
        start_all(by_step)
        total_ref[...] = jnp.zeros_like(total_ref)

    wait_step(by_step, drop_ref, out_ref, out_sems, (0, 1))
    expert_back_step(
        mine_ref, grad_ref, slope_ref, feed_ref, lift_ref, drop_ref, grad_weight_ref, total_ref, lifted_ref, vision_rows
    )

    @pl.when(pl.program_id(0) == pl.num_programs(0) - 1)
    def _():
        wait_out(drop_ref, out_ref, out_sems, (0, 1))


def expert_back_end_kernel(mine_ref, grad_ref, slope_ref, feed_ref, lift_ref, *refs, vision_rows):
    pieces, (_, before_ref, residual_ref, norm_ref) = refs[:5], refs[5:9]
    grad_weight_ref, out_ref, grad_residual_ref, grad_attended_ref, grad_norm_ref = refs[9:14]
    lifted_ref, drop_ref, sems, out_sems = refs[14:]
    by_step = step_copies(step_parts(pieces), mine_ref[0], drop_ref, sems)

    @pl.when(pl.program_id(0) == 0)
    def _():
        start_all(by_step)
        grad_residual_ref[...] = before_ref[...]

    wait_step(by_step, drop_ref, out_ref, out_sems, (2, 3))
    expert_back_step(
        mine_ref,
        grad_ref,
        slope_ref,
        feed_ref,
        lift_ref,
        drop_ref,
        grad_weight_ref,
        grad_residual_ref,
        lifted_ref,
        vision_rows,
    )

    @pl.when(pl.program_id(0) == pl.num_programs(0) - 1)
    def _():
        grad_norm_ref[...] = jnp.zeros_like(grad_norm_ref)

        def chunk(i):
            rows = rows_at(i, ITEM_ROWS)
            grad, gain, shift = norm_backward(
                residual_ref[rows, :], norm_ref[2:3, :], grad_residual_ref[rows, :]
            )
            grad_norm_ref[0:1, :] += gain
            grad_norm_ref[1:2, :] += shift
            grad = grad + grad_ref[rows, :].astype(f32)
            grad_residual_ref[rows, :] = grad
            grad_attended_ref[rows, :] = grad.astype(bf16)

        loop(grad_ref.shape[0] // ITEM_ROWS, chunk)
        wait_out(drop_ref, out_ref, out_sems, (2, 3))


def whole(*shape):
    return pl.BlockSpec(shape, lambda *_: (0,) * len(shape))


def stepped(*shape, first=0):
    return pl.BlockSpec(shape, lambda i, *_: (i + first,) + (0,) * (len(shape) - 1))


def stepped_pair(*shape, first=0):
    return pl.BlockSpec(shape, lambda i, *_: (0, i + first) + (0,) * (len(shape) - 2))


def every_other(*shape, first=0):
    return pl.BlockSpec(shape, lambda i, *_: (2 * i + first,) + (0,) * (len(shape) - 1))


def anywhere(values):
    return (values, pl.BlockSpec(memory_space=pl.ANY))


def call(kernel, name, steps, ins, outs, scratch, microseconds, scalars=(), aliases=None):
    return pl.pallas_call(
        kernel,
        name=name,
        grid_spec=pltpu.PrefetchScalarGridSpec(
            num_scalar_prefetch=len(scalars),
            grid=(steps,),
            in_specs=[block for _, block in ins],
            out_specs=[block for _, _, block in outs],
            scratch_shapes=scratch,
        ),
        out_shape=[jax.ShapeDtypeStruct(shape, kind) for shape, kind, _ in outs],
        input_output_aliases=aliases or {},
        compiler_params=pltpu.CompilerParams(
            dimension_semantics=("arbitrary",), vmem_limit_bytes=VMEM_LIMIT
        ),
        cost_estimate=pl.CostEstimate(
            flops=int(microseconds * 1e9), bytes_accessed=int(microseconds * 1e6), transcendentals=0
        ),
    )(*scalars, *[array for array, _ in ins])


def body(
    tokens,
    cotangent,
    text_lengths,
    modality,
    masked_positions,
    joint_weight,
    joint_first,
    joint_second,
    output_weight,
    output_first,
    output_second,
    lift_weight,
    lift_first,
    lift_second,
    drop_weight,
    drop_first,
    drop_second,
    norm_params,
    norm_first,
    norm_second,
    extra_params,
    extra_first,
    extra_second,
):
    micro_count, shard_rows, model_width = tokens.shape
    block_rows = modality.shape[1]
    parts = block_rows // shard_rows
    assert micro_count == parts
    items = text_lengths.shape[1]
    width = joint_weight.shape[2]
    heads = width // HEAD_DIM
    hidden_width = lift_weight.shape[2]
    shard = joint_weight.shape[1]
    vision_rows = items * PATCH_STRIDE
    main_rows = items * ITEM_ROWS
    tail = block_rows - items * PATCHES - TEXT_MAX - (items - 1)
    tail = (tail + 47) // 48 * 48
    all_rows = main_rows + tail
    assert 4 * width == model_width and hidden_width == model_width

    shard_attend = jnp.concatenate(
        [joint_weight[0], joint_weight[1], joint_weight[2], output_weight.T], axis=1
    ).astype(bf16)[None]
    shard_lift = lift_weight.astype(bf16)
    shard_drop = jnp.swapaxes(drop_weight, 1, 2).astype(bf16)

    groups = lax.axis_size("dp")
    cube = groups == 8
    piece = model_width // 8
    if cube:
        mine = jnp.stack([lax.axis_index("dp"), lax.axis_index("mp")]).astype(jnp.int32)
    else:
        mine = jnp.zeros((2,), jnp.int32)

    def together(*values):
        return lax.optimization_barrier(values)

    def swap(values, axis, bit):
        size = lax.axis_size(axis)
        return lax.ppermute(values, axis, [(i, i ^ bit) for i in range(size)])

    def exchange(values):
        return lax.all_to_all(values, "mp", split_axis=0, concat_axis=1, tiled=True)[0]

    def give_back(values):
        return lax.all_to_all(
            values.reshape(parts, shard_rows, model_width), "mp", split_axis=0, concat_axis=0, tiled=True
        )

    def gather(values):
        whole_values = lax.all_gather(values, ("mp", "dp"), axis=1, tiled=True)
        return whole_values.reshape(-1, parts, model_width, values.shape[2])

    def gather_pieces(values):
        whole_values = jnp.swapaxes(gather(values).reshape(-1, parts, 4, 2, piece, model_width), 0, 3)
        pieces = []
        for core in range(2):
            low, high = whole_values[:, core], whole_values[:, 2 + core]
            pieces += [low[0], low[1], high[0], high[1, :2], high[1, 2:]]
        return pieces

    def line_parts(values):
        return (values,) + tuple(swap(values, "dp", bit) for bit in (2, 4, 6))

    def gather_line(values):
        return jnp.stack(line_parts(values))

    def gather_plane(line):
        return swap(line, "dp", 1), swap(line, "mp", 2)

    def gather_corner(along_x, along_y):
        return swap(along_x[:2], "mp", 2), swap(along_y[2:], "dp", 1)

    def over_cores(*pieces):
        return tuple(swap(part, "mp", 1) for part in pieces)

    def add(*terms):
        total = terms[0].astype(f32)
        for term in terms[1:]:
            total = total + term.astype(f32)
        return total

    def scatter(keep, send):
        shape = (2, 2, 4) + keep.shape[2:]
        both = jnp.stack([keep.reshape(shape), send.reshape(shape)], axis=1)
        both = jnp.transpose(both, (4, 0, 1, 3, 2, 5, 6))
        return reduce(both.reshape(both.shape[0], parts * model_width, shape[-1]))

    def reduce(values):
        values = lax.psum_scatter(values, ("mp", "dp"), scatter_dimension=1, tiled=True)
        return values.astype(f32)

    def quarters(keep, received, *others):
        keep, received, others = together(keep, received, others)
        shape = (2, 2, 4) + keep.shape[2:]
        keep, received = keep.reshape(shape), received.reshape(shape)
        return (lambda y, x: add(keep[y, x], received[y, x])), others

    def scatter_corner(keep, received):
        quarter, _ = quarters(keep, received)
        return quarter(1, 1).astype(bf16)

    def scatter_plane(keep, received, from_x, from_y):
        quarter, (from_x, from_y) = quarters(keep, received, from_x, from_y)
        part_x, part_y = quarter(0, 1), quarter(1, 0)
        part_x = jnp.concatenate([part_x[:2], add(part_x[2:], from_y)]).astype(bf16)
        part_y = jnp.concatenate([add(part_y[:2], from_x), part_y[2:]]).astype(bf16)
        return part_x, part_y

    def scatter_line(keep, received, from_x, from_y):
        quarter, (from_x, from_y) = quarters(keep, received, from_x, from_y)
        return add(quarter(0, 0), from_x, from_y).astype(bf16)

    def send_corner(corner):
        return swap(corner[:2], "dp", 1), swap(corner[2:], "mp", 2)

    def send_plane(part_x, part_y):
        return swap(part_x, "dp", 1), swap(part_y, "mp", 2)

    def send_line(line):
        return tuple(swap(line[i], "dp", 2 * i) for i in (1, 2, 3))

    micro = lax.axis_index("mp")
    lengths = lax.dynamic_index_in_dim(text_lengths, micro, 0, keepdims=False)
    masked = lax.dynamic_index_in_dim(masked_positions, micro, 0, keepdims=False)
    item_ids = jnp.arange(items, dtype=jnp.int32)
    sizes = PATCHES + lengths
    ends = jnp.sum(jnp.where(item_ids[:, None] <= item_ids[None, :], sizes[:, None], 0), axis=0)
    used = jnp.sum(sizes)

    def place_of(row):
        segment = jnp.sum((row[..., None] >= ends).astype(jnp.int32), axis=-1)
        start = jnp.sum(jnp.where(row[..., None] >= ends, sizes, 0), axis=-1)
        inside = row - start
        return jnp.where(
            segment == items,
            main_rows + inside,
            jnp.where(
                inside < PATCHES,
                PATCH_STRIDE * segment + inside,
                vision_rows + TEXT_STRIDE * segment + inside - PATCHES,
            ),
        )

    places = together(place_of(jnp.arange(block_rows, dtype=jnp.int32)))[0]
    place_row, place_column = places[None, :], places[:, None]
    targets = (vision_rows + TEXT_STRIDE * item_ids[:, None] + masked).reshape(-1)
    spots = jnp.arange(all_rows, dtype=jnp.int32)
    hidden = jnp.any(spots[:, None] == targets[None, :], axis=1).astype(jnp.int32)[:, None]
    text_spot = spots - vision_rows
    text_item = text_spot // TEXT_STRIDE
    text_end = jnp.sum(jnp.where(text_item[:, None] == item_ids, lengths, 0), axis=1)
    valid = jnp.where(
        text_spot < 0, spots % PATCH_STRIDE < PATCHES, text_spot - text_item * TEXT_STRIDE < text_end
    )
    valid = valid.astype(f32)[:, None]
    meta = jnp.concatenate([lengths, (block_rows - used)[None], mine[:1]])

    def rows_of(count, kind):
        return ((count, model_width), kind, whole(count, model_width))

    def plain(values):
        return (values, whole(*values.shape))

    def heads_out(first):
        shapes = [
            (parts, all_rows, 3 * width),
            (parts, all_rows, width),
            (parts, items, heads, ITEM_ROWS, ITEM_ROWS),
        ]
        return [(shape, bf16, every_other(1, *shape[1:], first=first)) for shape in shapes]

    def whole_weight(count):
        return ((count, parts, model_width, model_width), bf16, pl.BlockSpec(memory_space=pl.ANY))

    def weight_scratch(count, steps):
        return [
            pltpu.VMEM((count, steps, model_width, model_width), bf16),
            pltpu.SemaphoreType.DMA((steps, 8)),
            pltpu.SemaphoreType.DMA((steps,)),
        ]

    def part_weight(values, first, count=2):
        return (values, stepped_pair(count, 1, *values.shape[2:], first=first))

    def grad_out(count):
        shape = (2, 8, count, piece, model_width)
        return (shape, bf16, stepped(1, *shape[1:]))

    head_sizes = dict(items=items, heads=heads)
    row_sizes = dict(main_rows=main_rows, all_rows=all_rows)

    def attention(raw, pieces):
        return call(
            functools.partial(attention_kernel, **head_sizes, **row_sizes),
            "attention",
            2,
            [plain(raw), plain(place_row), plain(hidden), plain(norm_params), plain(extra_params)]
            + [anywhere(values) for values in pieces],
            [rows_of(all_rows, f32), rows_of(all_rows, bf16), rows_of(all_rows, f32), whole_weight(1)]
            + heads_out(0),
            weight_scratch(1, 2),
            ATTENTION_US,
            (meta,),
        )

    def attention_end(normed, block_input, residual, pieces, made):
        return call(
            functools.partial(attention_end_kernel, **head_sizes, **row_sizes),
            "attention_end",
            2,
            [plain(normed), plain(block_input), plain(residual), plain(valid), plain(norm_params)]
            + [anywhere(values) for values in pieces]
            + [anywhere(values) for values in made],
            [rows_of(all_rows, f32), rows_of(all_rows, bf16), rows_of(1, f32), whole_weight(1)]
            + heads_out(1),
            weight_scratch(1, 2),
            ATTENTION_US,
            (meta,),
            {10 + i: 3 + i for i in range(4)},
        )

    def lift(feed_input, pieces):
        shape = (parts, all_rows, hidden_width)
        return call(
            functools.partial(lift_kernel, vision_rows=vision_rows, all_rows=all_rows),
            "lift",
            parts,
            [plain(feed_input)] + [anywhere(values) for values in pieces],
            [(shape, bf16, stepped(1, *shape[1:]))] * 2 + [whole_weight(2)],
            weight_scratch(2, parts),
            LIFT_US,
            (mine,),
        )

    def place_grad(raw):
        return call(
            functools.partial(place_grad_kernel, vision_rows=vision_rows),
            "place_grad",
            1,
            [plain(raw), plain(place_row)],
            [rows_of(main_rows, bf16), rows_of(2, f32)],
            [],
            5,
        )

    def drop_weight_grad(grad_rows, acted, first):
        return call(
            functools.partial(drop_weight_kernel, vision_rows=vision_rows),
            "drop_weight_grad",
            2,
            [plain(grad_rows), (acted, stepped(1, main_rows, hidden_width, first=first))],
            [grad_out(2)],
            [],
            DROP_WEIGHT_US,
            (mine,),
        )[0]

    def expert_ins(grad_rows, slope, feed_input, lift_weights, pieces, first):
        return [
            plain(grad_rows),
            (slope, stepped(1, main_rows, hidden_width, first=first)),
            (feed_input, whole(main_rows, model_width)),
            part_weight(lift_weights, first),
        ] + [anywhere(values) for values in pieces]

    drop_out = whole_weight(2)
    expert_scratch = [pltpu.VMEM((main_rows, hidden_width), bf16)] + weight_scratch(2, 2)

    def expert_back(pieces, *args):
        return call(
            functools.partial(expert_back_kernel, vision_rows=vision_rows),
            "expert_back",
            2,
            expert_ins(*args, pieces[5:], 0),
            [grad_out(2), drop_out, rows_of(main_rows, f32)],
            expert_scratch,
            EXPERT_BACK_US,
            (mine,),
        )

    def expert_back_end(made, before, residual, pieces, *args):
        return call(
            functools.partial(expert_back_end_kernel, vision_rows=vision_rows),
            "expert_back_end",
            2,
            expert_ins(*args, pieces[:5], 2)
            + [anywhere(made), plain(before), (residual, whole(main_rows, model_width))]
            + [plain(norm_params)],
            [grad_out(2), drop_out, rows_of(main_rows, f32), rows_of(main_rows, bf16)]
            + [rows_of(2, f32)],
            expert_scratch,
            EXPERT_BACK_US,
            (mine,),
            {10: 1},
        )

    def heads_ins(grad_attended, normed, weights, joint_rows, mixed, probs, first):
        return [
            plain(grad_attended),
            (joint_rows, stepped(1, main_rows, 3 * width, first=first)),
            (mixed, stepped(1, main_rows, width, first=first)),
            (probs, stepped(1, *probs.shape[1:], first=first)),
            (normed, whole(main_rows, model_width)),
            (weights, stepped(1, model_width, model_width, first=first)),
        ]

    heads_scratch = [
        pltpu.VMEM((main_rows, width), bf16),
        pltpu.VMEM((main_rows, 3 * width), bf16),
    ]

    def attention_back(*args):
        return call(
            functools.partial(attention_back_kernel, **head_sizes),
            "attention_back",
            2,
            heads_ins(*args, 0),
            [grad_out(1), rows_of(main_rows, f32)],
            heads_scratch,
            ATTENTION_BACK_US,
            (mine,),
        )

    def attention_back_end(before, *args):
        return call(
            functools.partial(attention_back_end_kernel, **head_sizes),
            "attention_back_end",
            2,
            heads_ins(*args, 2) + [plain(before)],
            [grad_out(1), rows_of(main_rows, f32)],
            heads_scratch,
            ATTENTION_BACK_US,
            (mine,),
        )

    def finish_input_grad(grad_normed, grad_residual, block_input, *sums):
        return call(
            input_grad_kernel,
            "input_grad",
            main_rows // ITEM_ROWS,
            [
                (grad_normed, stepped(ITEM_ROWS, model_width)),
                (grad_residual, stepped(ITEM_ROWS, model_width)),
                (block_input, stepped(ITEM_ROWS, model_width)),
                (hidden, stepped(ITEM_ROWS, 1)),
                plain(place_column),
                plain(norm_params),
            ]
            + [plain(values) for values in sums],
            [rows_of(block_rows, bf16), rows_of(16, f32)],
            [pltpu.VMEM((main_rows, model_width), bf16)],
            9,
        )

    def drop(acted, residual, weights):
        return call(
            functools.partial(drop_kernel, vision_rows=vision_rows, all_rows=all_rows),
            "drop",
            parts,
            [(acted, stepped(1, all_rows, hidden_width)), plain(residual), plain(valid)]
            + [plain(place_column), plain(extra_params)]
            + [part_weight(weights, 0)],
            [rows_of(block_rows, bf16), rows_of(2, f32)],
            [pltpu.VMEM((all_rows, model_width), f32)],
            DROP_US,
        )

    used_row = jnp.where(jnp.arange(model_width)[None, :] == 0, used.astype(f32), 0.0)
    tables = (place_row, place_column, hidden, valid, meta)
    raw_tokens = exchange(tokens)
    if cube:
        line = gather_line(shard_attend)
        even, high = gather_plane(line)
        even, high, raw_tokens, shard_lift, cotangent, tables = together(
            even, high, raw_tokens, shard_lift, cotangent, tables
        )
        place_row, place_column, hidden, valid, meta = tables
        corner = swap(high, "dp", 1)
        line_lift = line_parts(shard_lift)
        raw_grad = exchange(cotangent.astype(bf16))
        early = over_cores(line, even) + (line, even)
    else:
        pieces = gather_pieces(shard_attend)
        early = [pieces[i] for i in (5, 6, 0, 1)]
        late = [pieces[7], jnp.concatenate(pieces[8:10]), pieces[2], jnp.concatenate(pieces[3:5])]
        raw_grad = exchange(cotangent.astype(bf16))

    block_input, normed, residual, *made = attention(raw_tokens, early)
    if cube:
        corner, line_lift, raw_grad, residual = together(corner, line_lift, raw_grad, residual)
        late = over_cores(high, corner) + (high, corner)
        line_lift, shard_drop = together(jnp.stack(line_lift), shard_drop)
        plane_lift = gather_plane(line_lift)
        line_drop = line_parts(shard_drop)
    residual, feed_input, attended_square, *made = attention_end(normed, block_input, residual, late, made)
    made[0] = made[0][0]
    if cube:
        plane_lift, line_drop, raw_grad, feed_input = together(plane_lift, line_drop, raw_grad, feed_input)
        corner_lift = gather_corner(*plane_lift)
        lift_others = over_cores(line_lift, *plane_lift)
    grad_rows, grad_bias = place_grad(raw_grad)
    if cube:
        corner_lift, lift_others, line_drop, grad_rows = together(
            corner_lift, lift_others, line_drop, grad_rows
        )
        lift_pieces = (line_lift,) + plane_lift + corner_lift
        lift_pieces += lift_others + over_cores(*corner_lift)
        line_drop = jnp.stack(line_drop)
        plane_drop = gather_plane(line_drop)
    else:
        lift_pieces = gather_pieces(shard_lift)
    acted, slope, lift_all = lift(feed_input, lift_pieces)
    if cube:
        plane_drop, acted = together(plane_drop, acted)
        corner_drop = gather_corner(*plane_drop)
        drop_others = over_cores(line_drop, *plane_drop)
    drop_send = drop_weight_grad(grad_rows, acted, 0)
    if cube:
        corner_drop, drop_others, drop_send, acted = together(corner_drop, drop_others, drop_send, acted)
        drop_received = swap(drop_send, "mp", 1)
        drop_pieces = (line_drop,) + plane_drop + corner_drop
        drop_pieces += drop_others + over_cores(*corner_drop)
    drop_keep = drop_weight_grad(grad_rows, acted, 2)
    if cube:
        drop_pieces, drop_received, drop_keep = together(drop_pieces, drop_received, drop_keep)
        corner, grad_rows = together(scatter_corner(drop_keep, drop_received), grad_rows)
        from_corner = send_corner(corner)
    else:
        drop_pieces = gather_pieces(shard_drop)
        drop_grad = scatter(drop_keep, drop_send)

    lift_send, drop_all, grad_feed = expert_back(drop_pieces, grad_rows, slope, feed_input, lift_all)
    if cube:
        from_corner, grad_feed = together(from_corner, grad_feed)
        plane = scatter_plane(drop_keep, drop_received, *from_corner)
        plane, lift_send, grad_feed = together(plane, lift_send, grad_feed)
        from_plane = send_plane(*plane)
        lift_received = swap(lift_send, "mp", 1)
    lift_keep, drop_all, grad_residual, grad_attended, grad_norm_second = expert_back_end(
        drop_all, grad_feed, residual, drop_pieces, grad_rows, slope, feed_input, lift_all
    )
    if cube:
        lift_received, from_plane, grad_attended = together(lift_received, from_plane, grad_attended)
        corner = scatter_corner(lift_keep, lift_received)
        drop_line = scatter_line(drop_keep, drop_received, *from_plane)
        corner, drop_line, acted = together(corner, drop_line, acted)
        from_corner = send_corner(corner)
        from_drop_line = send_line(drop_line)
    else:
        lift_grad = scatter(lift_keep, lift_send)
    raw_out, squares = drop(acted, residual, drop_all)
    if cube:
        from_corner, raw_out = together(from_corner, raw_out)
        plane = scatter_plane(lift_keep, lift_received, *from_corner)
        from_drop_line, plane, grad_attended = together(from_drop_line, plane, grad_attended)
        from_plane = send_plane(*plane)

    attend_send, grad_normed = attention_back(grad_attended, normed, *made)
    if cube:
        attend_received = swap(attend_send, "mp", 1)
        from_plane, raw_out, grad_normed = together(from_plane, raw_out, grad_normed)
        lift_line = scatter_line(lift_keep, lift_received, *from_plane)
        lift_line, grad_normed = together(lift_line, grad_normed)
        from_lift_line = send_line(lift_line)
    block_output = give_back(raw_out)
    attend_keep, grad_normed = attention_back_end(grad_normed, grad_attended, normed, *made)
    if cube:
        attend_received, from_lift_line, block_output, attend_keep = together(
            attend_received, from_lift_line, block_output, attend_keep
        )
        corner = scatter_corner(attend_keep, attend_received)
        corner, grad_normed = together(corner, grad_normed)
        from_corner = send_corner(corner)
    grad_raw, small = finish_input_grad(
        grad_normed,
        grad_residual,
        block_input,
        *(grad_norm_second, grad_bias, squares, attended_square, used_row),
    )
    if cube:
        from_corner, small, grad_raw = together(from_corner, small, grad_raw)
        plane = scatter_plane(attend_keep, attend_received, *from_corner)
        plane, small, grad_raw = together(plane, small, grad_raw)
        from_plane = send_plane(*plane)
        for axis, bit in (("mp", 1), ("dp", 1)):
            small = small + swap(small, axis, bit)
        line = scatter_line(attend_keep, attend_received, *from_plane)
        line, small, grad_raw, drop_line, lift_line, block_output = together(
            line, small, grad_raw, drop_line, lift_line, block_output
        )
        attend_grad = add(line[0], *send_line(line))[0]
        drop_grad = add(drop_line[0], *from_drop_line)
        lift_grad = add(lift_line[0], *from_lift_line)
    else:
        attend_grad = scatter(attend_keep, attend_send)[0]
    input_grad = give_back(grad_raw).astype(f32)
    block_output = block_output.astype(f32)

    if cube:
        for axis, bit in (("mp", 2), ("dp", 2), ("dp", 4)):
            small = small + swap(small, axis, bit)
    else:
        small = lax.psum(small, ("dp", "mp"))
    norm_total = jnp.concatenate([small[0:2], small[3:5]])
    extra_total = jnp.concatenate([small[5:7], small[2:3]])
    sums = jnp.sum(small[7:11], axis=1)
    rms_values = jnp.sqrt(jnp.stack([sums[0], sums[2], sums[1]]) / (sums[3] * model_width))

    joint_grad = jnp.stack([attend_grad[:, k * width : (k + 1) * width] for k in range(3)])
    output_grad = attend_grad[:, 3 * width :].T
    drop_grad = jnp.swapaxes(drop_grad, 1, 2)
    results = [block_output, input_grad, rms_values]
    results += adamw(joint_weight, joint_first, joint_second, joint_grad, matrix_rate, weight_decay)
    results += adamw(output_weight, output_first, output_second, output_grad, matrix_rate, weight_decay)
    results += adamw(lift_weight, lift_first, lift_second, lift_grad, matrix_rate, weight_decay)
    results += adamw(drop_weight, drop_first, drop_second, drop_grad, matrix_rate, weight_decay)
    results += adamw(norm_params, norm_first, norm_second, norm_total, vector_rate, 0.0)
    results += adamw(extra_params, extra_first, extra_second, extra_total, vector_rate, 0.0)
    return tuple(results)


def solution(mesh):
    rows = P(None, ("dp", "mp"), None)
    joint, output, lift, drop = (
        P(None, "dp", "mp"),
        P("mp", "dp"),
        P(None, "dp", "mp"),
        P(None, "mp", "dp"),
    )
    return jax.shard_map(
        body,
        mesh=mesh,
        in_specs=(rows, rows, P(None, "dp"), P(None, "dp"), P(None, "dp", None))
        + (joint,) * 3
        + (output,) * 3
        + (lift,) * 3
        + (drop,) * 3
        + (P(),) * 6,
        out_specs=(rows, rows, P())
        + (joint,) * 4
        + (output,) * 4
        + (lift,) * 4
        + (drop,) * 4
        + (P(),) * 8,
        check_vma=False,
    )
```

```python
import functools

import jax
import jax.numpy as jnp
from jax import lax
from jax.experimental import pallas as pl
from jax.experimental.pallas import tpu as pltpu
from jax.sharding import PartitionSpec as P

HEAD_DIM = 64
PATCHES = 197
TEXT_MAX = 40
STEP = 7

norm_epsilon = 1e-06
masked_score = -1000000000.0
first_decay = 0.9
second_decay = 0.98
adam_epsilon = 1e-06
matrix_rate = 0.04
vector_rate = 0.5
weight_decay = 0.01

PATCH_STRIDE = 208
TEXT_STRIDE = 48
ITEM_ROWS = PATCH_STRIDE + TEXT_STRIDE

bf16 = jnp.bfloat16
f32 = jnp.float32
VMEM_LIMIT = 58 * 1024 * 1024
ATTENTION_US = 18
LIFT_US = 16
DROP_WEIGHT_US = 7
EXPERT_BACK_US = 17
ATTENTION_BACK_US = 19
DROP_US = 17


def adamw(weight, first_state, second_state, gradient, step_rate, decay_rate):
    first_new = first_decay * first_state + (1.0 - first_decay) * gradient
    second_new = second_decay * second_state + (1.0 - second_decay) * gradient * gradient
    first_hat = first_new / (1.0 - first_decay**STEP)
    second_hat = second_new / (1.0 - second_decay**STEP)
    weight_new = weight - step_rate * (
        first_hat / (jnp.sqrt(second_hat) + adam_epsilon) + decay_rate * weight
    )
    return (weight_new, first_new, second_new, weight_new.astype(bf16))


def dot(left, right, left_dim, right_dim):
    return lax.dot_general(
        left,
        right,
        (((left_dim,), (right_dim,)), ((), ())),
        preferred_element_type=f32,
    )


def loop(count, body):
    lax.fori_loop(0, count, lambda i, c: (body(i), c)[1], 0)


def rows_at(index, size):
    return pl.ds(pl.multiple_of(index * size, 16), size)


def norm_forward(values, gain, shift):
    centred = values - jnp.mean(values, axis=-1, keepdims=True)
    spread = jnp.mean(centred * centred, axis=-1, keepdims=True)
    return centred * lax.rsqrt(spread + norm_epsilon) * gain + shift


def norm_backward(values, gain, grad):
    centred = values - jnp.mean(values, axis=-1, keepdims=True)
    spread = jnp.mean(centred * centred, axis=-1, keepdims=True)
    scale = lax.rsqrt(spread + norm_epsilon)
    hat = centred * scale
    grad_hat = grad * gain
    grad_values = scale * (
        grad_hat
        - jnp.mean(grad_hat, axis=-1, keepdims=True)
        - hat * jnp.mean(grad_hat * hat, axis=-1, keepdims=True)
    )
    grad_gain = jnp.sum(grad * hat, axis=0, keepdims=True)
    grad_shift = jnp.sum(grad, axis=0, keepdims=True)
    return grad_values, grad_gain, grad_shift


def one_hot(row_place, first_row, count):
    place = lax.broadcasted_iota(jnp.int32, (count, row_place.shape[1]), 0) + first_row
    return (place == row_place).astype(bf16)


def relative_block(mine, block):
    other = jnp.bitwise_xor(mine, block)
    return jnp.bitwise_and(other, 1) * 4 + jnp.right_shift(other, 1)


def piece_copies(pieces, mine, place_of, sems):
    even, *odd = pieces
    blocks = [(even, i, 2 * i) for i in range(4)]
    z = 0
    for ref in odd:
        for i in range(ref.shape[0]):
            blocks.append((ref, i, 2 * z + 1))
            z += 1
    size = even.shape[2]
    copies = []
    for index, (ref, i, block) in enumerate(blocks):
        first = jnp.bitwise_xor(mine, block) * size
        rows = pl.ds(pl.multiple_of(first, 16), size)
        copies.append(pltpu.make_async_copy(ref.at[i], place_of(rows), sems.at[index]))
    return copies


def step_parts(pieces):
    parts = []
    for step in range(2 * len(pieces) // 5):
        even, odd, high, front, back = pieces[len(pieces) - 5 - 5 * (step // 2) :][:5]
        parts.append((high, front, back) if step % 2 else (even, odd))
    return parts


def step_copies(parts, mine, weight_ref, sems):
    by_step = []
    for step, pieces in enumerate(parts):
        place_of = lambda rows, step=step: weight_ref.at[:, step, rows, :]
        by_step.append(piece_copies(pieces, mine, place_of, sems.at[step]))
    return by_step


def start_all(by_step):
    for copies in by_step:
        for copy in copies:
            copy.start()


def out_copy(weight_ref, out_ref, out_sems, step, places):
    return pltpu.make_async_copy(
        weight_ref.at[:, step], out_ref.at[:, places[step]], out_sems.at[step]
    )


def wait_step(by_step, weight_ref, out_ref, out_sems, places):
    for step, copies in enumerate(by_step):

        @pl.when(pl.program_id(0) == step)
        def _():
            for copy in copies:
                copy.wait()
            out_copy(weight_ref, out_ref, out_sems, step, places).start()


def wait_out(weight_ref, out_ref, out_sems, places):
    for step in range(weight_ref.shape[1]):
        out_copy(weight_ref, out_ref, out_sems, step, places).wait()


def store_grad(grad_ref, mine, index, first, rows, value):
    value = value.astype(bf16)
    size = grad_ref.shape[-2]
    for part in range(rows // size):
        place = relative_block(mine, first // size + part)
        grad_ref[0, place, index] = value[part * size : (part + 1) * size]


def attend(queries, keys, values, allowed):
    scores = [dot(key, query, 1, 1) for query, key in zip(queries, keys)]
    scores = [jnp.where(mask, score, masked_score) for mask, score in zip(allowed, scores)]
    tops = [jnp.max(score, axis=0, keepdims=True) for score in scores]
    weights = [jnp.exp(score - top) for score, top in zip(scores, tops)]
    totals = [jnp.sum(weight, axis=0, keepdims=True) for weight in weights]
    weights = [(weight * (1.0 / total)).astype(bf16) for weight, total in zip(weights, totals)]
    return weights, [dot(value, weight, 0, 0) for value, weight in zip(values, weights)]


def item_slices(items, i):
    first = items * PATCH_STRIDE + i * TEXT_STRIDE
    return slice(i * PATCH_STRIDE, (i + 1) * PATCH_STRIDE), slice(first, first + TEXT_STRIDE)


def item_rows(ref, index, items, i):
    patch_rows, text_rows = item_slices(items, i)
    return jnp.concatenate([ref[index + (patch_rows,)], ref[index + (text_rows,)]], axis=0)


def head_columns(rows, kind, heads, h):
    first = (kind * heads + h) * HEAD_DIM
    return rows[:, first : first + HEAD_DIM]


def attention_kernel(meta_ref, raw_ref, place_ref, hidden_ref, norm_ref, extra_ref, *refs, **sizes):
    parts, outs = (refs[:2], refs[2:4]), refs[4:]
    block_ref, normed_ref, residual_ref, out_ref, joint_ref, mixed_ref, probs_ref = outs[:7]
    weight_ref, sems, out_sems = outs[7:]
    items, main_rows, all_rows = sizes["items"], sizes["main_rows"], sizes["all_rows"]
    step = pl.program_id(0)
    by_step = step_copies(parts, meta_ref[items + 1], weight_ref, sems)

    @pl.when(step == 0)
    def _():
        start_all(by_step)

        def chunk(first, size):
            rows = pl.ds(first, size)
            picked = dot(one_hot(place_ref[...], first, size), raw_ref[...], 1, 0)
            picked = jnp.where(hidden_ref[rows, :] > 0, extra_ref[2:3, :], picked)
            block_ref[rows, :] = picked
            residual_ref[rows, :] = picked
            normed_ref[rows, :] = norm_forward(picked, norm_ref[0:1, :], norm_ref[1:2, :]).astype(bf16)

        loop(items, lambda i: chunk(pl.multiple_of(i * ITEM_ROWS, 16), ITEM_ROWS))
        chunk(main_rows, all_rows - main_rows)

    wait_step(by_step, weight_ref, out_ref, out_sems, (0, 2))
    attend_heads(
        meta_ref, weight_ref.at[0, step], normed_ref, residual_ref, joint_ref, mixed_ref, probs_ref, **sizes
    )

    @pl.when(step == pl.num_programs(0) - 1)
    def _():
        wait_out(weight_ref, out_ref, out_sems, (0, 2))


def attention_end_kernel(meta_ref, normed_ref, block_ref, before_ref, valid_ref, norm_ref, *refs, **sizes):
    parts, outs = (refs[:2], refs[2:4]), refs[8:]
    residual_ref, feed_ref, square_ref, out_ref, joint_ref, mixed_ref, probs_ref = outs[:7]
    weight_ref, sems, out_sems = outs[7:]
    items, main_rows, all_rows = sizes["items"], sizes["main_rows"], sizes["all_rows"]
    step = pl.program_id(0)
    by_step = step_copies(parts, meta_ref[items + 1], weight_ref, sems)

    @pl.when(step == 0)
    def _():
        start_all(by_step)
        residual_ref[...] = before_ref[...]

    wait_step(by_step, weight_ref, out_ref, out_sems, (1, 3))
    attend_heads(
        meta_ref, weight_ref.at[0, step], normed_ref, residual_ref, joint_ref, mixed_ref, probs_ref, **sizes
    )

    @pl.when(step == pl.num_programs(0) - 1)
    def _():
        square_ref[...] = jnp.zeros_like(square_ref)

        def chunk(rows):
            residual = residual_ref[rows, :]
            feed_ref[rows, :] = norm_forward(residual, norm_ref[2:3, :], norm_ref[3:4, :]).astype(bf16)
            attended = (residual - block_ref[rows, :]) * valid_ref[rows, :]
            square_ref[...] += jnp.sum(attended * attended, axis=0, keepdims=True)

        loop(items, lambda i: chunk(rows_at(i, ITEM_ROWS)))
        chunk(pl.ds(main_rows, all_rows - main_rows))
        wait_out(weight_ref, out_ref, out_sems, (1, 3))


def attend_heads(
    meta_ref,
    weight_ref,
    normed_ref,
    residual_ref,
    joint_ref,
    mixed_ref,
    probs_ref,
    *,
    items,
    heads,
    main_rows,
    all_rows,
):
    width = heads * HEAD_DIM
    tail_rows = all_rows - main_rows

    def project(rows):
        joint = dot(normed_ref[rows, :], weight_ref[:, : 3 * width], 1, 0)
        joint_ref[0, rows, :width] = (joint[:, :width].astype(bf16).astype(f32) * HEAD_DIM**-0.5).astype(bf16)
        joint_ref[0, rows, width:] = joint[:, width:].astype(bf16)

    project(pl.ds(0, all_rows))

    key_row = lax.broadcasted_iota(jnp.int32, (ITEM_ROWS, 1), 0)
    blocks = [item_rows(joint_ref, (0,), items, i) for i in range(items)]
    masks = [
        (key_row < PATCHES)
        | ((key_row >= PATCH_STRIDE) & (key_row < PATCH_STRIDE + meta_ref[i]))
        for i in range(items)
    ]
    blocks.append(joint_ref[0, main_rows:, :])
    masks.append(lax.broadcasted_iota(jnp.int32, (tail_rows, 1), 0) < meta_ref[items])
    pairs = [(i, h) for i in range(items + 1) for h in range(heads)]
    weights, outs = attend(
        *[[head_columns(blocks[i], kind, heads, h) for i, h in pairs] for kind in range(3)],
        [masks[i] for i, _ in pairs],
    )
    for (i, h), weight in zip(pairs, weights):
        if i < items:
            probs_ref[0, i, h] = weight
    for i in range(items + 1):
        mixed = jnp.concatenate(outs[i * heads : (i + 1) * heads], axis=0).T.astype(bf16)
        if i == items:
            mixed_ref[0, main_rows:, :] = mixed
        else:
            patch_rows, text_rows = item_slices(items, i)
            mixed_ref[0, patch_rows, :] = mixed[:PATCH_STRIDE]
            mixed_ref[0, text_rows, :] = mixed[PATCH_STRIDE:]

    def add_output(rows):
        residual_ref[rows, :] += dot(mixed_ref[0, rows, :], weight_ref[:, 3 * width :], 1, 1)

    add_output(pl.ds(0, all_rows))


def attention_back_kernel(
    mine_ref,
    grad_attended_ref,
    joint_ref,
    mixed_ref,
    probs_ref,
    normed_ref,
    weight_ref,
    grad_weight_ref,
    grad_normed_ref,
    grad_mixed_ref,
    grad_joint_ref,
    **sizes,
):
    @pl.when(pl.program_id(0) == 0)
    def _():
        grad_normed_ref[...] = jnp.zeros_like(grad_normed_ref)

    heads_back(
        mine_ref,
        grad_attended_ref,
        joint_ref,
        mixed_ref,
        probs_ref,
        normed_ref,
        weight_ref,
        grad_weight_ref,
        grad_normed_ref,
        grad_mixed_ref,
        grad_joint_ref,
        **sizes,
    )


def attention_back_end_kernel(
    mine_ref,
    grad_attended_ref,
    joint_ref,
    mixed_ref,
    probs_ref,
    normed_ref,
    weight_ref,
    before_ref,
    grad_weight_ref,
    grad_normed_ref,
    grad_mixed_ref,
    grad_joint_ref,
    **sizes,
):
    @pl.when(pl.program_id(0) == 0)
    def _():
        grad_normed_ref[...] = before_ref[...]

    heads_back(
        mine_ref,
        grad_attended_ref,
        joint_ref,
        mixed_ref,
        probs_ref,
        normed_ref,
        weight_ref,
        grad_weight_ref,
        grad_normed_ref,
        grad_mixed_ref,
        grad_joint_ref,
        **sizes,
    )


def input_grad_kernel(
    grad_normed_ref,
    grad_residual_ref,
    block_ref,
    hidden_ref,
    place_ref,
    norm_ref,
    *refs,
):
    small_refs, (grad_raw_ref, small_ref, grad_block_ref) = refs[:-3], refs[-3:]
    step = pl.program_id(0)

    @pl.when(step == 0)
    def _():
        small_ref[...] = jnp.zeros_like(small_ref)
        first = 3
        for ref in small_refs:
            small_ref[first : first + ref.shape[0], :] = ref[...]
            first += ref.shape[0]

    grad, gain, shift = norm_backward(block_ref[...], norm_ref[0:1, :], grad_normed_ref[...])
    small_ref[0:1, :] += gain
    small_ref[1:2, :] += shift
    grad = grad + grad_residual_ref[...]
    hidden = hidden_ref[...] > 0
    small_ref[2:3, :] += jnp.sum(jnp.where(hidden, grad, 0.0), axis=0, keepdims=True)
    grad_block_ref[rows_at(step, ITEM_ROWS), :] = jnp.where(hidden, 0.0, grad).astype(bf16)

    @pl.when(step == pl.num_programs(0) - 1)
    def _():
        unplace(place_ref, grad_block_ref, grad_raw_ref, grad_block_ref.shape[0])


def heads_back(
    mine_ref,
    grad_attended_ref,
    joint_ref,
    mixed_ref,
    probs_ref,
    normed_ref,
    weight_ref,
    grad_weight_ref,
    grad_normed_ref,
    grad_mixed_ref,
    grad_joint_ref,
    *,
    items,
    heads,
):
    width = heads * HEAD_DIM
    half = HEAD_DIM**-0.5

    grad_mixed_ref[...] = dot(grad_attended_ref[...], weight_ref[0, :, 3 * width :], 1, 0).astype(bf16)

    blocks = [item_rows(joint_ref, (0,), items, i) for i in range(items)]
    outs = [item_rows(grad_mixed_ref, (), items, i) for i in range(items)]
    products = [
        (outs[i].astype(f32) * item_rows(mixed_ref, (0,), items, i).astype(f32)).T for i in range(items)
    ]
    pairs = [(i, h) for i in range(items) for h in range(heads)]
    queries, keys, values = [
        [head_columns(blocks[i], kind, heads, h) for i, h in pairs] for kind in range(3)
    ]
    grad_outs = [head_columns(outs[i], 0, heads, h) for i, h in pairs]
    weights = [probs_ref[0, i, h] for i, h in pairs]
    grad_probs = [dot(value, grad_out, 1, 1) for value, grad_out in zip(values, grad_outs)]
    means = [
        jnp.sum(products[i][h * HEAD_DIM : (h + 1) * HEAD_DIM], axis=0, keepdims=True) for i, h in pairs
    ]
    grad_scores = [
        (weight.astype(f32) * (grad - mean)).astype(bf16)
        for weight, grad, mean in zip(weights, grad_probs, means)
    ]
    grad_values = [dot(weight, grad_out, 1, 0).astype(bf16) for weight, grad_out in zip(weights, grad_outs)]
    grad_keys = [dot(score, query, 1, 0).astype(bf16) for score, query in zip(grad_scores, queries)]
    grad_queries = [dot(key, score, 0, 0) * half for key, score in zip(keys, grad_scores)]
    for i in range(items):
        own = slice(i * heads, (i + 1) * heads)
        grad_query = jnp.concatenate(grad_queries[own], axis=0).T.astype(bf16)
        grad_joint = jnp.concatenate([grad_query] + grad_keys[own] + grad_values[own], axis=1)
        patch_rows, text_rows = item_slices(items, i)
        grad_joint_ref[patch_rows, :] = grad_joint[:PATCH_STRIDE]
        grad_joint_ref[text_rows, :] = grad_joint[PATCH_STRIDE:]

    model_width = weight_ref.shape[1]
    for first in range(0, model_width, 384):
        cols = slice(first, first + 384)
        grad_weight = jnp.concatenate(
            [
                dot(normed_ref[:, cols], grad_joint_ref[...], 0, 0),
                dot(grad_attended_ref[:, cols], mixed_ref[0], 0, 0),
            ],
            axis=1,
        )
        store_grad(grad_weight_ref, mine_ref[0], 0, first, 384, grad_weight)

    grad_normed_ref[...] += dot(grad_joint_ref[...], weight_ref[0, :, : 3 * width], 1, 1)


def unplace(place_ref, source_ref, raw_ref, source_rows):
    source = source_ref[...].astype(bf16)
    raw_rows = raw_ref.shape[0]
    size = 240 if raw_rows % 240 == 0 else raw_rows

    def chunk(i):
        rows = rows_at(i, size)
        place = lax.broadcasted_iota(jnp.int32, (size, source_rows), 1)
        pick = (place == place_ref[rows, :]).astype(bf16)
        raw_ref[rows, :] = dot(pick, source, 1, 0).astype(bf16)

    loop(raw_rows // size, chunk)


def lift_kernel(mine_ref, feed_ref, *refs, vision_rows, all_rows):
    pieces, (acted_ref, slope_ref, out_ref, weight_ref, sems, out_sems) = refs[:10], refs[10:]
    by_step = step_copies(step_parts(pieces), mine_ref[0], weight_ref, sems)

    @pl.when(pl.program_id(0) == 0)
    def _():
        start_all(by_step)

    wait_step(by_step, weight_ref, out_ref, out_sems, (0, 1, 2, 3))

    def piece(rows, expert):
        lifted = dot(feed_ref[rows, :], weight_ref[expert, pl.program_id(0)], 1, 0)
        cumulative = 0.5 * (1.0 + lax.erf(lifted * (0.5**0.5)))
        density = jnp.exp(-0.5 * lifted * lifted) * ((2.0 * jnp.pi) ** -0.5)
        acted_ref[0, rows, :] = (lifted * cumulative).astype(bf16)
        slope_ref[0, rows, :] = (cumulative + lifted * density).astype(bf16)

    loop(2, lambda i: piece(rows_at(i, vision_rows // 2), 0))
    piece(pl.ds(vision_rows, all_rows - vision_rows), 1)

    @pl.when(pl.program_id(0) == pl.num_programs(0) - 1)
    def _():
        wait_out(weight_ref, out_ref, out_sems, (0, 1, 2, 3))


def place_grad_kernel(raw_ref, place_ref, grad_ref, grad_bias_ref, *, vision_rows):
    def chunk(i):
        rows = rows_at(i, ITEM_ROWS)
        pick = one_hot(place_ref[...], i * ITEM_ROWS, ITEM_ROWS)
        grad_ref[rows, :] = dot(pick, raw_ref[...], 1, 0).astype(bf16)

    loop(grad_ref.shape[0] // ITEM_ROWS, chunk)
    grad_bias_ref[0:1, :] = jnp.sum(grad_ref[:vision_rows, :].astype(f32), axis=0, keepdims=True)
    grad_bias_ref[1:2, :] = jnp.sum(grad_ref[vision_rows:, :].astype(f32), axis=0, keepdims=True)


def expert_weight_grad(grad_weight_ref, mine, left_ref, right, vision_rows):
    rows_total, width = left_ref.shape
    for expert, rows in ((0, slice(0, vision_rows)), (1, slice(vision_rows, rows_total))):
        for first in range(0, width, 384):
            grad_weight = dot(left_ref[rows, first : first + 384], right(rows), 0, 0)
            store_grad(grad_weight_ref, mine, expert, first, 384, grad_weight)


def drop_weight_kernel(mine_ref, grad_ref, acted_ref, grad_weight_ref, *, vision_rows):
    expert_weight_grad(
        grad_weight_ref, mine_ref[0], grad_ref, lambda rows: acted_ref[0, rows, :], vision_rows
    )


def drop_kernel(
    acted_ref,
    residual_ref,
    valid_ref,
    place_ref,
    extra_ref,
    weight_ref,
    raw_ref,
    square_ref,
    total_ref,
    *,
    vision_rows,
    all_rows,
):
    step = pl.program_id(0)
    text = all_rows - vision_rows

    @pl.when(step == 0)
    def _():
        total_ref[:vision_rows, :] = jnp.broadcast_to(extra_ref[0:1, :], (vision_rows, total_ref.shape[1]))
        total_ref[vision_rows:, :] = jnp.broadcast_to(extra_ref[1:2, :], (text, total_ref.shape[1]))

    def piece(rows, expert):
        total_ref[rows, :] += dot(acted_ref[0, rows, :], weight_ref[expert, 0], 1, 1)

    piece(pl.ds(0, vision_rows), 0)
    piece(pl.ds(vision_rows, text), 1)

    @pl.when(step == pl.num_programs(0) - 1)
    def _():
        square_ref[...] = jnp.zeros_like(square_ref)

        def finish(rows, expert):
            fed = total_ref[rows, :]
            out = residual_ref[rows, :] + fed
            valid = valid_ref[rows, :]
            square_ref[0:1, :] += jnp.sum(valid * out * out, axis=0, keepdims=True)
            square_ref[1:2, :] += jnp.sum(valid * fed * fed, axis=0, keepdims=True)
            total_ref[rows, :] = out

        loop(2, lambda i: finish(rows_at(i, vision_rows // 2), 0))
        finish(pl.ds(vision_rows, text), 1)
        unplace(place_ref, total_ref, raw_ref, all_rows)


def expert_back_step(
    mine_ref, grad_ref, slope_ref, feed_ref, lift_ref, drop_ref, grad_weight_ref, total_ref, lifted_ref, vision_rows
):
    step = pl.program_id(0)

    def piece(rows, expert):
        grad_acted = dot(grad_ref[rows, :], drop_ref[expert, step], 1, 0)
        grad_lifted = (grad_acted * slope_ref[0, rows, :].astype(f32)).astype(bf16)
        lifted_ref[rows, :] = grad_lifted
        total_ref[rows, :] += dot(grad_lifted, lift_ref[expert, 0], 1, 1)

    piece(pl.ds(0, vision_rows), 0)
    piece(pl.ds(vision_rows, grad_ref.shape[0] - vision_rows), 1)
    expert_weight_grad(
        grad_weight_ref, mine_ref[0], feed_ref, lambda rows: lifted_ref[rows, :], vision_rows
    )


def expert_back_kernel(mine_ref, grad_ref, slope_ref, feed_ref, lift_ref, *refs, vision_rows):
    pieces, (grad_weight_ref, out_ref, total_ref) = refs[:5], refs[5:8]
    lifted_ref, drop_ref, sems, out_sems = refs[8:]
    by_step = step_copies(step_parts(pieces), mine_ref[0], drop_ref, sems)

    @pl.when(pl.program_id(0) == 0)
    def _():
        start_all(by_step)
        total_ref[...] = jnp.zeros_like(total_ref)

    wait_step(by_step, drop_ref, out_ref, out_sems, (0, 1))
    expert_back_step(
        mine_ref, grad_ref, slope_ref, feed_ref, lift_ref, drop_ref, grad_weight_ref, total_ref, lifted_ref, vision_rows
    )

    @pl.when(pl.program_id(0) == pl.num_programs(0) - 1)
    def _():
        wait_out(drop_ref, out_ref, out_sems, (0, 1))


def expert_back_end_kernel(mine_ref, grad_ref, slope_ref, feed_ref, lift_ref, *refs, vision_rows):
    pieces, (_, before_ref, residual_ref, norm_ref) = refs[:5], refs[5:9]
    grad_weight_ref, out_ref, grad_residual_ref, grad_attended_ref, grad_norm_ref = refs[9:14]
    lifted_ref, drop_ref, sems, out_sems = refs[14:]
    by_step = step_copies(step_parts(pieces), mine_ref[0], drop_ref, sems)

    @pl.when(pl.program_id(0) == 0)
    def _():
        start_all(by_step)
        grad_residual_ref[...] = before_ref[...]

    wait_step(by_step, drop_ref, out_ref, out_sems, (2, 3))
    expert_back_step(
        mine_ref,
        grad_ref,
        slope_ref,
        feed_ref,
        lift_ref,
        drop_ref,
        grad_weight_ref,
        grad_residual_ref,
        lifted_ref,
        vision_rows,
    )

    @pl.when(pl.program_id(0) == pl.num_programs(0) - 1)
    def _():
        grad_norm_ref[...] = jnp.zeros_like(grad_norm_ref)

        def chunk(i):
            rows = rows_at(i, ITEM_ROWS)
            grad, gain, shift = norm_backward(
                residual_ref[rows, :], norm_ref[2:3, :], grad_residual_ref[rows, :]
            )
            grad_norm_ref[0:1, :] += gain
            grad_norm_ref[1:2, :] += shift
            grad = grad + grad_ref[rows, :].astype(f32)
            grad_residual_ref[rows, :] = grad
            grad_attended_ref[rows, :] = grad.astype(bf16)

        loop(grad_ref.shape[0] // ITEM_ROWS, chunk)
        wait_out(drop_ref, out_ref, out_sems, (2, 3))


def whole(*shape):
    return pl.BlockSpec(shape, lambda *_: (0,) * len(shape))


def stepped(*shape, first=0):
    return pl.BlockSpec(shape, lambda i, *_: (i + first,) + (0,) * (len(shape) - 1))


def stepped_pair(*shape, first=0):
    return pl.BlockSpec(shape, lambda i, *_: (0, i + first) + (0,) * (len(shape) - 2))


def every_other(*shape, first=0):
    return pl.BlockSpec(shape, lambda i, *_: (2 * i + first,) + (0,) * (len(shape) - 1))


def anywhere(values):
    return (values, pl.BlockSpec(memory_space=pl.ANY))


def call(kernel, name, steps, ins, outs, scratch, microseconds, scalars=(), aliases=None):
    return pl.pallas_call(
        kernel,
        name=name,
        grid_spec=pltpu.PrefetchScalarGridSpec(
            num_scalar_prefetch=len(scalars),
            grid=(steps,),
            in_specs=[block for _, block in ins],
            out_specs=[block for _, _, block in outs],
            scratch_shapes=scratch,
        ),
        out_shape=[jax.ShapeDtypeStruct(shape, kind) for shape, kind, _ in outs],
        input_output_aliases=aliases or {},
        compiler_params=pltpu.CompilerParams(
            dimension_semantics=("arbitrary",), vmem_limit_bytes=VMEM_LIMIT
        ),
        cost_estimate=pl.CostEstimate(
            flops=int(microseconds * 1e9), bytes_accessed=int(microseconds * 1e6), transcendentals=0
        ),
    )(*scalars, *[array for array, _ in ins])


def body(
    tokens,
    cotangent,
    text_lengths,
    modality,
    masked_positions,
    joint_weight,
    joint_first,
    joint_second,
    output_weight,
    output_first,
    output_second,
    lift_weight,
    lift_first,
    lift_second,
    drop_weight,
    drop_first,
    drop_second,
    norm_params,
    norm_first,
    norm_second,
    extra_params,
    extra_first,
    extra_second,
):
    micro_count, shard_rows, model_width = tokens.shape
    block_rows = modality.shape[1]
    parts = block_rows // shard_rows
    assert micro_count == parts
    items = text_lengths.shape[1]
    width = joint_weight.shape[2]
    heads = width // HEAD_DIM
    hidden_width = lift_weight.shape[2]
    shard = joint_weight.shape[1]
    vision_rows = items * PATCH_STRIDE
    main_rows = items * ITEM_ROWS
    tail = block_rows - items * PATCHES - TEXT_MAX - (items - 1)
    tail = (tail + 47) // 48 * 48
    all_rows = main_rows + tail
    assert 4 * width == model_width and hidden_width == model_width

    shard_attend = jnp.concatenate(
        [joint_weight[0], joint_weight[1], joint_weight[2], output_weight.T], axis=1
    ).astype(bf16)[None]
    shard_lift = lift_weight.astype(bf16)
    shard_drop = jnp.swapaxes(drop_weight, 1, 2).astype(bf16)

    groups = lax.axis_size("dp")
    cube = groups == 8
    piece = model_width // 8
    if cube:
        mine = jnp.stack([lax.axis_index("dp"), lax.axis_index("mp")]).astype(jnp.int32)
    else:
        mine = jnp.zeros((2,), jnp.int32)

    def together(*values):
        return lax.optimization_barrier(values)

    def swap(values, axis, bit):
        size = lax.axis_size(axis)
        return lax.ppermute(values, axis, [(i, i ^ bit) for i in range(size)])

    def exchange(values):
        return lax.all_to_all(values, "mp", split_axis=0, concat_axis=1, tiled=True)[0]

    def give_back(values):
        return lax.all_to_all(
            values.reshape(parts, shard_rows, model_width), "mp", split_axis=0, concat_axis=0, tiled=True
        )

    def gather(values):
        whole_values = lax.all_gather(values, ("mp", "dp"), axis=1, tiled=True)
        return whole_values.reshape(-1, parts, model_width, values.shape[2])

    def gather_pieces(values):
        whole_values = jnp.swapaxes(gather(values).reshape(-1, parts, 4, 2, piece, model_width), 0, 3)
        pieces = []
        for core in range(2):
            low, high = whole_values[:, core], whole_values[:, 2 + core]
            pieces += [low[0], low[1], high[0], high[1, :2], high[1, 2:]]
        return pieces

    def line_parts(values):
        return (values,) + tuple(swap(values, "dp", bit) for bit in (2, 4, 6))

    def gather_line(values):
        return jnp.stack(line_parts(values))

    def gather_plane(line):
        return swap(line, "dp", 1), swap(line, "mp", 2)

    def gather_corner(along_x, along_y):
        return swap(along_x[:2], "mp", 2), swap(along_y[2:], "dp", 1)

    def over_cores(*pieces):
        return tuple(swap(part, "mp", 1) for part in pieces)

    def add(*terms):
        total = terms[0].astype(f32)
        for term in terms[1:]:
            total = total + term.astype(f32)
        return total

    def scatter(keep, send):
        shape = (2, 2, 4) + keep.shape[2:]
        both = jnp.stack([keep.reshape(shape), send.reshape(shape)], axis=1)
        both = jnp.transpose(both, (4, 0, 1, 3, 2, 5, 6))
        return reduce(both.reshape(both.shape[0], parts * model_width, shape[-1]))

    def reduce(values):
        values = lax.psum_scatter(values, ("mp", "dp"), scatter_dimension=1, tiled=True)
        return values.astype(f32)

    def quarters(keep, received, *others):
        keep, received, others = together(keep, received, others)
        shape = (2, 2, 4) + keep.shape[2:]
        keep, received = keep.reshape(shape), received.reshape(shape)
        return (lambda y, x: add(keep[y, x], received[y, x])), others

    def scatter_corner(keep, received):
        quarter, _ = quarters(keep, received)
        return quarter(1, 1).astype(bf16)

    def scatter_plane(keep, received, from_x, from_y):
        quarter, (from_x, from_y) = quarters(keep, received, from_x, from_y)
        part_x, part_y = quarter(0, 1), quarter(1, 0)
        part_x = jnp.concatenate([part_x[:2], add(part_x[2:], from_y)]).astype(bf16)
        part_y = jnp.concatenate([add(part_y[:2], from_x), part_y[2:]]).astype(bf16)
        return part_x, part_y

    def scatter_line(keep, received, from_x, from_y):
        quarter, (from_x, from_y) = quarters(keep, received, from_x, from_y)
        return add(quarter(0, 0), from_x, from_y).astype(bf16)

    def send_corner(corner):
        return swap(corner[:2], "dp", 1), swap(corner[2:], "mp", 2)

    def send_plane(part_x, part_y):
        return swap(part_x, "dp", 1), swap(part_y, "mp", 2)

    def send_line(line):
        return tuple(swap(line[i], "dp", 2 * i) for i in (1, 2, 3))

    micro = lax.axis_index("mp")
    lengths = lax.dynamic_index_in_dim(text_lengths, micro, 0, keepdims=False)
    masked = lax.dynamic_index_in_dim(masked_positions, micro, 0, keepdims=False)
    item_ids = jnp.arange(items, dtype=jnp.int32)
    sizes = PATCHES + lengths
    ends = jnp.sum(jnp.where(item_ids[:, None] <= item_ids[None, :], sizes[:, None], 0), axis=0)
    used = jnp.sum(sizes)

    def place_of(row):
        segment = jnp.sum((row[..., None] >= ends).astype(jnp.int32), axis=-1)
        start = jnp.sum(jnp.where(row[..., None] >= ends, sizes, 0), axis=-1)
        inside = row - start
        return jnp.where(
            segment == items,
            main_rows + inside,
            jnp.where(
                inside < PATCHES,
                PATCH_STRIDE * segment + inside,
                vision_rows + TEXT_STRIDE * segment + inside - PATCHES,
            ),
        )

    places = together(place_of(jnp.arange(block_rows, dtype=jnp.int32)))[0]
    place_row, place_column = places[None, :], places[:, None]
    targets = (vision_rows + TEXT_STRIDE * item_ids[:, None] + masked).reshape(-1)
    spots = jnp.arange(all_rows, dtype=jnp.int32)
    hidden = jnp.any(spots[:, None] == targets[None, :], axis=1).astype(jnp.int32)[:, None]
    text_spot = spots - vision_rows
    text_item = text_spot // TEXT_STRIDE
    text_end = jnp.sum(jnp.where(text_item[:, None] == item_ids, lengths, 0), axis=1)
    valid = jnp.where(
        text_spot < 0, spots % PATCH_STRIDE < PATCHES, text_spot - text_item * TEXT_STRIDE < text_end
    )
    valid = valid.astype(f32)[:, None]
    meta = jnp.concatenate([lengths, (block_rows - used)[None], mine[:1]])

    def rows_of(count, kind):
        return ((count, model_width), kind, whole(count, model_width))

    def plain(values):
        return (values, whole(*values.shape))

    def heads_out(first):
        shapes = [
            (parts, all_rows, 3 * width),
            (parts, all_rows, width),
            (parts, items, heads, ITEM_ROWS, ITEM_ROWS),
        ]
        return [(shape, bf16, every_other(1, *shape[1:], first=first)) for shape in shapes]

    def whole_weight(count):
        return ((count, parts, model_width, model_width), bf16, pl.BlockSpec(memory_space=pl.ANY))

    def weight_scratch(count, steps):
        return [
            pltpu.VMEM((count, steps, model_width, model_width), bf16),
            pltpu.SemaphoreType.DMA((steps, 8)),
            pltpu.SemaphoreType.DMA((steps,)),
        ]

    def part_weight(values, first, count=2):
        return (values, stepped_pair(count, 1, *values.shape[2:], first=first))

    def grad_out(count):
        shape = (2, 8, count, piece, model_width)
        return (shape, bf16, stepped(1, *shape[1:]))

    head_sizes = dict(items=items, heads=heads)
    row_sizes = dict(main_rows=main_rows, all_rows=all_rows)

    def attention(raw, pieces):
        return call(
            functools.partial(attention_kernel, **head_sizes, **row_sizes),
            "attention",
            2,
            [plain(raw), plain(place_row), plain(hidden), plain(norm_params), plain(extra_params)]
            + [anywhere(values) for values in pieces],
            [rows_of(all_rows, f32), rows_of(all_rows, bf16), rows_of(all_rows, f32), whole_weight(1)]
            + heads_out(0),
            weight_scratch(1, 2),
            ATTENTION_US,
            (meta,),
        )

    def attention_end(normed, block_input, residual, pieces, made):
        return call(
            functools.partial(attention_end_kernel, **head_sizes, **row_sizes),
            "attention_end",
            2,
            [plain(normed), plain(block_input), plain(residual), plain(valid), plain(norm_params)]
            + [anywhere(values) for values in pieces]
            + [anywhere(values) for values in made],
            [rows_of(all_rows, f32), rows_of(all_rows, bf16), rows_of(1, f32), whole_weight(1)]
            + heads_out(1),
            weight_scratch(1, 2),
            ATTENTION_US,
            (meta,),
            {10 + i: 3 + i for i in range(4)},
        )

    def lift(feed_input, pieces):
        shape = (parts, all_rows, hidden_width)
        return call(
            functools.partial(lift_kernel, vision_rows=vision_rows, all_rows=all_rows),
            "lift",
            parts,
            [plain(feed_input)] + [anywhere(values) for values in pieces],
            [(shape, bf16, stepped(1, *shape[1:]))] * 2 + [whole_weight(2)],
            weight_scratch(2, parts),
            LIFT_US,
            (mine,),
        )

    def place_grad(raw):
        return call(
            functools.partial(place_grad_kernel, vision_rows=vision_rows),
            "place_grad",
            1,
            [plain(raw), plain(place_row)],
            [rows_of(main_rows, bf16), rows_of(2, f32)],
            [],
            5,
        )

    def drop_weight_grad(grad_rows, acted, first):
        return call(
            functools.partial(drop_weight_kernel, vision_rows=vision_rows),
            "drop_weight_grad",
            2,
            [plain(grad_rows), (acted, stepped(1, main_rows, hidden_width, first=first))],
            [grad_out(2)],
            [],
            DROP_WEIGHT_US,
            (mine,),
        )[0]

    def expert_ins(grad_rows, slope, feed_input, lift_weights, pieces, first):
        return [
            plain(grad_rows),
            (slope, stepped(1, main_rows, hidden_width, first=first)),
            (feed_input, whole(main_rows, model_width)),
            part_weight(lift_weights, first),
        ] + [anywhere(values) for values in pieces]

    drop_out = whole_weight(2)
    expert_scratch = [pltpu.VMEM((main_rows, hidden_width), bf16)] + weight_scratch(2, 2)

    def expert_back(pieces, *args):
        return call(
            functools.partial(expert_back_kernel, vision_rows=vision_rows),
            "expert_back",
            2,
            expert_ins(*args, pieces[5:], 0),
            [grad_out(2), drop_out, rows_of(main_rows, f32)],
            expert_scratch,
            EXPERT_BACK_US,
            (mine,),
        )

    def expert_back_end(made, before, residual, pieces, *args):
        return call(
            functools.partial(expert_back_end_kernel, vision_rows=vision_rows),
            "expert_back_end",
            2,
            expert_ins(*args, pieces[:5], 2)
            + [anywhere(made), plain(before), (residual, whole(main_rows, model_width))]
            + [plain(norm_params)],
            [grad_out(2), drop_out, rows_of(main_rows, f32), rows_of(main_rows, bf16)]
            + [rows_of(2, f32)],
            expert_scratch,
            EXPERT_BACK_US,
            (mine,),
            {10: 1},
        )

    def heads_ins(grad_attended, normed, weights, joint_rows, mixed, probs, first):
        return [
            plain(grad_attended),
            (joint_rows, stepped(1, main_rows, 3 * width, first=first)),
            (mixed, stepped(1, main_rows, width, first=first)),
            (probs, stepped(1, *probs.shape[1:], first=first)),
            (normed, whole(main_rows, model_width)),
            (weights, stepped(1, model_width, model_width, first=first)),
        ]

    heads_scratch = [
        pltpu.VMEM((main_rows, width), bf16),
        pltpu.VMEM((main_rows, 3 * width), bf16),
    ]

    def attention_back(*args):
        return call(
            functools.partial(attention_back_kernel, **head_sizes),
            "attention_back",
            2,
            heads_ins(*args, 0),
            [grad_out(1), rows_of(main_rows, f32)],
            heads_scratch,
            ATTENTION_BACK_US,
            (mine,),
        )

    def attention_back_end(before, *args):
        return call(
            functools.partial(attention_back_end_kernel, **head_sizes),
            "attention_back_end",
            2,
            heads_ins(*args, 2) + [plain(before)],
            [grad_out(1), rows_of(main_rows, f32)],
            heads_scratch,
            ATTENTION_BACK_US,
            (mine,),
        )

    def finish_input_grad(grad_normed, grad_residual, block_input, *sums):
        return call(
            input_grad_kernel,
            "input_grad",
            main_rows // ITEM_ROWS,
            [
                (grad_normed, stepped(ITEM_ROWS, model_width)),
                (grad_residual, stepped(ITEM_ROWS, model_width)),
                (block_input, stepped(ITEM_ROWS, model_width)),
                (hidden, stepped(ITEM_ROWS, 1)),
                plain(place_column),
                plain(norm_params),
            ]
            + [plain(values) for values in sums],
            [rows_of(block_rows, bf16), rows_of(16, f32)],
            [pltpu.VMEM((main_rows, model_width), bf16)],
            9,
        )

    def drop(acted, residual, weights):
        return call(
            functools.partial(drop_kernel, vision_rows=vision_rows, all_rows=all_rows),
            "drop",
            parts,
            [(acted, stepped(1, all_rows, hidden_width)), plain(residual), plain(valid)]
            + [plain(place_column), plain(extra_params)]
            + [part_weight(weights, 0)],
            [rows_of(block_rows, bf16), rows_of(2, f32)],
            [pltpu.VMEM((all_rows, model_width), f32)],
            DROP_US,
        )

    used_row = jnp.where(jnp.arange(model_width)[None, :] == 0, used.astype(f32), 0.0)
    tables = (place_row, place_column, hidden, valid, meta)
    raw_tokens = exchange(tokens)
    if cube:
        line = gather_line(shard_attend)
        even, high = gather_plane(line)
        even, high, raw_tokens, shard_lift, cotangent, tables = together(
            even, high, raw_tokens, shard_lift, cotangent, tables
        )
        place_row, place_column, hidden, valid, meta = tables
        corner = swap(high, "dp", 1)
        line_lift = line_parts(shard_lift)
        raw_grad = exchange(cotangent.astype(bf16))
        early = over_cores(line, even) + (line, even)
    else:
        pieces = gather_pieces(shard_attend)
        early = [pieces[i] for i in (5, 6, 0, 1)]
        late = [pieces[7], jnp.concatenate(pieces[8:10]), pieces[2], jnp.concatenate(pieces[3:5])]
        raw_grad = exchange(cotangent.astype(bf16))

    block_input, normed, residual, *made = attention(raw_tokens, early)
    if cube:
        corner, line_lift, raw_grad, residual = together(corner, line_lift, raw_grad, residual)
        late = over_cores(high, corner) + (high, corner)
        line_lift, shard_drop = together(jnp.stack(line_lift), shard_drop)
        plane_lift = gather_plane(line_lift)
        line_drop = line_parts(shard_drop)
    residual, feed_input, attended_square, *made = attention_end(normed, block_input, residual, late, made)
    made[0] = made[0][0]
    if cube:
        plane_lift, line_drop, raw_grad, feed_input = together(plane_lift, line_drop, raw_grad, feed_input)
        corner_lift = gather_corner(*plane_lift)
        lift_others = over_cores(line_lift, *plane_lift)
    grad_rows, grad_bias = place_grad(raw_grad)
    if cube:
        corner_lift, lift_others, line_drop, grad_rows = together(
            corner_lift, lift_others, line_drop, grad_rows
        )
        lift_pieces = (line_lift,) + plane_lift + corner_lift
        lift_pieces += lift_others + over_cores(*corner_lift)
        line_drop = jnp.stack(line_drop)
        plane_drop = gather_plane(line_drop)
    else:
        lift_pieces = gather_pieces(shard_lift)
    acted, slope, lift_all = lift(feed_input, lift_pieces)
    if cube:
        plane_drop, acted = together(plane_drop, acted)
        corner_drop = gather_corner(*plane_drop)
        drop_others = over_cores(line_drop, *plane_drop)
    drop_send = drop_weight_grad(grad_rows, acted, 0)
    if cube:
        corner_drop, drop_others, drop_send, acted = together(corner_drop, drop_others, drop_send, acted)
        drop_received = swap(drop_send, "mp", 1)
        drop_pieces = (line_drop,) + plane_drop + corner_drop
        drop_pieces += drop_others + over_cores(*corner_drop)
    drop_keep = drop_weight_grad(grad_rows, acted, 2)
    if cube:
        drop_pieces, drop_received, drop_keep = together(drop_pieces, drop_received, drop_keep)
        corner, grad_rows = together(scatter_corner(drop_keep, drop_received), grad_rows)
        from_corner = send_corner(corner)
    else:
        drop_pieces = gather_pieces(shard_drop)
        drop_grad = scatter(drop_keep, drop_send)

    lift_send, drop_all, grad_feed = expert_back(drop_pieces, grad_rows, slope, feed_input, lift_all)
    if cube:
        from_corner, grad_feed = together(from_corner, grad_feed)
        plane = scatter_plane(drop_keep, drop_received, *from_corner)
        plane, lift_send, grad_feed = together(plane, lift_send, grad_feed)
        from_plane = send_plane(*plane)
        lift_received = swap(lift_send, "mp", 1)
    lift_keep, drop_all, grad_residual, grad_attended, grad_norm_second = expert_back_end(
        drop_all, grad_feed, residual, drop_pieces, grad_rows, slope, feed_input, lift_all
    )
    if cube:
        lift_received, from_plane, grad_attended = together(lift_received, from_plane, grad_attended)
        corner = scatter_corner(lift_keep, lift_received)
        drop_line = scatter_line(drop_keep, drop_received, *from_plane)
        corner, drop_line, acted = together(corner, drop_line, acted)
        from_corner = send_corner(corner)
        from_drop_line = send_line(drop_line)
    else:
        lift_grad = scatter(lift_keep, lift_send)
    raw_out, squares = drop(acted, residual, drop_all)
    if cube:
        from_corner, raw_out = together(from_corner, raw_out)
        plane = scatter_plane(lift_keep, lift_received, *from_corner)
        from_drop_line, plane, grad_attended = together(from_drop_line, plane, grad_attended)
        from_plane = send_plane(*plane)

    attend_send, grad_normed = attention_back(grad_attended, normed, *made)
    if cube:
        attend_received = swap(attend_send, "mp", 1)
        from_plane, raw_out, grad_normed = together(from_plane, raw_out, grad_normed)
        lift_line = scatter_line(lift_keep, lift_received, *from_plane)
        lift_line, grad_normed = together(lift_line, grad_normed)
        from_lift_line = send_line(lift_line)
    block_output = give_back(raw_out)
    attend_keep, grad_normed = attention_back_end(grad_normed, grad_attended, normed, *made)
    if cube:
        attend_received, from_lift_line, block_output, attend_keep = together(
            attend_received, from_lift_line, block_output, attend_keep
        )
        corner = scatter_corner(attend_keep, attend_received)
        corner, grad_normed = together(corner, grad_normed)
        from_corner = send_corner(corner)
    grad_raw, small = finish_input_grad(
        grad_normed,
        grad_residual,
        block_input,
        *(grad_norm_second, grad_bias, squares, attended_square, used_row),
    )
    if cube:
        from_corner, small, grad_raw = together(from_corner, small, grad_raw)
        plane = scatter_plane(attend_keep, attend_received, *from_corner)
        plane, small, grad_raw = together(plane, small, grad_raw)
        from_plane = send_plane(*plane)
        for axis, bit in (("mp", 1), ("dp", 1)):
            small = small + swap(small, axis, bit)
        line = scatter_line(attend_keep, attend_received, *from_plane)
        line, small, grad_raw, drop_line, lift_line, block_output = together(
            line, small, grad_raw, drop_line, lift_line, block_output
        )
        attend_grad = add(line[0], *send_line(line))[0]
        drop_grad = add(drop_line[0], *from_drop_line)
        lift_grad = add(lift_line[0], *from_lift_line)
    else:
        attend_grad = scatter(attend_keep, attend_send)[0]
    input_grad = give_back(grad_raw).astype(f32)
    block_output = block_output.astype(f32)

    if cube:
        for axis, bit in (("mp", 2), ("dp", 2), ("dp", 4)):
            small = small + swap(small, axis, bit)
    else:
        small = lax.psum(small, ("dp", "mp"))
    norm_total = jnp.concatenate([small[0:2], small[3:5]])
    extra_total = jnp.concatenate([small[5:7], small[2:3]])
    sums = jnp.sum(small[7:11], axis=1)
    rms_values = jnp.sqrt(jnp.stack([sums[0], sums[2], sums[1]]) / (sums[3] * model_width))

    joint_grad = jnp.stack([attend_grad[:, k * width : (k + 1) * width] for k in range(3)])
    output_grad = attend_grad[:, 3 * width :].T
    drop_grad = jnp.swapaxes(drop_grad, 1, 2)
    results = [block_output, input_grad, rms_values]
    results += adamw(joint_weight, joint_first, joint_second, joint_grad, matrix_rate, weight_decay)
    results += adamw(output_weight, output_first, output_second, output_grad, matrix_rate, weight_decay)
    results += adamw(lift_weight, lift_first, lift_second, lift_grad, matrix_rate, weight_decay)
    results += adamw(drop_weight, drop_first, drop_second, drop_grad, matrix_rate, weight_decay)
    results += adamw(norm_params, norm_first, norm_second, norm_total, vector_rate, 0.0)
    results += adamw(extra_params, extra_first, extra_second, extra_total, vector_rate, 0.0)
    return tuple(results)


def solution(mesh):
    rows = P(None, ("dp", "mp"), None)
    joint, output, lift, drop = (
        P(None, "dp", "mp"),
        P("mp", "dp"),
        P(None, "dp", "mp"),
        P(None, "mp", "dp"),
    )
    return jax.shard_map(
        body,
        mesh=mesh,
        in_specs=(rows, rows, P(None, "dp"), P(None, "dp"), P(None, "dp", None))
        + (joint,) * 3
        + (output,) * 3
        + (lift,) * 3
        + (drop,) * 3
        + (P(),) * 6,
        out_specs=(rows, rows, P())
        + (joint,) * 4
        + (output,) * 4
        + (lift,) * 4
        + (drop,) * 4
        + (P(),) * 8,
        check_vma=False,
    )
```
